256 devices in a mesh: tm: 32 (over y, z), order: 8 (over x, core).
Axes of the slice: x: 4, y: 4, z: 8, core: 2. Of those that a mesh axis runs over, the one named last changes fastest.
Arguments:
- design: bfloat16 [3, 4096, 65536], P(None, 'tm', 'order'), may hold values from -0.0546875 to 0.0546875
- gap_flags: int32 [4096], P('tm'), may hold values 0 or 1
- segment_ids: int32 [4096], P('tm'), may hold values from 0 to 3, never falling along the last dimension, each value on 1 to 2048 neighbouring positions
- ar_order: int32 [3], replicated, may hold values from 1 to 4
- ma_order: int32 [3], replicated, may hold values from 1 to 4
- ar_roots: float32 [3, 4], replicated, may hold values from -0.5 to 1, as said below
- ma_roots: float32 [3, 4], replicated, may hold values from -0.5 to 1, as said below
- kaula: float32 [8, 8192], P('order', 'tm'), may hold values from 0.2 to 2
- precond: float32 [8, 64, 128, 128], P('order', 'tm'), as said below
- solution: float32 [16, 8, 8192], P(None, 'order', 'tm'), may hold values from -6 to 6
- residual: float32 [16, 8, 8192], P(None, 'order', 'tm'), may hold values from -6 to 6
- direction: float32 [16, 8, 8192], P(None, 'order', 'tm'), may hold values from -6 to 6
Outputs:
- new_solution: float32 [16, 8, 8192], P(None, 'order', 'tm')
- new_residual: float32 [16, 8, 8192], P(None, 'order', 'tm')
- new_direction: float32 [16, 8, 8192], P(None, 'order', 'tm')
The draws below stay inside these ranges and needn't reach their ends.
Inputs may be any that keep to these rules, and one draw needn't show every extreme that they name: The first root of each component of ar_roots lies within 2 / 4096 below 1; the others lie within 0.5 of zero. The first root of each component of ma_roots lies within 12 / 4096 below 1; the others lie within 0.5 of zero. `precond`: every block is symmetric positive definite.
All inputs are finite; a program needn't handle non-finite values. No bound on the sum of `gap_flags` on one device may be relied on, other than what follows from the above.
Results may differ from the reference program's by a relative error of at most 0.0036.
Values may be sent and summed in bfloat16 or wider, within the bound.
No kernel may reach another device: no remote copies, remote signals or barrier semaphores. Data moves between devices by JAX's collectives and lax.ppermute only.
A program may use at most 64 MiB of HBM per device.

```python
import math
import jax
import jax.numpy as jnp
import numpy as np
from jax import lax

NCOEF = 65536
BLK = 128
PMAX = 4
QMAX = 4
SEGMENTS = 4
NRHS = 16
EPOCHS = 4096
CD = 8192
BLOCKS_O = 64
N_ORDER = 8


def draw_ar_roots(key, part):
    lead_key, rest_key = jax.random.split(jax.random.fold_in(key, 11))
    spread = jax.random.uniform(lead_key, (3,), jnp.float32, 0.5, 2.0)
    leading = 1.0 - spread / EPOCHS
    others = jax.random.uniform(rest_key, (3, PMAX - 1), jnp.float32, -0.5, 0.5)
    return jnp.concatenate([leading[:, None], others], axis=1)


def draw_ma_roots(key, part):
    lead_key, rest_key = jax.random.split(jax.random.fold_in(key, 23))
    spread = jax.random.uniform(lead_key, (3,), jnp.float32, 1.0, 3.0)
    leading = 1.0 - 4.0 * spread / EPOCHS
    others = jax.random.uniform(rest_key, (3, QMAX - 1), jnp.float32, -0.5, 0.5)
    return jnp.concatenate([leading[:, None], others], axis=1)


def draw_precond(key, part):
    off_key, diag_key = jax.random.split(jax.random.fold_in(key, 37), 2)
    raw = jax.random.normal(off_key, (N_ORDER, BLOCKS_O, BLK, BLK), jnp.float32) / BLK
    symmetric = raw + jnp.swapaxes(raw, 2, 3)
    identity = jnp.eye(BLK, dtype=jnp.float32)
    off_diag = symmetric * (1.0 - identity)
    extra = jax.random.uniform(diag_key, (N_ORDER, BLOCKS_O, BLK), jnp.float32, 0.1, 1.0)
    diagonal = 1.25 * jnp.sum(jnp.abs(off_diag), axis=3) + extra
    matrix = off_diag + diagonal[..., None] * identity
    return matrix


def set_ends(values, key, low, top_value):
    dims = values.shape
    place = [jax.random.randint(jax.random.fold_in(key, axis), (), 0, dims[axis]) for axis in range(len(dims))]
    values = values.at[tuple(place)].set(low)
    longest = dims.index(max(dims))
    place[longest] = (place[longest] + 1) % dims[longest]
    return values.at[tuple(place)].set(top_value)


def levels(stream_key, dims, cuts, low, top_value):
    loudness = 1.0
    for axis_at, shards_of in cuts:
        steps = jax.random.uniform(jax.random.fold_in(jax.random.fold_in(stream_key, 6), axis_at), (shards_of,), jnp.float32, low / len(cuts), top_value / len(cuts))
        loudness = loudness * jnp.repeat(jnp.exp(steps), dims[axis_at] // shards_of).reshape((-1,) + (1,) * (len(dims) - 1 - axis_at))
    return loudness


def split_up(count, total, most, skew):
    weights = [(1 << 20) // math.isqrt(rank ** skew) + 1 for rank in range(2, count + 1)]
    spare, holding = total - most - (count - 1), [1] * (count - 1)
    while spare > 0:
        movable = [i for i in range(count - 1) if holding[i] < most]
        whole, remaining = sum([weights[i] for i in movable]), spare
        for i in movable:
            more = min(most - holding[i], max(1, remaining * weights[i] // whole), spare)
            holding[i] = holding[i] + more
            spare = spare - more
    return np.array([most] + holding)


def uneven(own_key, number_of, total, limit, slope):
    if number_of == 2:
        one = jax.random.randint(own_key, (), max(1, total - limit), min(limit, total - 1) + 1)
        return jnp.stack([one, total - one])
    tallies = jnp.asarray(split_up(number_of, total, limit, slope), jnp.int32)
    pairs = (number_of - 1) // 2
    source_of, sink = tallies[1:1 + 2 * pairs:2], tallies[2:2 + 2 * pairs:2]
    slack = jnp.minimum(source_of - 1, limit - sink)
    moved = jax.random.randint(jax.random.fold_in(own_key, 1), (pairs,), 0, 1 << 20) % (slack + 1)
    tallies = tallies.at[1:1 + 2 * pairs:2].set(source_of - moved).at[2:2 + 2 * pairs:2].set(sink + moved)
    return tallies[jax.random.permutation(jax.random.fold_in(own_key, 2), number_of)]


def scatter_about(own_key, extent, scale, reach, cuts=(), kind=jnp.bfloat16):
    gain = levels(own_key, extent, cuts, -0.22, 0.18) if cuts else 1.0
    entries = jax.random.normal(own_key, extent, jnp.float32) * scale * gain
    return jnp.minimum(jnp.maximum(entries, -reach), reach).astype(kind)


def setup_inputs(seed: int = 0) -> dict:
    seeds = jax.random.split(jax.random.key(seed), 13)
    design = scatter_about(seeds[0], (3, EPOCHS, NCOEF), (3 * EPOCHS) ** -0.5, 0.0546875, ((1, 32), (2, 8)))
    gap_flags = set_ends((jax.random.randint(seeds[1], (EPOCHS,), 0, 16) < 15).astype(jnp.int32), jax.random.fold_in(seeds[1], 1), 0, 1)
    segment_ids = jnp.searchsorted(jnp.cumsum(uneven(seeds[2], SEGMENTS, EPOCHS, EPOCHS // 2, 0)), jnp.arange(EPOCHS), side="right").astype(jnp.int32)
    ar_order = jax.random.randint(seeds[3], (3,), 1, PMAX + 1).astype(jnp.int32)
    ma_order = jax.random.randint(seeds[4], (3,), 1, QMAX + 1).astype(jnp.int32)
    ar_roots = draw_ar_roots(jax.random.fold_in(seeds[12], 71), 0)
    ma_roots = draw_ma_roots(jax.random.fold_in(seeds[12], 71), 0)
    kaula = jnp.clip(jnp.exp(math.log(2.0) - 2.3025851 * jax.random.uniform(seeds[7], (N_ORDER, CD), jnp.float32) ** levels(seeds[7], (N_ORDER, CD), ((0, 8), (1, 32)), -0.2, 0.2)), 0.2, 2.0)
    precond = draw_precond(jax.random.fold_in(seeds[12], 71), 0)
    solution = scatter_about(seeds[9], (NRHS, N_ORDER, CD), 1.0, 6.0, ((1, 8), (2, 32)), jnp.float32)
    residual = scatter_about(seeds[10], (NRHS, N_ORDER, CD), 1.0, 6.0, ((1, 8), (2, 32)), jnp.float32)
    direction = scatter_about(seeds[11], (NRHS, N_ORDER, CD), 1.0, 6.0, ((1, 8), (2, 32)), jnp.float32)
    return {"design": design, "gap_flags": gap_flags, "segment_ids": segment_ids, "ar_order": ar_order, "ma_order": ma_order, "ar_roots": ar_roots, "ma_roots": ma_roots, "kaula": kaula, "precond": precond, "solution": solution, "residual": residual, "direction": direction}


def polynomial(root_values, filter_order):
    number_roots = root_values.shape[1]
    coeffs = jnp.concatenate([jnp.ones((3, 1), root_values.dtype), jnp.zeros((3, number_roots), root_values.dtype)], axis=1)
    for position in range(number_roots):
        active = jnp.where(position < filter_order, root_values[:, position], jnp.zeros_like(root_values[:, position]))
        lagged = jnp.concatenate([jnp.zeros_like(coeffs[:, :1]), coeffs[:, :-1]], axis=1)
        coeffs = coeffs - active[:, None] * lagged
    return coeffs


def moving_part(series, coeffs, seg_ids, backward):
    length = series.shape[2]
    total = jnp.zeros_like(series)
    for lag_step in range(coeffs.shape[1]):
        if backward:
            moved = jnp.pad(series, ((0, 0), (0, 0), (0, lag_step)))[:, :, lag_step:]
            moved_ids = jnp.pad(seg_ids, (0, lag_step), constant_values=-1)[lag_step:]
        else:
            moved = jnp.pad(series, ((0, 0), (0, 0), (lag_step, 0)))[:, :, :length]
            moved_ids = jnp.pad(seg_ids, (lag_step, 0), constant_values=-1)[:length]
        joined = (moved_ids == seg_ids)[None, None, :]
        total = total + coeffs[:, lag_step][None, :, None] * jnp.where(joined, moved, jnp.zeros_like(moved))
    return total


def recursive_part(series, coeffs, seg_ids, backward):
    lags = coeffs.shape[1] - 1
    weights = coeffs[:, 1:].T[:, None, :]

    def advance(carry, inputs):
        buffer, id_buffer = carry
        value, current = inputs
        joined = (id_buffer == current)[:, None, None]
        coupling = jnp.sum(jnp.where(joined, weights * buffer, jnp.zeros_like(buffer)), axis=0)
        result = value - coupling
        new_buffer = jnp.concatenate([result[None], buffer[:-1]], axis=0)
        new_ids = jnp.concatenate([current[None], id_buffer[:-1]], axis=0)
        return (new_buffer, new_ids), result

    start = (jnp.zeros((lags,) + series.shape[:2], series.dtype), jnp.full((lags,), -1, jnp.int32))
    _, outputs = lax.scan(advance, start, (jnp.moveaxis(series, 2, 0), seg_ids), reverse=backward)
    return jnp.moveaxis(outputs, 0, 2)


def precondition(blocks, vector):
    rows = vector.shape[0]
    shaped = vector.reshape(rows, blocks.shape[0], blocks.shape[1])
    return jnp.einsum("bij,rbj->rbi", blocks, shaped, precision=lax.Precision.HIGHEST).reshape(rows, -1)


def reference(design, gap_flags, segment_ids, ar_order, ma_order, ar_roots, ma_roots, kaula, precond, solution, residual, direction):
    rhs_count = direction.shape[0]
    epochs = design.shape[1]
    columns = design.shape[2]
    flat_dir = direction.reshape(rhs_count, columns)
    flat_res = residual.reshape(rhs_count, columns)
    flat_sol = solution.reshape(rhs_count, columns)
    flat_kaula = kaula.reshape(columns)
    blocks = precond.reshape(-1, precond.shape[2], precond.shape[3])
    design_flat = design.reshape(3 * epochs, columns)
    packed = flat_dir.astype(jnp.bfloat16)
    observed = lax.dot_general(packed, design_flat, (((1,), (1,)), ((), ())), preferred_element_type=jnp.float32)
    observed = observed.reshape(rhs_count, 3, epochs)
    gaps = gap_flags.astype(observed.dtype)
    ar_coeffs = polynomial(ar_roots, ar_order)
    ma_coeffs = polynomial(ma_roots, ma_order)
    masked = observed * gaps[None, None, :]
    moving = moving_part(masked, ma_coeffs, segment_ids, False)
    filtered = recursive_part(moving, ar_coeffs, segment_ids, False)
    adjoint = recursive_part(filtered, ar_coeffs, segment_ids, True)
    weighted = (moving_part(adjoint, ma_coeffs, segment_ids, True) * gaps[None, None, :]).astype(jnp.bfloat16)
    gradient = jnp.dot(weighted.reshape(rhs_count, 3 * epochs), design_flat, preferred_element_type=jnp.float32)
    image = gradient + flat_kaula[None, :] * flat_dir
    applied = precondition(blocks, flat_res)
    old_rz = jnp.sum(flat_res * applied, axis=1)
    curvature = jnp.sum(flat_dir * image, axis=1)
    step_len = (old_rz / curvature)[:, None]
    new_solution = flat_sol + step_len * flat_dir
    new_residual = flat_res - step_len * image
    new_applied = precondition(blocks, new_residual)
    new_rz = jnp.sum(new_residual * new_applied, axis=1)
    new_direction = new_applied + (new_rz / old_rz)[:, None] * flat_dir
    shape = direction.shape
    return new_solution.reshape(shape), new_residual.reshape(shape), new_direction.reshape(shape)
```

```python
import jax
import jax.numpy as jnp
from jax import lax
from jax.experimental import pallas as pl
from jax.experimental.pallas import tpu as pltpu
from jax.sharding import Mesh
from jax.sharding import PartitionSpec as P

TM = ("tm_0", "tm_1")
ORDER = ("order_0", "order_1")
TM_ORDER = TM + ORDER
CHUNKS = 8
VMEM_LIMIT = 32 * 1024 * 1024

precise = lax.Precision.HIGHEST
LEVELS = 12
RADIX = 7


def dot(a, b, dims):
    return lax.dot_general(
        a, b, (dims, ((), ())), precision=precise, preferred_element_type=jnp.float32
    )


def splat_rows(read):
    row = lax.broadcasted_iota(jnp.int32, (8, 128), 0)
    out = jnp.zeros((8, 128), jnp.float32)
    for c in range(3):
        out = jnp.where(row == c, read(c), out)
    return out


LOWER = [(i, j) for i in range(4) for j in range(i + 1)]
UPPER = [(i, j) for i in range(4) for j in range(i, 4)]


def active_roots(roots_ref, order_ref):
    return [
        splat_rows(lambda c: jnp.where(k < order_ref[c], roots_ref[c, k], jnp.float32(0.0)))
        for k in range(4)
    ]


def sum_of(terms):
    while len(terms) > 1:
        terms = [
            terms[k] + terms[k + 1] if k + 1 < len(terms) else terms[k]
            for k in range(0, len(terms), 2)
        ]
    return terms[0]


def times(left, right):
    return {
        (i, j): sum_of([left[i, k] * right[k, j] for k in range(j, i + 1)]) for i, j in LOWER
    }


def gram_step(gram, power):
    half = {
        (i, j): sum_of([gram[min(i, k), max(i, k)] * power[k, j] for k in range(j, 4)])
        for i in range(4)
        for j in range(4)
    }
    return {(i, j): sum_of([power[k, i] * half[k, j] for k in range(i, 4)]) for i, j in UPPER}


def row_times(vector, power):
    return [sum_of([vector[i] * power[i, j] for i in range(j, 4)]) for j in range(4)]


def row_power(vector, powers, number, bits):
    for k in range(bits):
        on = ((number >> k) & 1) == 1
        moved = row_times(vector, powers[k])
        vector = [jnp.where(on, moved[j], vector[j]) for j in range(4)]
    return vector


def column_power(vector, powers, number, bits):
    for k in range(bits):
        on = ((number >> k) & 1) == 1
        moved = [sum_of([powers[k][i, j] * vector[j] for j in range(i + 1)]) for i in range(4)]
        vector = [jnp.where(on, moved[i], vector[i]) for i in range(4)]
    return vector


def response_kernel(
    place_ref, aro_ref, mao_ref, arr_ref, mar_ref, toep_ref, gam_ref, fin_ref, reach_ref, pow_ref, gram_ref
):
    poles = active_roots(arr_ref, aro_ref)
    zeros = active_roots(mar_ref, mao_ref)
    kappa = [poles[j] - zeros[j] for j in range(4)]
    one = jnp.ones((8, 128), jnp.float32)
    powers = [{(i, j): poles[i] if i == j else kappa[j] for i, j in LOWER}]
    for _ in range(LEVELS - 1):
        powers.append(times(powers[-1], powers[-1]))
    gram = {(i, j): kappa[i] * kappa[j] for i, j in UPPER}
    for k in range(LEVELS - 1):
        for at, (i, j) in enumerate(LOWER):
            pow_ref[k, at] = powers[k][i, j]
        for at, (i, j) in enumerate(UPPER):
            gram_ref[k, at] = gram[i, j]
        if k < LEVELS - 2:
            add = gram_step(gram, powers[k])
            gram = {at: gram[at] + add[at] for at in UPPER}
    lane = lax.broadcasted_iota(jnp.int32, (8, 128), 1)
    gam = row_power(kappa, powers, lane, RADIX)
    fin = column_power([one] * 4, powers, 127 - lane, RADIX)
    for i in range(4):
        gam_ref[i] = gam[i]
        fin_ref[i] = fin[i]
    eta = jnp.where(lane == 0, 1.0, pltpu.roll(sum_of(gam), 1, 1))
    big_row = lax.broadcasted_iota(jnp.int32, (128, 128), 0)
    big_lane = lax.broadcasted_iota(jnp.int32, (128, 128), 1)
    for c in range(3):
        base = jnp.broadcast_to(eta[c : c + 1, :], (128, 128))
        turned = pltpu.roll(base, 0, 1, stride=1, stride_axis=0)
        toep_ref[c] = jnp.where(big_lane >= big_row, turned, 0.0)
    place = place_ref[0, 0]
    row = lax.broadcasted_iota(jnp.int32, (8, 128), 0)
    front = row < 4
    for side in range(2):
        wide = lane + 128 * side
        peer, kind = wide >> 3, wide & 7
        gap = jnp.where(front, place - 1 - peer, peer - 1 - place)
        steps = jnp.maximum(gap, 0)
        for c in range(3):
            vector = [jnp.where((row & 3) == j, 1.0, 0.0) for j in range(4)]
            for k in range(5):
                cut = {at: powers[RADIX + k][at][c : c + 1, :] for at in LOWER}
                on = ((steps >> k) & 1) == 1
                moved = []
                for j in range(4):
                    terms = [vector[j] * cut[j, j]]
                    for i in range(4):
                        if i > j:
                            terms.append(vector[i] * jnp.where(front, cut[i, j], 0.0))
                        if i < j:
                            terms.append(vector[i] * jnp.where(front, 0.0, cut[j, i]))
                    moved.append(sum_of(terms))
                vector = [jnp.where(on, moved[j], vector[j]) for j in range(4)]
            picked = jnp.zeros((8, 128), jnp.float32)
            for j in range(4):
                picked = jnp.where((kind & 3) == j, vector[j], picked)
            used = ((kind < 4) == front) & (gap >= 0)
            reach_ref[c, :, 128 * side : 128 * side + 128] = jnp.where(used, picked, 0.0)


def segment_kernel(
    place_ref, got_ref, toep_ref, gam_ref, fin_ref, reach_ref, pow_ref, gram_ref, own_ref, near_ref, far_ref
):
    place = place_ref[0, 0]
    ids = got_ref[:, 32:40, :].astype(jnp.float32)
    peer = lax.broadcasted_iota(jnp.int32, (32, 8, 128), 0)
    mine = jnp.sum(jnp.where(peer == place, ids, 0.0), axis=0)
    before = jnp.sum(jnp.where(peer == place - 1, ids, 0.0), axis=0)
    ends = jnp.broadcast_to(ids[:, :, 127:128], (32, 8, 128))
    last = jnp.broadcast_to(mine[:, 127:128], (8, 128))
    prev = jnp.where(place > 0, jnp.broadcast_to(before[:, 127:128], (8, 128)), -1.0)
    count = jnp.sum(jnp.where((peer > place) & (ids == last[None]), 1.0, 0.0), axis=0)
    left = jnp.broadcast_to(jnp.sum(count, axis=1, keepdims=True), (8, 128)).astype(jnp.int32)
    ends_before = jnp.concatenate([ends[:1], ends[:-1]], axis=0)
    sub = lax.broadcasted_iota(jnp.int32, (32, 8, 128), 1)
    keep = jnp.where(
        sub < 4,
        jnp.where((peer < place) & (ends == prev[None]), 1.0, 0.0),
        jnp.where((peer > place) & (ends_before == last[None]), 1.0, 0.0),
    ).reshape(256, 128)
    gram = {at: jnp.zeros((8, 128), jnp.float32) for at in UPPER}
    for k in range(LEVELS - 1):
        power = {pair: pow_ref[k, at] for at, pair in enumerate(LOWER)}
        add = gram_step(gram, power)
        on = ((left >> k) & 1) == 1
        gram = {
            pair: jnp.where(on, gram_ref[k, at] + add[pair], gram[pair])
            for at, pair in enumerate(UPPER)
        }
    lead = jnp.where(mine == prev, 1.0, 0.0)
    trail = jnp.where(mine == last, 1.0, 0.0)
    cont = jnp.where(last == prev, 1.0, 0.0)
    fin = [fin_ref[i] * trail for i in range(4)]
    gam = [gam_ref[i] * lead for i in range(4)]
    fold = [
        sum_of([fin[j] * gram[min(i, j), max(i, j)] for j in range(4)]) for i in range(4)
    ]
    block = {pair: pow_ref[RADIX, at] for at, pair in enumerate(LOWER)}
    past = [cont * value for value in row_times(fold, block)]
    row = lax.broadcasted_iota(jnp.int32, (8, 128), 0)
    big_row = lax.broadcasted_iota(jnp.int32, (128, 128), 0)
    big_lane = lax.broadcasted_iota(jnp.int32, (128, 128), 1)
    wide = jnp.broadcast_to(mine[0:1, :], (128, 128))
    tall = jnp.sum(jnp.where(big_row == big_lane, wide, 0.0), axis=1, keepdims=True)
    same = wide == jnp.broadcast_to(tall, (128, 128))

    def rows(values, c, start):
        out = jnp.zeros((8, 128), jnp.float32)
        for i in range(4):
            out = jnp.where(row == start + i, values[i][c : c + 1, :], out)
        return out

    for c in range(3):
        toep = jnp.where(same, toep_ref[c], 0.0)
        probe = dot(rows(gam, c, 0), toep, ((1,), (1,)))
        out_p = jnp.where(row < 4, probe, 0.0) + rows(past, c, 0)
        fin_low = rows(fin, c, 0)
        near_ref[c] = dot(toep, toep, ((1,), (1,))) + dot(rows(fold, c, 0), fin_low, ((0,), (0,)))
        own_ref[c] = fin_low + pltpu.roll(out_p, 4, 0)
        far_ref[c] = keep * dot(reach_ref[c], out_p + rows(fin, c, 4), ((0,), (0,)))


def state_kernel(parts_ref, gaps_ref, own_ref, message_ref, masked_ref):
    total = parts_ref[0]
    for o in range(1, parts_ref.shape[0]):
        total = total + parts_ref[o]
    gaps = gaps_ref[...].astype(jnp.float32)
    masked = jnp.concatenate([total[:, 128 * c : 128 * c + 128] * gaps for c in range(3)], axis=0)
    masked_ref[...] = masked
    padded = jnp.concatenate([masked, jnp.zeros((80, 128), jnp.float32)], axis=0)
    lane = lax.broadcasted_iota(jnp.int32, (8, 128), 1)
    out = jnp.zeros((8, 128), jnp.float32)
    for c in range(3):
        out = jnp.where((lane >> 4) == c, dot(own_ref[c], padded, ((1,), (1,))), out)
    message_ref[...] = jnp.broadcast_to(out[None], message_ref.shape)


def weighted_rows(masked_ref, near_ref, far_ref, gaps_ref, states_ref):
    gaps = gaps_ref[...].astype(jnp.float32)
    states = states_ref[...].reshape(256, 128)
    pieces = []
    for c in range(3):
        here = dot(masked_ref[16 * c : 16 * c + 16, :], near_ref[c], ((1,), (0,)))
        there = dot(states, far_ref[c], ((0,), (0,)))[16 * c : 16 * c + 16, :]
        pieces.append((here + there) * gaps)
    return pieces


def pack_kernel(direction_ref, ids_ref, out_ref):
    packed = direction_ref[:, 0, :].astype(jnp.bfloat16)
    ids = jnp.broadcast_to(ids_ref[...].astype(jnp.float32), (8, 128)).astype(jnp.bfloat16)
    sheet = jnp.concatenate([packed[:, :128], packed[:, 128:], ids], axis=0)
    out_ref[...] = jnp.broadcast_to(sheet[None], out_ref.shape)


def chunk_copies(design_ref, held_ref, sems):
    width = held_ref.shape[3]
    return [
        pltpu.make_async_copy(
            design_ref.at[:, :, pl.ds(width * k, width)], held_ref.at[k], sems.at[k]
        )
        for k in range(held_ref.shape[0])
    ]


def observe_kernel(got_ref, design_ref, out_ref, held_ref, sems):
    copies = chunk_copies(design_ref, held_ref, sems)
    for copy in copies:
        copy.start()
    count, _, _, width = held_ref.shape
    peers = width // 256
    total = jnp.zeros((384, 128), jnp.float32)
    for k in range(count):
        pieces = []
        for p in range(peers * k, peers * k + peers):
            pieces += [got_ref[p, 0:16, :], got_ref[p, 16:32, :]]
        packed = jnp.concatenate(pieces, axis=1)
        packed = jnp.concatenate([packed, jnp.zeros((112, width), jnp.bfloat16)], axis=0)
        copies[k].wait()
        total = total + lax.dot_general(
            held_ref[k].reshape(384, width),
            packed,
            (((1,), (1,)), ((), ())),
            preferred_element_type=jnp.float32,
        )
    out_ref[...] = jnp.broadcast_to(total.T[None, 0:16, :], out_ref.shape)


def gradient_kernel(
    masked_ref, near_ref, far_ref, gaps_ref, states_ref, design_ref, out_ref, held_ref, sems
):
    copies = chunk_copies(design_ref, held_ref, sems)
    for copy in copies:
        copy.start()
    pieces = weighted_rows(masked_ref, near_ref, far_ref, gaps_ref, states_ref)
    weighted = jnp.concatenate(pieces, axis=1).astype(jnp.bfloat16)
    count, _, _, width = held_ref.shape
    peers = width // 256
    for k in range(count):
        copies[k].wait()
        part = jnp.dot(
            weighted, held_ref[k].reshape(384, width), preferred_element_type=jnp.float32
        ).astype(jnp.bfloat16)
        for p in range(peers):
            out_ref[peers * k + p] = part[:, 256 * p : 256 * p + 256]


def image_kernel(
    arrived_ref, kaula_ref, precond_ref, residual_ref, direction_ref, message_ref, image_ref, applied_ref, both_ref
):
    total = arrived_ref[0].astype(jnp.float32)
    for p in range(1, arrived_ref.shape[0]):
        total = total + arrived_ref[p].astype(jnp.float32)
    direction = direction_ref[:, 0, :]
    residual = residual_ref[:, 0, :]
    image = total + kaula_ref[...] * direction
    stack = jnp.concatenate([residual, image], axis=0)
    mixed = jnp.concatenate(
        [dot(stack[:, 128 * k : 128 * k + 128], precond_ref[0, k], ((1,), (1,))) for k in range(2)],
        axis=1,
    )
    applied, image_applied = mixed[0:16], mixed[16:32]
    products = jnp.concatenate(
        [
            residual * applied,
            direction * image,
            image * applied,
            image * image_applied,
            jnp.zeros((64, 256), jnp.float32),
        ],
        axis=0,
    )
    sums = dot(jnp.ones((8, 256), jnp.float32), products, ((1,), (1,)))
    message_ref[...] = jnp.broadcast_to(sums[None, 0:1, :], message_ref.shape)
    image_ref[...] = image
    applied_ref[...] = applied
    both_ref[...] = image_applied


def update_kernel(
    sums_ref, image_ref, applied_ref, both_ref, solution_ref, residual_ref, direction_ref, sol_ref, res_ref, dir_ref
):
    total = jnp.sum(sums_ref[...], axis=0)
    row = lax.broadcasted_iota(jnp.int32, (16, 128), 0)
    lane = lax.broadcasted_iota(jnp.int32, (16, 128), 1)
    wide = jnp.broadcast_to(total, (16, 128))
    old_rz, curvature, cross, square = [
        jnp.sum(jnp.where(lane == row + 16 * k, wide, 0.0), axis=1, keepdims=True)
        for k in range(4)
    ]
    step = old_rz / curvature
    new_rz = old_rz - 2.0 * step * cross + step * step * square
    direction = direction_ref[:, 0, :]
    fresh = applied_ref[...] - step * both_ref[...] + (new_rz / old_rz) * direction
    sol_ref[:, 0, :] = solution_ref[:, 0, :] + step * direction
    res_ref[:, 0, :] = residual_ref[:, 0, :] - step * image_ref[...]
    dir_ref[:, 0, :] = fresh


def run(kernel, outs, args, scalars=(), anywhere=(), scratch=(), flops=100000, limit=None):
    spaces = [
        pltpu.SMEM if i in scalars else pl.ANY if i in anywhere else pltpu.VMEM
        for i in range(len(args))
    ]
    shapes = [jax.ShapeDtypeStruct(*out) for out in outs]
    found = pl.pallas_call(
        kernel,
        out_shape=shapes,
        in_specs=[pl.BlockSpec(memory_space=space) for space in spaces],
        out_specs=[pl.BlockSpec(memory_space=pltpu.VMEM) for _ in shapes],
        scratch_shapes=list(scratch),
        cost_estimate=pl.CostEstimate(flops=flops, bytes_accessed=1000000, transcendentals=0),
        compiler_params=pltpu.CompilerParams(vmem_limit_bytes=limit),
    )(*args)
    return found


def exchange(value, axes):
    return lax.all_to_all(value, axes, split_axis=0, concat_axis=0, tiled=True)


def on_device(
    design,
    gap_flags,
    segment_ids,
    ar_order,
    ma_order,
    ar_roots,
    ma_roots,
    kaula,
    precond,
    solution,
    residual,
    direction,
):
    f32, bf16 = jnp.float32, jnp.bfloat16
    count = lax.axis_size(TM)
    others = lax.axis_size(ORDER)
    everyone = count * others
    place = lax.axis_index(TM).astype(jnp.int32).reshape(1, 1)
    gaps = gap_flags.reshape(1, 128)
    (sheets,) = run(
        pack_kernel, [((count, 40, 128), bf16)], [direction, segment_ids.reshape(1, 128)]
    )
    tables = run(
        response_kernel,
        [
            ((3, 128, 128), f32),
            ((4, 8, 128), f32),
            ((4, 8, 128), f32),
            ((3, 8, 256), f32),
            ((LEVELS - 1, 10, 8, 128), f32),
            ((LEVELS - 1, 10, 8, 128), f32),
        ],
        [place, ar_order, ma_order, ar_roots, ma_roots],
        scalars=(0, 1, 2, 3, 4),
        flops=10000000,
    )
    got = exchange(sheets, TM)
    held = [
        pltpu.VMEM((CHUNKS, 3, 128, design.shape[2] // CHUNKS), bf16),
        pltpu.SemaphoreType.DMA((CHUNKS,)),
    ]
    (partial,) = run(
        observe_kernel,
        [((others, 16, 384), f32)],
        [got, design],
        anywhere=(1,),
        scratch=held,
        limit=VMEM_LIMIT,
    )
    parts = exchange(partial, ORDER)
    own, near, far = run(
        segment_kernel,
        [((3, 8, 128), f32), ((3, 128, 128), f32), ((3, 256, 128), f32)],
        [place, got, *tables],
        scalars=(0,),
        flops=10000000,
    )
    message, masked = run(
        state_kernel, [((count, 8, 128), f32), ((48, 128), f32)], [parts, gaps, own]
    )
    states = exchange(message, TM)
    (gradient,) = run(
        gradient_kernel,
        [((count, 16, 256), bf16)],
        [masked, near, far, gaps, states, design],
        anywhere=(5,),
        scratch=held,
        limit=VMEM_LIMIT,
    )
    arrived = exchange(gradient, TM)
    sums, image, applied, image_applied = run(
        image_kernel,
        [((everyone, 1, 128), f32)] + [((16, 256), f32)] * 3,
        [arrived, kaula, precond, residual, direction],
    )
    gathered = exchange(sums, TM_ORDER)
    return tuple(
        run(
            update_kernel,
            [((16, 1, 256), f32)] * 3,
            [gathered, image, applied, image_applied, solution, residual, direction],
        )
    )


def solution(mesh):
    split = Mesh(mesh.devices.reshape(4, 8, 4, 2), TM_ORDER)
    in_specs = (
        P(None, TM, ORDER),
        P(TM),
        P(TM),
        P(),
        P(),
        P(),
        P(),
        P(ORDER, TM),
        P(ORDER, TM, None, None),
        P(None, ORDER, TM),
        P(None, ORDER, TM),
        P(None, ORDER, TM),
    )
    out_specs = (P(None, ORDER, TM),) * 3
    return jax.shard_map(
        on_device, mesh=split, in_specs=in_specs, out_specs=out_specs, check_vma=False
    )
```

```python
import jax
import jax.numpy as jnp
from jax import lax
from jax.experimental import pallas as pl
from jax.experimental.pallas import tpu as pltpu
from jax.sharding import Mesh
from jax.sharding import PartitionSpec as P

TM = ("tm_0", "tm_1")
ORDER = ("order_0", "order_1")
TM_ORDER = TM + ORDER
CHUNKS = 8
VMEM_LIMIT = 50 * 1024 * 1024
PACK_LIMIT = 59 * 1024 * 1024
SMALL_LIMIT = 8 * 1024 * 1024

precise = lax.Precision.HIGHEST
LEVELS = 12
RADIX = 7


def dot(a, b, dims):
    return lax.dot_general(
        a, b, (dims, ((), ())), precision=precise, preferred_element_type=jnp.float32
    )


def splat_rows(read):
    row = lax.broadcasted_iota(jnp.int32, (8, 128), 0)
    out = jnp.zeros((8, 128), jnp.float32)
    for c in range(3):
        out = jnp.where(row == c, read(c), out)
    return out


LOWER = [(i, j) for i in range(4) for j in range(i + 1)]
UPPER = [(i, j) for i in range(4) for j in range(i, 4)]


def active_roots(roots_ref, order_ref):
    return [
        splat_rows(lambda c: jnp.where(k < order_ref[c], roots_ref[c, k], jnp.float32(0.0)))
        for k in range(4)
    ]


def sum_of(terms):
    while len(terms) > 1:
        terms = [
            terms[k] + terms[k + 1] if k + 1 < len(terms) else terms[k]
            for k in range(0, len(terms), 2)
        ]
    return terms[0]


def times(left, right):
    return {
        (i, j): sum_of([left[i, k] * right[k, j] for k in range(j, i + 1)]) for i, j in LOWER
    }


def gram_step(gram, power):
    half = {
        (i, j): sum_of([gram[min(i, k), max(i, k)] * power[k, j] for k in range(j, 4)])
        for i in range(4)
        for j in range(4)
    }
    return {(i, j): sum_of([power[k, i] * half[k, j] for k in range(i, 4)]) for i, j in UPPER}


def row_times(vector, power):
    return [sum_of([vector[i] * power[i, j] for i in range(j, 4)]) for j in range(4)]


def row_power(vector, powers, number, bits):
    for k in range(bits):
        on = ((number >> k) & 1) == 1
        moved = row_times(vector, powers[k])
        vector = [jnp.where(on, moved[j], vector[j]) for j in range(4)]
    return vector


def column_power(vector, powers, number, bits):
    for k in range(bits):
        on = ((number >> k) & 1) == 1
        moved = [sum_of([powers[k][i, j] * vector[j] for j in range(i + 1)]) for i in range(4)]
        vector = [jnp.where(on, moved[i], vector[i]) for i in range(4)]
    return vector


def response_kernel(
    place_ref, aro_ref, mao_ref, arr_ref, mar_ref, toep_ref, gam_ref, fin_ref, reach_ref, pow_ref, gram_ref
):
    poles = active_roots(arr_ref, aro_ref)
    zeros = active_roots(mar_ref, mao_ref)
    kappa = [poles[j] - zeros[j] for j in range(4)]
    one = jnp.ones((8, 128), jnp.float32)
    powers = [{(i, j): poles[i] if i == j else kappa[j] for i, j in LOWER}]
    for _ in range(LEVELS - 1):
        powers.append(times(powers[-1], powers[-1]))
    gram = {(i, j): kappa[i] * kappa[j] for i, j in UPPER}
    for k in range(LEVELS - 1):
        for at, (i, j) in enumerate(LOWER):
            pow_ref[k, at] = powers[k][i, j]
        for at, (i, j) in enumerate(UPPER):
            gram_ref[k, at] = gram[i, j]
        if k < LEVELS - 2:
            add = gram_step(gram, powers[k])
            gram = {at: gram[at] + add[at] for at in UPPER}
    lane = lax.broadcasted_iota(jnp.int32, (8, 128), 1)
    gam = row_power(kappa, powers, lane, RADIX)
    fin = column_power([one] * 4, powers, 127 - lane, RADIX)
    for i in range(4):
        gam_ref[i] = gam[i]
        fin_ref[i] = fin[i]
    eta = jnp.where(lane == 0, 1.0, pltpu.roll(sum_of(gam), 1, 1))
    big_row = lax.broadcasted_iota(jnp.int32, (128, 128), 0)
    big_lane = lax.broadcasted_iota(jnp.int32, (128, 128), 1)
    for c in range(3):
        base = jnp.broadcast_to(eta[c : c + 1, :], (128, 128))
        turned = pltpu.roll(base, 0, 1, stride=1, stride_axis=0)
        toep_ref[c] = jnp.where(big_lane >= big_row, turned, 0.0)
    place = place_ref[0, 0]
    row = lax.broadcasted_iota(jnp.int32, (8, 128), 0)
    front = row < 4
    for side in range(2):
        wide = lane + 128 * side
        peer, kind = wide >> 3, wide & 7
        gap = jnp.where(front, place - 1 - peer, peer - 1 - place)
        steps = jnp.maximum(gap, 0)
        for c in range(3):
            vector = [jnp.where((row & 3) == j, 1.0, 0.0) for j in range(4)]
            for k in range(5):
                cut = {at: powers[RADIX + k][at][c : c + 1, :] for at in LOWER}
                on = ((steps >> k) & 1) == 1
                moved = []
                for j in range(4):
                    terms = [vector[j] * cut[j, j]]
                    for i in range(4):
                        if i > j:
                            terms.append(vector[i] * jnp.where(front, cut[i, j], 0.0))
                        if i < j:
                            terms.append(vector[i] * jnp.where(front, 0.0, cut[j, i]))
                    moved.append(sum_of(terms))
                vector = [jnp.where(on, moved[j], vector[j]) for j in range(4)]
            picked = jnp.zeros((8, 128), jnp.float32)
            for j in range(4):
                picked = jnp.where((kind & 3) == j, vector[j], picked)
            used = ((kind < 4) == front) & (gap >= 0)
            reach_ref[c, :, 128 * side : 128 * side + 128] = jnp.where(used, picked, 0.0)


def segment_kernel(
    place_ref, got_ref, toep_ref, gam_ref, fin_ref, reach_ref, pow_ref, gram_ref, own_ref, near_ref, far_ref
):
    place = place_ref[0, 0]
    ids = got_ref[:, 32:40, :].astype(jnp.float32)
    peer = lax.broadcasted_iota(jnp.int32, (32, 8, 128), 0)
    mine = jnp.sum(jnp.where(peer == place, ids, 0.0), axis=0)
    before = jnp.sum(jnp.where(peer == place - 1, ids, 0.0), axis=0)
    ends = jnp.broadcast_to(ids[:, :, 127:128], (32, 8, 128))
    last = jnp.broadcast_to(mine[:, 127:128], (8, 128))
    prev = jnp.where(place > 0, jnp.broadcast_to(before[:, 127:128], (8, 128)), -1.0)
    count = jnp.sum(jnp.where((peer > place) & (ids == last[None]), 1.0, 0.0), axis=0)
    left = jnp.broadcast_to(jnp.sum(count, axis=1, keepdims=True), (8, 128)).astype(jnp.int32)
    ends_before = jnp.concatenate([ends[:1], ends[:-1]], axis=0)
    sub = lax.broadcasted_iota(jnp.int32, (32, 8, 128), 1)
    keep = jnp.where(
        sub < 4,
        jnp.where((peer < place) & (ends == prev[None]), 1.0, 0.0),
        jnp.where((peer > place) & (ends_before == last[None]), 1.0, 0.0),
    ).reshape(256, 128)
    gram = {at: jnp.zeros((8, 128), jnp.float32) for at in UPPER}
    for k in range(LEVELS - 1):
        power = {pair: pow_ref[k, at] for at, pair in enumerate(LOWER)}
        add = gram_step(gram, power)
        on = ((left >> k) & 1) == 1
        gram = {
            pair: jnp.where(on, gram_ref[k, at] + add[pair], gram[pair])
            for at, pair in enumerate(UPPER)
        }
    lead = jnp.where(mine == prev, 1.0, 0.0)
    trail = jnp.where(mine == last, 1.0, 0.0)
    cont = jnp.where(last == prev, 1.0, 0.0)
    fin = [fin_ref[i] * trail for i in range(4)]
    gam = [gam_ref[i] * lead for i in range(4)]
    fold = [
        sum_of([fin[j] * gram[min(i, j), max(i, j)] for j in range(4)]) for i in range(4)
    ]
    block = {pair: pow_ref[RADIX, at] for at, pair in enumerate(LOWER)}
    past = [cont * value for value in row_times(fold, block)]
    row = lax.broadcasted_iota(jnp.int32, (8, 128), 0)
    big_row = lax.broadcasted_iota(jnp.int32, (128, 128), 0)
    big_lane = lax.broadcasted_iota(jnp.int32, (128, 128), 1)
    wide = jnp.broadcast_to(mine[0:1, :], (128, 128))
    tall = jnp.sum(jnp.where(big_row == big_lane, wide, 0.0), axis=1, keepdims=True)
    same = wide == jnp.broadcast_to(tall, (128, 128))

    def rows(values, c, start):
        out = jnp.zeros((8, 128), jnp.float32)
        for i in range(4):
            out = jnp.where(row == start + i, values[i][c : c + 1, :], out)
        return out

    for c in range(3):
        toep = jnp.where(same, toep_ref[c], 0.0)
        probe = dot(rows(gam, c, 0), toep, ((1,), (1,)))
        out_p = jnp.where(row < 4, probe, 0.0) + rows(past, c, 0)
        fin_low = rows(fin, c, 0)
        near_ref[c] = dot(toep, toep, ((1,), (1,))) + dot(rows(fold, c, 0), fin_low, ((0,), (0,)))
        own_ref[c] = fin_low + pltpu.roll(out_p, 4, 0)
        far_ref[c] = keep * dot(reach_ref[c], out_p + rows(fin, c, 4), ((0,), (0,)))


def state_kernel(parts_ref, gaps_ref, own_ref, message_ref, masked_ref):
    total = parts_ref[0]
    for o in range(1, parts_ref.shape[0]):
        total = total + parts_ref[o]
    gaps = gaps_ref[...].astype(jnp.float32)
    masked = jnp.concatenate([total[:, 128 * c : 128 * c + 128] * gaps for c in range(3)], axis=0)
    masked_ref[...] = masked
    padded = jnp.concatenate([masked, jnp.zeros((80, 128), jnp.float32)], axis=0)
    lane = lax.broadcasted_iota(jnp.int32, (8, 128), 1)
    out = jnp.zeros((8, 128), jnp.float32)
    for c in range(3):
        out = jnp.where((lane >> 4) == c, dot(own_ref[c], padded, ((1,), (1,))), out)
    message_ref[...] = jnp.broadcast_to(out[None], message_ref.shape)


def weighted_rows(masked_ref, near_ref, far_ref, gaps_ref, states_ref):
    gaps = gaps_ref[...].astype(jnp.float32)
    states = states_ref[...].reshape(256, 128)
    pieces = []
    for c in range(3):
        here = dot(masked_ref[16 * c : 16 * c + 16, :], near_ref[c], ((1,), (0,)))
        there = dot(states, far_ref[c], ((0,), (0,)))[16 * c : 16 * c + 16, :]
        pieces.append((here + there) * gaps)
    return pieces


def pack_kernel(direction_ref, ids_ref, out_ref):
    packed = direction_ref[:, 0, :].astype(jnp.bfloat16)
    ids = jnp.broadcast_to(ids_ref[...].astype(jnp.float32), (8, 128)).astype(jnp.bfloat16)
    sheet = jnp.concatenate([packed[:, :128], packed[:, 128:], ids], axis=0)
    out_ref[...] = jnp.broadcast_to(sheet[None], out_ref.shape)


def chunk_copies(design_ref, held_ref, sems):
    width = held_ref.shape[3]
    return [
        pltpu.make_async_copy(
            design_ref.at[:, :, pl.ds(width * k, width)], held_ref.at[k], sems.at[k]
        )
        for k in range(held_ref.shape[0])
    ]


def observe_kernel(got_ref, design_ref, early_ref, out_ref, held_ref, sems):
    copies = chunk_copies(design_ref, held_ref, sems)
    for copy in copies:
        copy.start()
    count, _, _, width = held_ref.shape
    peers = width // 256
    total = jnp.zeros((384, 128), jnp.float32)
    for k in range(count):
        pieces = []
        for p in range(peers * k, peers * k + peers):
            pieces += [got_ref[p, 0:16, :], got_ref[p, 16:32, :]]
        packed = jnp.concatenate(pieces, axis=1)
        packed = jnp.concatenate([packed, jnp.zeros((112, width), jnp.bfloat16)], axis=0)
        copies[k].wait()
        total = total + lax.dot_general(
            held_ref[k].reshape(384, width),
            packed,
            (((1,), (1,)), ((), ())),
            preferred_element_type=jnp.float32,
        )
    out_ref[...] = jnp.broadcast_to(total.T[None, 0:16, :], out_ref.shape)


def gradient_kernel(
    masked_ref, near_ref, far_ref, gaps_ref, states_ref, design_ref, out_ref, held_ref, sems
):
    copies = chunk_copies(design_ref, held_ref, sems)
    for copy in copies:
        copy.start()
    pieces = weighted_rows(masked_ref, near_ref, far_ref, gaps_ref, states_ref)
    weighted = jnp.concatenate(pieces, axis=1).astype(jnp.bfloat16)
    count, _, _, width = held_ref.shape
    peers = width // 256
    for k in range(count):
        copies[k].wait()
        part = jnp.dot(
            weighted, held_ref[k].reshape(384, width), preferred_element_type=jnp.float32
        ).astype(jnp.bfloat16)
        for p in range(peers):
            out_ref[peers * k + p] = part[:, 256 * p : 256 * p + 256]


def image_kernel(
    arrived_ref, kaula_ref, precond_ref, residual_ref, direction_ref, message_ref, image_ref, applied_ref, both_ref
):
    total = arrived_ref[0].astype(jnp.float32)
    for p in range(1, arrived_ref.shape[0]):
        total = total + arrived_ref[p].astype(jnp.float32)
    direction = direction_ref[:, 0, :]
    residual = residual_ref[:, 0, :]
    image = total + kaula_ref[...] * direction
    stack = jnp.concatenate([residual, image], axis=0)
    mixed = jnp.concatenate(
        [dot(stack[:, 128 * k : 128 * k + 128], precond_ref[0, k], ((1,), (1,))) for k in range(2)],
        axis=1,
    )
    applied, image_applied = mixed[0:16], mixed[16:32]
    products = jnp.concatenate(
        [
            residual * applied,
            direction * image,
            image * applied,
            image * image_applied,
            jnp.zeros((64, 256), jnp.float32),
        ],
        axis=0,
    )
    sums = dot(jnp.ones((8, 256), jnp.float32), products, ((1,), (1,)))
    message_ref[...] = jnp.broadcast_to(sums[None, 0:1, :], message_ref.shape)
    image_ref[...] = image
    applied_ref[...] = applied
    both_ref[...] = image_applied


def update_kernel(
    sums_ref, image_ref, applied_ref, both_ref, solution_ref, residual_ref, direction_ref, sol_ref, res_ref, dir_ref
):
    total = jnp.sum(sums_ref[...], axis=0)
    row = lax.broadcasted_iota(jnp.int32, (16, 128), 0)
    lane = lax.broadcasted_iota(jnp.int32, (16, 128), 1)
    wide = jnp.broadcast_to(total, (16, 128))
    old_rz, curvature, cross, square = [
        jnp.sum(jnp.where(lane == row + 16 * k, wide, 0.0), axis=1, keepdims=True)
        for k in range(4)
    ]
    step = old_rz / curvature
    new_rz = old_rz - 2.0 * step * cross + step * step * square
    direction = direction_ref[:, 0, :]
    fresh = applied_ref[...] - step * both_ref[...] + (new_rz / old_rz) * direction
    sol_ref[:, 0, :] = solution_ref[:, 0, :] + step * direction
    res_ref[:, 0, :] = residual_ref[:, 0, :] - step * image_ref[...]
    dir_ref[:, 0, :] = fresh


def run(kernel, outs, args, scalars=(), anywhere=(), scratch=(), flops=100000, limit=SMALL_LIMIT):
    spaces = [
        pltpu.SMEM if i in scalars else pltpu.HBM if i in anywhere else pltpu.VMEM
        for i in range(len(args))
    ]
    shapes = [jax.ShapeDtypeStruct(*out) for out in outs]
    found = pl.pallas_call(
        kernel,
        out_shape=shapes,
        in_specs=[pl.BlockSpec(memory_space=space) for space in spaces],
        out_specs=[pl.BlockSpec(memory_space=pltpu.VMEM) for _ in shapes],
        scratch_shapes=list(scratch),
        cost_estimate=pl.CostEstimate(flops=flops, bytes_accessed=1000000, transcendentals=0),
        compiler_params=pltpu.CompilerParams(vmem_limit_bytes=limit),
    )(*args)
    return found


def exchange(value, axes):
    return lax.all_to_all(value, axes, split_axis=0, concat_axis=0, tiled=True)


def on_device(
    design,
    gap_flags,
    segment_ids,
    ar_order,
    ma_order,
    ar_roots,
    ma_roots,
    kaula,
    precond,
    solution,
    residual,
    direction,
):
    f32, bf16 = jnp.float32, jnp.bfloat16
    count = lax.axis_size(TM)
    others = lax.axis_size(ORDER)
    everyone = count * others
    place = lax.axis_index(TM).astype(jnp.int32).reshape(1, 1)
    gaps = gap_flags.reshape(1, 128)
    (sheets,) = run(
        pack_kernel,
        [((count, 40, 128), bf16)],
        [direction, segment_ids.reshape(1, 128)],
        limit=PACK_LIMIT,
    )
    tables = run(
        response_kernel,
        [
            ((3, 128, 128), f32),
            ((4, 8, 128), f32),
            ((4, 8, 128), f32),
            ((3, 8, 256), f32),
            ((LEVELS - 1, 10, 8, 128), f32),
            ((LEVELS - 1, 10, 8, 128), f32),
        ],
        [place, ar_order, ma_order, ar_roots, ma_roots],
        scalars=(0, 1, 2, 3, 4),
        flops=10000000,
    )
    got = exchange(sheets, TM)
    held = [
        pltpu.VMEM((CHUNKS, 3, 128, design.shape[2] // CHUNKS), bf16),
        pltpu.SemaphoreType.DMA((CHUNKS,)),
    ]
    (partial,) = run(
        observe_kernel,
        [((others, 16, 384), f32)],
        [got, design, tables[2]],
        anywhere=(1,),
        scratch=held,
        limit=VMEM_LIMIT,
    )
    parts = exchange(partial, ORDER)
    own, near, far = run(
        segment_kernel,
        [((3, 8, 128), f32), ((3, 128, 128), f32), ((3, 256, 128), f32)],
        [place, got, *tables],
        scalars=(0,),
        flops=10000000,
    )
    message, masked = run(
        state_kernel, [((count, 8, 128), f32), ((48, 128), f32)], [parts, gaps, own]
    )
    states = exchange(message, TM)
    (gradient,) = run(
        gradient_kernel,
        [((count, 16, 256), bf16)],
        [masked, near, far, gaps, states, design],
        anywhere=(5,),
        scratch=held,
        limit=VMEM_LIMIT,
    )
    arrived = exchange(gradient, TM)
    sums, image, applied, image_applied = run(
        image_kernel,
        [((everyone, 1, 128), f32)] + [((16, 256), f32)] * 3,
        [arrived, kaula, precond, residual, direction],
    )
    gathered = exchange(sums, TM_ORDER)
    return tuple(
        run(
            update_kernel,
            [((16, 1, 256), f32)] * 3,
            [gathered, image, applied, image_applied, solution, residual, direction],
        )
    )


def solution(mesh):
    split = Mesh(mesh.devices.reshape(4, 8, 4, 2), TM_ORDER)
    in_specs = (
        P(None, TM, ORDER),
        P(TM),
        P(TM),
        P(),
        P(),
        P(),
        P(),
        P(ORDER, TM),
        P(ORDER, TM, None, None),
        P(None, ORDER, TM),
        P(None, ORDER, TM),
        P(None, ORDER, TM),
    )
    out_specs = (P(None, ORDER, TM),) * 3
    return jax.shard_map(
        on_device, mesh=split, in_specs=in_specs, out_specs=out_specs, check_vma=False
    )
```

```python
import jax
import jax.numpy as jnp
from jax import lax
from jax.experimental import pallas as pl
from jax.experimental.pallas import tpu as pltpu
from jax.sharding import Mesh
from jax.sharding import PartitionSpec as P

TM = ("tm_0", "tm_1")
ORDER = ("order_0", "order_1")
TM_ORDER = TM + ORDER
VMEM_LIMIT = 50 * 1024 * 1024
PACK_LIMIT = 59 * 1024 * 1024
SMALL_LIMIT = 8 * 1024 * 1024

precise = lax.Precision.HIGHEST
LEVELS = 12
RADIX = 7


def dot(a, b, dims):
    return lax.dot_general(
        a, b, (dims, ((), ())), precision=precise, preferred_element_type=jnp.float32
    )


def splat_rows(read):
    row = lax.broadcasted_iota(jnp.int32, (8, 128), 0)
    out = jnp.zeros((8, 128), jnp.float32)
    for c in range(3):
        out = jnp.where(row == c, read(c), out)
    return out


LOWER = [(i, j) for i in range(4) for j in range(i + 1)]
UPPER = [(i, j) for i in range(4) for j in range(i, 4)]


def active_roots(roots_ref, order_ref):
    return [
        splat_rows(lambda c: jnp.where(k < order_ref[c], roots_ref[c, k], jnp.float32(0.0)))
        for k in range(4)
    ]


def sum_of(terms):
    while len(terms) > 1:
        terms = [
            terms[k] + terms[k + 1] if k + 1 < len(terms) else terms[k]
            for k in range(0, len(terms), 2)
        ]
    return terms[0]


def times(left, right):
    return {
        (i, j): sum_of([left[i, k] * right[k, j] for k in range(j, i + 1)]) for i, j in LOWER
    }


def gram_step(gram, power):
    half = {
        (i, j): sum_of([gram[min(i, k), max(i, k)] * power[k, j] for k in range(j, 4)])
        for i in range(4)
        for j in range(4)
    }
    return {(i, j): sum_of([power[k, i] * half[k, j] for k in range(i, 4)]) for i, j in UPPER}


def row_times(vector, power):
    return [sum_of([vector[i] * power[i, j] for i in range(j, 4)]) for j in range(4)]


def row_power(vector, powers, number, bits):
    for k in range(bits):
        on = ((number >> k) & 1) == 1
        moved = row_times(vector, powers[k])
        vector = [jnp.where(on, moved[j], vector[j]) for j in range(4)]
    return vector


def column_power(vector, powers, number, bits):
    for k in range(bits):
        on = ((number >> k) & 1) == 1
        moved = [sum_of([powers[k][i, j] * vector[j] for j in range(i + 1)]) for i in range(4)]
        vector = [jnp.where(on, moved[i], vector[i]) for i in range(4)]
    return vector


def response_kernel(
    place_ref, aro_ref, mao_ref, arr_ref, mar_ref, toep_ref, gam_ref, fin_ref, reach_ref, pow_ref, gram_ref
):
    poles = active_roots(arr_ref, aro_ref)
    zeros = active_roots(mar_ref, mao_ref)
    kappa = [poles[j] - zeros[j] for j in range(4)]
    one = jnp.ones((8, 128), jnp.float32)
    powers = [{(i, j): poles[i] if i == j else kappa[j] for i, j in LOWER}]
    for _ in range(LEVELS - 1):
        powers.append(times(powers[-1], powers[-1]))
    gram = {(i, j): kappa[i] * kappa[j] for i, j in UPPER}
    for k in range(LEVELS - 1):
        for at, (i, j) in enumerate(LOWER):
            pow_ref[k, at] = powers[k][i, j]
        for at, (i, j) in enumerate(UPPER):
            gram_ref[k, at] = gram[i, j]
        if k < LEVELS - 2:
            add = gram_step(gram, powers[k])
            gram = {at: gram[at] + add[at] for at in UPPER}
    lane = lax.broadcasted_iota(jnp.int32, (8, 128), 1)
    gam = row_power(kappa, powers, lane, RADIX)
    fin = column_power([one] * 4, powers, 127 - lane, RADIX)
    for i in range(4):
        gam_ref[i] = gam[i]
        fin_ref[i] = fin[i]
    eta = jnp.where(lane == 0, 1.0, pltpu.roll(sum_of(gam), 1, 1))
    big_row = lax.broadcasted_iota(jnp.int32, (128, 128), 0)
    big_lane = lax.broadcasted_iota(jnp.int32, (128, 128), 1)
    for c in range(3):
        base = jnp.broadcast_to(eta[c : c + 1, :], (128, 128))
        turned = pltpu.roll(base, 0, 1, stride=1, stride_axis=0)
        toep_ref[c] = jnp.where(big_lane >= big_row, turned, 0.0)
    place = place_ref[0, 0]
    row = lax.broadcasted_iota(jnp.int32, (8, 128), 0)
    front = row < 4
    for side in range(2):
        wide = lane + 128 * side
        peer, kind = wide & 31, wide >> 5
        gap = jnp.where(front, place - 1 - peer, peer - 1 - place)
        steps = jnp.maximum(gap, 0)
        for c in range(3):
            vector = [jnp.where((row & 3) == j, 1.0, 0.0) for j in range(4)]
            for k in range(5):
                cut = {at: powers[RADIX + k][at][c : c + 1, :] for at in LOWER}
                on = ((steps >> k) & 1) == 1
                moved = []
                for j in range(4):
                    terms = [vector[j] * cut[j, j]]
                    for i in range(4):
                        if i > j:
                            terms.append(vector[i] * jnp.where(front, cut[i, j], 0.0))
                        if i < j:
                            terms.append(vector[i] * jnp.where(front, 0.0, cut[j, i]))
                    moved.append(sum_of(terms))
                vector = [jnp.where(on, moved[j], vector[j]) for j in range(4)]
            picked = jnp.zeros((8, 128), jnp.float32)
            for j in range(4):
                picked = jnp.where((kind & 3) == j, vector[j], picked)
            used = ((kind < 4) == front) & (gap >= 0)
            reach_ref[c, :, 128 * side : 128 * side + 128] = jnp.where(used, picked, 0.0)


def segment_kernel(
    place_ref, got_ref, toep_ref, gam_ref, fin_ref, reach_ref, pow_ref, gram_ref, own_ref, near_ref, far_ref
):
    place = place_ref[0, 0]
    row = lax.broadcasted_iota(jnp.int32, (8, 128), 0)
    groups = []
    for g in range(4):
        group = jnp.zeros((8, 128), jnp.float32)
        for s in range(8):
            group = jnp.where(row == s, got_ref[8 * g + s, 32:40, :].astype(jnp.float32), group)
        groups.append(group)
    ids = jnp.concatenate(groups, axis=0)
    peer = lax.broadcasted_iota(jnp.int32, (32, 128), 0)
    mine = jnp.sum(jnp.where(peer == place, ids, 0.0), axis=0, keepdims=True)
    before = jnp.sum(jnp.where(peer == place - 1, ids, 0.0), axis=0, keepdims=True)
    ends = jnp.broadcast_to(ids[:, 127:128], (32, 128))
    last = jnp.broadcast_to(mine[:, 127:128], (1, 128))
    prev = jnp.where(place > 0, jnp.broadcast_to(before[:, 127:128], (1, 128)), -1.0)
    count = jnp.sum(
        jnp.where((peer > place) & (ids == last), 1.0, 0.0), axis=0, keepdims=True
    )
    left = jnp.sum(count, axis=1, keepdims=True).astype(jnp.int32)
    left = jnp.broadcast_to(left, (8, 128))
    ends_before = pltpu.roll(ends, 1, 0)
    keep_past = jnp.where((peer < place) & (ends == prev), 1.0, 0.0)
    keep_next = jnp.where((peer > place) & (ends_before == last), 1.0, 0.0)
    keep = jnp.concatenate([keep_past] * 4 + [keep_next] * 4, axis=0)
    gram = {at: jnp.zeros((8, 128), jnp.float32) for at in UPPER}
    for k in range(LEVELS - 1):
        power = {pair: pow_ref[k, at] for at, pair in enumerate(LOWER)}
        add = gram_step(gram, power)
        on = ((left >> k) & 1) == 1
        gram = {
            pair: jnp.where(on, gram_ref[k, at] + add[pair], gram[pair])
            for at, pair in enumerate(UPPER)
        }
    lead = jnp.where(mine == prev, 1.0, 0.0)
    trail = jnp.where(mine == last, 1.0, 0.0)
    cont = jnp.where(last == prev, 1.0, 0.0)
    fin = [fin_ref[i] * trail for i in range(4)]
    gam = [gam_ref[i] * lead for i in range(4)]
    fold = [
        sum_of([fin[j] * gram[min(i, j), max(i, j)] for j in range(4)]) for i in range(4)
    ]
    block = {pair: pow_ref[RADIX, at] for at, pair in enumerate(LOWER)}
    past = [cont * value for value in row_times(fold, block)]
    big_row = lax.broadcasted_iota(jnp.int32, (128, 128), 0)
    big_lane = lax.broadcasted_iota(jnp.int32, (128, 128), 1)
    wide = jnp.broadcast_to(mine, (128, 128))
    tall = jnp.sum(jnp.where(big_row == big_lane, wide, 0.0), axis=1, keepdims=True)
    same = wide == jnp.broadcast_to(tall, (128, 128))

    def rows(values, c, start):
        out = jnp.zeros((8, 128), jnp.float32)
        for i in range(4):
            out = jnp.where(row == start + i, values[i][c : c + 1, :], out)
        return out

    for c in range(3):
        toep = jnp.where(same, toep_ref[c], 0.0)
        probe = dot(rows(gam, c, 0), toep, ((1,), (1,)))
        out_p = jnp.where(row < 4, probe, 0.0) + rows(past, c, 0)
        fin_low = rows(fin, c, 0)
        near_ref[c] = dot(toep, toep, ((1,), (1,))) + dot(rows(fold, c, 0), fin_low, ((0,), (0,)))
        own_ref[c] = fin_low + pltpu.roll(out_p, 4, 0)
        far_ref[c] = keep * dot(reach_ref[c], out_p + rows(fin, c, 4), ((0,), (0,)))


def state_kernel(parts_ref, gaps_ref, own_ref, message_ref, masked_ref):
    total = parts_ref[0].astype(jnp.float32)
    for o in range(1, parts_ref.shape[0]):
        total = total + parts_ref[o].astype(jnp.float32)
    gaps = gaps_ref[...].astype(jnp.float32)
    rows = []
    for c in range(3):
        masked = total[:, 128 * c : 128 * c + 128] * gaps
        masked_ref[16 * c : 16 * c + 16, :] = masked
        padded = jnp.concatenate([masked, jnp.zeros((112, 128), jnp.float32)], axis=0)
        spread = pltpu.roll(
            dot(own_ref[c], padded, ((1,), (1,))), 0, 1, stride=16, stride_axis=0
        )
        rows.append(jnp.sum(spread, axis=0, keepdims=True))
    message_ref[...] = jnp.broadcast_to(jnp.concatenate(rows, axis=0)[None], message_ref.shape)


def weighted_rows(masked_ref, near_ref, far_ref, gaps_ref, states_ref):
    gaps = gaps_ref[...].astype(jnp.float32)
    pieces = []
    for c in range(3):
        here = dot(masked_ref[16 * c : 16 * c + 16, :], near_ref[c], ((1,), (0,)))
        states = states_ref[:, c, :]
        turned = [states] + [pltpu.roll(states, 128 - 16 * i, 1) for i in range(1, 8)]
        there = dot(jnp.concatenate(turned, axis=0), far_ref[c], ((0,), (0,)))[0:16, :]
        pieces.append((here + there) * gaps)
    return pieces


def pack_kernel(direction_ref, ids_ref, out_ref):
    packed = direction_ref[:, 0, :].astype(jnp.bfloat16)
    ids = jnp.broadcast_to(ids_ref[...].astype(jnp.float32), (8, 128)).astype(jnp.bfloat16)
    sheet = jnp.concatenate([packed[:, :128], packed[:, 128:], ids], axis=0)
    out_ref[...] = jnp.broadcast_to(sheet[None], out_ref.shape)


def chunk_copies(design_ref, held_ref, sems):
    width = held_ref.shape[3]
    return [
        pltpu.make_async_copy(
            design_ref.at[:, :, pl.ds(width * k, width)], held_ref.at[k], sems.at[k]
        )
        for k in range(held_ref.shape[0])
    ]


def observe_kernel(got_ref, design_ref, early_ref, out_ref, held_ref, sems):
    copies = chunk_copies(design_ref, held_ref, sems)
    for copy in copies:
        copy.start()
    count, _, _, width = held_ref.shape
    peers = width // 256
    total = jnp.zeros((16, 384), jnp.float32)
    for k in range(count):
        pieces = []
        for p in range(peers * k, peers * k + peers):
            pieces += [got_ref[p, 0:16, :], got_ref[p, 16:32, :]]
        packed = jnp.concatenate(pieces, axis=1)
        copies[k].wait()
        total = total + lax.dot_general(
            packed,
            held_ref[k].reshape(384, width),
            (((1,), (1,)), ((), ())),
            preferred_element_type=jnp.float32,
        )
    out_ref[...] = jnp.broadcast_to(total.astype(jnp.bfloat16)[None], out_ref.shape)


def gradient_kernel(
    masked_ref, near_ref, far_ref, gaps_ref, states_ref, design_ref, out_ref, held_ref, sems
):
    copies = chunk_copies(design_ref, held_ref, sems)
    for copy in copies:
        copy.start()
    pieces = weighted_rows(masked_ref, near_ref, far_ref, gaps_ref, states_ref)
    weighted = jnp.concatenate(pieces, axis=1).astype(jnp.bfloat16)
    count, _, _, width = held_ref.shape
    peers = width // 256
    for k in range(count):
        copies[k].wait()
        part = jnp.dot(
            weighted, held_ref[k].reshape(384, width), preferred_element_type=jnp.float32
        ).astype(jnp.bfloat16)
        for p in range(peers):
            out_ref[peers * k + p] = part[:, 256 * p : 256 * p + 256]


def image_kernel(
    arrived_ref, kaula_ref, precond_ref, residual_ref, direction_ref, message_ref, image_ref, applied_ref, both_ref
):
    total = arrived_ref[0].astype(jnp.float32)
    for p in range(1, arrived_ref.shape[0]):
        total = total + arrived_ref[p].astype(jnp.float32)
    direction = direction_ref[:, 0, :]
    residual = residual_ref[:, 0, :]
    image = total + kaula_ref[...] * direction
    stack = jnp.concatenate([residual, image], axis=0)
    mixed = jnp.concatenate(
        [dot(stack[:, 128 * k : 128 * k + 128], precond_ref[0, k], ((1,), (1,))) for k in range(2)],
        axis=1,
    )
    applied, image_applied = mixed[0:16], mixed[16:32]
    products = jnp.concatenate(
        [
            residual * applied,
            direction * image,
            image * applied,
            image * image_applied,
            jnp.zeros((64, 256), jnp.float32),
        ],
        axis=0,
    )
    sums = dot(jnp.ones((8, 256), jnp.float32), products, ((1,), (1,)))
    message_ref[...] = jnp.broadcast_to(sums[None, 0:1, :], message_ref.shape)
    image_ref[...] = image
    applied_ref[...] = applied
    both_ref[...] = image_applied


def update_kernel(
    sums_ref, image_ref, applied_ref, both_ref, solution_ref, residual_ref, direction_ref, sol_ref, res_ref, dir_ref
):
    total = jnp.sum(sums_ref[...], axis=0)
    row = lax.broadcasted_iota(jnp.int32, (16, 128), 0)
    lane = lax.broadcasted_iota(jnp.int32, (16, 128), 1)
    wide = jnp.broadcast_to(total, (16, 128))
    old_rz, curvature, cross, square = [
        jnp.sum(jnp.where(lane == row + 16 * k, wide, 0.0), axis=1, keepdims=True)
        for k in range(4)
    ]
    step = old_rz / curvature
    new_rz = old_rz - 2.0 * step * cross + step * step * square
    direction = direction_ref[:, 0, :]
    fresh = applied_ref[...] - step * both_ref[...] + (new_rz / old_rz) * direction
    sol_ref[:, 0, :] = solution_ref[:, 0, :] + step * direction
    res_ref[:, 0, :] = residual_ref[:, 0, :] - step * image_ref[...]
    dir_ref[:, 0, :] = fresh


def run(kernel, outs, args, scalars=(), anywhere=(), scratch=(), flops=100000, limit=SMALL_LIMIT):
    spaces = [
        pltpu.SMEM if i in scalars else pltpu.HBM if i in anywhere else pltpu.VMEM
        for i in range(len(args))
    ]
    shapes = [jax.ShapeDtypeStruct(*out) for out in outs]
    found = pl.pallas_call(
        kernel,
        out_shape=shapes,
        in_specs=[pl.BlockSpec(memory_space=space) for space in spaces],
        out_specs=[pl.BlockSpec(memory_space=pltpu.VMEM) for _ in shapes],
        scratch_shapes=list(scratch),
        cost_estimate=pl.CostEstimate(flops=flops, bytes_accessed=1000000, transcendentals=0),
        compiler_params=pltpu.CompilerParams(vmem_limit_bytes=limit),
    )(*args)
    return found


def exchange(value, axes):
    return lax.all_to_all(value, axes, split_axis=0, concat_axis=0, tiled=True)


def on_device(
    design,
    gap_flags,
    segment_ids,
    ar_order,
    ma_order,
    ar_roots,
    ma_roots,
    kaula,
    precond,
    solution,
    residual,
    direction,
):
    f32, bf16 = jnp.float32, jnp.bfloat16
    count = lax.axis_size(TM)
    others = lax.axis_size(ORDER)
    everyone = count * others
    place = lax.axis_index(TM).astype(jnp.int32).reshape(1, 1)
    gaps = gap_flags.reshape(1, 128)
    (sheets,) = run(
        pack_kernel,
        [((count, 40, 128), bf16)],
        [direction, segment_ids.reshape(1, 128)],
        limit=PACK_LIMIT,
    )
    tables = run(
        response_kernel,
        [
            ((3, 128, 128), f32),
            ((4, 8, 128), f32),
            ((4, 8, 128), f32),
            ((3, 8, 256), f32),
            ((LEVELS - 1, 10, 8, 128), f32),
            ((LEVELS - 1, 10, 8, 128), f32),
        ],
        [place, ar_order, ma_order, ar_roots, ma_roots],
        scalars=(0, 1, 2, 3, 4),
        flops=10000000,
    )
    got = exchange(sheets, TM)

    def held(chunks):
        return [
            pltpu.VMEM((chunks, 3, 128, design.shape[2] // chunks), bf16),
            pltpu.SemaphoreType.DMA((chunks,)),
        ]

    (partial,) = run(
        observe_kernel,
        [((others, 16, 384), bf16)],
        [got, design, tables[2]],
        anywhere=(1,),
        scratch=held(16),
        limit=VMEM_LIMIT,
    )
    parts = exchange(partial, ORDER)
    own, near, far = run(
        segment_kernel,
        [((3, 8, 128), f32), ((3, 128, 128), f32), ((3, 256, 128), f32)],
        [place, got, *tables],
        scalars=(0,),
        flops=10000000,
    )
    message, masked = run(
        state_kernel, [((count, 3, 128), f32), ((48, 128), f32)], [parts, gaps, own]
    )
    states = exchange(message, TM)
    (gradient,) = run(
        gradient_kernel,
        [((count, 16, 256), bf16)],
        [masked, near, far, gaps, states, design],
        anywhere=(5,),
        scratch=held(8),
        limit=VMEM_LIMIT,
    )
    arrived = exchange(gradient, TM)
    sums, image, applied, image_applied = run(
        image_kernel,
        [((everyone, 1, 128), f32)] + [((16, 256), f32)] * 3,
        [arrived, kaula, precond, residual, direction],
    )
    gathered = exchange(sums, TM_ORDER)
    return tuple(
        run(
            update_kernel,
            [((16, 1, 256), f32)] * 3,
            [gathered, image, applied, image_applied, solution, residual, direction],
        )
    )


def solution(mesh):
    split = Mesh(mesh.devices.reshape(4, 8, 4, 2), TM_ORDER)
    in_specs = (
        P(None, TM, ORDER),
        P(TM),
        P(TM),
        P(),
        P(),
        P(),
        P(),
        P(ORDER, TM),
        P(ORDER, TM, None, None),
        P(None, ORDER, TM),
        P(None, ORDER, TM),
        P(None, ORDER, TM),
    )
    out_specs = (P(None, ORDER, TM),) * 3
    return jax.shard_map(
        on_device, mesh=split, in_specs=in_specs, out_specs=out_specs, check_vma=False
    )
```

```python
import jax
import jax.numpy as jnp
from jax import lax
from jax.experimental import pallas as pl
from jax.experimental.pallas import tpu as pltpu
from jax.sharding import Mesh
from jax.sharding import PartitionSpec as P

TM = ("tm_0", "tm_1")
ORDER = ("order_0", "order_1")
TM_ORDER = TM + ORDER
VMEM_LIMIT = 50 * 1024 * 1024
SMALL_LIMIT = 8 * 1024 * 1024

precise = lax.Precision.HIGHEST
LEVELS = 12
RADIX = 7


def dot(a, b, dims):
    return lax.dot_general(
        a, b, (dims, ((), ())), precision=precise, preferred_element_type=jnp.float32
    )


def splat_rows(read):
    row = lax.broadcasted_iota(jnp.int32, (8, 128), 0)
    out = jnp.zeros((8, 128), jnp.float32)
    for c in range(3):
        out = jnp.where(row == c, read(c), out)
    return out


LOWER = [(i, j) for i in range(4) for j in range(i + 1)]
UPPER = [(i, j) for i in range(4) for j in range(i, 4)]


def active_roots(roots_ref, order_ref):
    return [
        splat_rows(lambda c: jnp.where(k < order_ref[c], roots_ref[c, k], jnp.float32(0.0)))
        for k in range(4)
    ]


def sum_of(terms):
    while len(terms) > 1:
        terms = [
            terms[k] + terms[k + 1] if k + 1 < len(terms) else terms[k]
            for k in range(0, len(terms), 2)
        ]
    return terms[0]


def times(left, right):
    return {
        (i, j): sum_of([left[i, k] * right[k, j] for k in range(j, i + 1)]) for i, j in LOWER
    }


def gram_step(gram, power):
    half = {
        (i, j): sum_of([gram[min(i, k), max(i, k)] * power[k, j] for k in range(j, 4)])
        for i in range(4)
        for j in range(4)
    }
    return {(i, j): sum_of([power[k, i] * half[k, j] for k in range(i, 4)]) for i, j in UPPER}


def row_times(vector, power):
    return [sum_of([vector[i] * power[i, j] for i in range(j, 4)]) for j in range(4)]


def row_power(vector, powers, number, bits):
    for k in range(bits):
        on = ((number >> k) & 1) == 1
        moved = row_times(vector, powers[k])
        vector = [jnp.where(on, moved[j], vector[j]) for j in range(4)]
    return vector


def column_power(vector, powers, number, bits):
    for k in range(bits):
        on = ((number >> k) & 1) == 1
        moved = [sum_of([powers[k][i, j] * vector[j] for j in range(i + 1)]) for i in range(4)]
        vector = [jnp.where(on, moved[i], vector[i]) for i in range(4)]
    return vector


def response_kernel(
    place_ref, aro_ref, mao_ref, arr_ref, mar_ref, toep_ref, gam_ref, fin_ref, reach_ref, pow_ref, gram_ref
):
    poles = active_roots(arr_ref, aro_ref)
    zeros = active_roots(mar_ref, mao_ref)
    kappa = [poles[j] - zeros[j] for j in range(4)]
    one = jnp.ones((8, 128), jnp.float32)
    powers = [{(i, j): poles[i] if i == j else kappa[j] for i, j in LOWER}]
    for _ in range(LEVELS - 1):
        powers.append(times(powers[-1], powers[-1]))
    gram = {(i, j): kappa[i] * kappa[j] for i, j in UPPER}
    for k in range(LEVELS - 1):
        for at, (i, j) in enumerate(LOWER):
            pow_ref[k, at] = powers[k][i, j]
        for at, (i, j) in enumerate(UPPER):
            gram_ref[k, at] = gram[i, j]
        if k < LEVELS - 2:
            add = gram_step(gram, powers[k])
            gram = {at: gram[at] + add[at] for at in UPPER}
    lane = lax.broadcasted_iota(jnp.int32, (8, 128), 1)
    gam = row_power(kappa, powers, lane, RADIX)
    fin = column_power([one] * 4, powers, 127 - lane, RADIX)
    for i in range(4):
        gam_ref[i] = gam[i]
        fin_ref[i] = fin[i]
    eta = jnp.where(lane == 0, 1.0, pltpu.roll(sum_of(gam), 1, 1))
    big_row = lax.broadcasted_iota(jnp.int32, (128, 128), 0)
    big_lane = lax.broadcasted_iota(jnp.int32, (128, 128), 1)
    for c in range(3):
        base = jnp.broadcast_to(eta[c : c + 1, :], (128, 128))
        turned = pltpu.roll(base, 0, 1, stride=1, stride_axis=0)
        toep_ref[c] = jnp.where(big_lane >= big_row, turned, 0.0)
    place = place_ref[0, 0]
    row = lax.broadcasted_iota(jnp.int32, (8, 128), 0)
    front = row < 4
    for side in range(2):
        wide = lane + 128 * side
        peer, kind = wide & 31, wide >> 5
        gap = jnp.where(front, place - 1 - peer, peer - 1 - place)
        steps = jnp.maximum(gap, 0)
        for c in range(3):
            vector = [jnp.where((row & 3) == j, 1.0, 0.0) for j in range(4)]
            for k in range(5):
                cut = {at: powers[RADIX + k][at][c : c + 1, :] for at in LOWER}
                on = ((steps >> k) & 1) == 1
                moved = []
                for j in range(4):
                    terms = [vector[j] * cut[j, j]]
                    for i in range(4):
                        if i > j:
                            terms.append(vector[i] * jnp.where(front, cut[i, j], 0.0))
                        if i < j:
                            terms.append(vector[i] * jnp.where(front, 0.0, cut[j, i]))
                    moved.append(sum_of(terms))
                vector = [jnp.where(on, moved[j], vector[j]) for j in range(4)]
            picked = jnp.zeros((8, 128), jnp.float32)
            for j in range(4):
                picked = jnp.where((kind & 3) == j, vector[j], picked)
            used = ((kind < 4) == front) & (gap >= 0)
            reach_ref[c, :, 128 * side : 128 * side + 128] = jnp.where(used, picked, 0.0)


def segment_kernel(
    place_ref, got_ref, toep_ref, gam_ref, fin_ref, reach_ref, pow_ref, gram_ref, own_ref, near_ref, far_ref
):
    place = place_ref[0, 0]
    row = lax.broadcasted_iota(jnp.int32, (8, 128), 0)
    groups = []
    for g in range(4):
        group = jnp.zeros((8, 128), jnp.float32)
        for s in range(8):
            group = jnp.where(row == s, got_ref[8 * g + s, 32:40, :].astype(jnp.float32), group)
        groups.append(group)
    ids = jnp.concatenate(groups, axis=0)
    peer = lax.broadcasted_iota(jnp.int32, (32, 128), 0)
    mine = jnp.sum(jnp.where(peer == place, ids, 0.0), axis=0, keepdims=True)
    before = jnp.sum(jnp.where(peer == place - 1, ids, 0.0), axis=0, keepdims=True)
    ends = jnp.broadcast_to(ids[:, 127:128], (32, 128))
    last = jnp.broadcast_to(mine[:, 127:128], (1, 128))
    prev = jnp.where(place > 0, jnp.broadcast_to(before[:, 127:128], (1, 128)), -1.0)
    count = jnp.sum(
        jnp.where((peer > place) & (ids == last), 1.0, 0.0), axis=0, keepdims=True
    )
    left = jnp.sum(count, axis=1, keepdims=True).astype(jnp.int32)
    left = jnp.broadcast_to(left, (8, 128))
    ends_before = pltpu.roll(ends, 1, 0)
    keep_past = jnp.where((peer < place) & (ends == prev), 1.0, 0.0)
    keep_next = jnp.where((peer > place) & (ends_before == last), 1.0, 0.0)
    keep = jnp.concatenate([keep_past] * 4 + [keep_next] * 4, axis=0)
    gram = {at: jnp.zeros((8, 128), jnp.float32) for at in UPPER}
    for k in range(LEVELS - 1):
        power = {pair: pow_ref[k, at] for at, pair in enumerate(LOWER)}
        add = gram_step(gram, power)
        on = ((left >> k) & 1) == 1
        gram = {
            pair: jnp.where(on, gram_ref[k, at] + add[pair], gram[pair])
            for at, pair in enumerate(UPPER)
        }
    lead = jnp.where(mine == prev, 1.0, 0.0)
    trail = jnp.where(mine == last, 1.0, 0.0)
    cont = jnp.where(last == prev, 1.0, 0.0)
    fin = [fin_ref[i] * trail for i in range(4)]
    gam = [gam_ref[i] * lead for i in range(4)]
    fold = [
        sum_of([fin[j] * gram[min(i, j), max(i, j)] for j in range(4)]) for i in range(4)
    ]
    block = {pair: pow_ref[RADIX, at] for at, pair in enumerate(LOWER)}
    past = [cont * value for value in row_times(fold, block)]
    big_row = lax.broadcasted_iota(jnp.int32, (128, 128), 0)
    big_lane = lax.broadcasted_iota(jnp.int32, (128, 128), 1)
    wide = jnp.broadcast_to(mine, (128, 128))
    tall = jnp.sum(jnp.where(big_row == big_lane, wide, 0.0), axis=1, keepdims=True)
    same = wide == jnp.broadcast_to(tall, (128, 128))

    def rows(values, c, start):
        out = jnp.zeros((8, 128), jnp.float32)
        for i in range(4):
            out = jnp.where(row == start + i, values[i][c : c + 1, :], out)
        return out

    for c in range(3):
        toep = jnp.where(same, toep_ref[c], 0.0)
        probe = dot(rows(gam, c, 0), toep, ((1,), (1,)))
        out_p = jnp.where(row < 4, probe, 0.0) + rows(past, c, 0)
        fin_low = rows(fin, c, 0)
        near_ref[c] = dot(toep, toep, ((1,), (1,))) + dot(rows(fold, c, 0), fin_low, ((0,), (0,)))
        own_ref[c] = fin_low + pltpu.roll(out_p, 4, 0)
        far_ref[c] = keep * dot(reach_ref[c], out_p + rows(fin, c, 4), ((0,), (0,)))


def state_kernel(parts_ref, gaps_ref, own_ref, message_ref, masked_ref):
    total = parts_ref[0].astype(jnp.float32)
    for o in range(1, parts_ref.shape[0]):
        total = total + parts_ref[o].astype(jnp.float32)
    gaps = gaps_ref[...].astype(jnp.float32)
    rows = []
    for c in range(3):
        masked = total[:, 128 * c : 128 * c + 128] * gaps
        masked_ref[16 * c : 16 * c + 16, :] = masked
        padded = jnp.concatenate([masked, jnp.zeros((112, 128), jnp.float32)], axis=0)
        spread = pltpu.roll(
            dot(own_ref[c], padded, ((1,), (1,))), 0, 1, stride=16, stride_axis=0
        )
        rows.append(jnp.sum(spread, axis=0, keepdims=True))
    message_ref[...] = jnp.broadcast_to(jnp.concatenate(rows, axis=0)[None], message_ref.shape)


def weighted_rows(masked_ref, near_ref, far_ref, gaps_ref, states_ref):
    gaps = gaps_ref[...].astype(jnp.float32)
    pieces = []
    for c in range(3):
        here = dot(masked_ref[16 * c : 16 * c + 16, :], near_ref[c], ((1,), (0,)))
        states = states_ref[:, c, :]
        turned = [states] + [pltpu.roll(states, 128 - 16 * i, 1) for i in range(1, 8)]
        there = dot(jnp.concatenate(turned, axis=0), far_ref[c], ((0,), (0,)))[0:16, :]
        pieces.append((here + there) * gaps)
    return pieces


def tables_kernel(
    place_ref, aro_ref, mao_ref, arr_ref, mar_ref, got_ref, own_ref, near_ref, far_ref, *tables
):
    response_kernel(place_ref, aro_ref, mao_ref, arr_ref, mar_ref, *tables)
    segment_kernel(place_ref, got_ref, *tables, own_ref, near_ref, far_ref)


def pack_kernel(direction_ref, ids_ref, out_ref):
    packed = direction_ref[:, 0, :].astype(jnp.bfloat16)
    ids = jnp.broadcast_to(ids_ref[...].astype(jnp.float32), (8, 128)).astype(jnp.bfloat16)
    sheet = jnp.concatenate([packed[:, :128], packed[:, 128:], ids], axis=0)
    out_ref[...] = jnp.broadcast_to(sheet[None], out_ref.shape)


def chunk_copies(design_ref, held_ref, sems):
    width = held_ref.shape[3]
    return [
        pltpu.make_async_copy(
            design_ref.at[:, :, pl.ds(width * k, width)], held_ref.at[k], sems.at[k]
        )
        for k in range(held_ref.shape[0])
    ]


def observe_kernel(got_ref, design_ref, out_ref, held_ref, sems):
    copies = chunk_copies(design_ref, held_ref, sems)
    for copy in copies:
        copy.start()
    count, _, _, width = held_ref.shape
    peers = width // 256
    total = jnp.zeros((16, 384), jnp.float32)
    for k in range(count):
        pieces = []
        for p in range(peers * k, peers * k + peers):
            pieces += [got_ref[p, 0:16, :], got_ref[p, 16:32, :]]
        packed = jnp.concatenate(pieces, axis=1)
        copies[k].wait()
        total = total + lax.dot_general(
            packed,
            held_ref[k].reshape(384, width),
            (((1,), (1,)), ((), ())),
            preferred_element_type=jnp.float32,
        )
    out_ref[...] = jnp.broadcast_to(total.astype(jnp.bfloat16)[None], out_ref.shape)


def gradient_kernel(
    masked_ref, near_ref, far_ref, gaps_ref, states_ref, design_ref, out_ref, held_ref, sems
):
    copies = chunk_copies(design_ref, held_ref, sems)
    for copy in copies:
        copy.start()
    pieces = weighted_rows(masked_ref, near_ref, far_ref, gaps_ref, states_ref)
    weighted = jnp.concatenate(pieces, axis=1).astype(jnp.bfloat16)
    count, _, _, width = held_ref.shape
    peers = width // 256
    for k in range(count):
        copies[k].wait()
        part = jnp.dot(
            weighted, held_ref[k].reshape(384, width), preferred_element_type=jnp.float32
        ).astype(jnp.bfloat16)
        for p in range(peers):
            out_ref[peers * k + p] = part[:, 256 * p : 256 * p + 256]


def image_kernel(
    arrived_ref, kaula_ref, precond_ref, residual_ref, direction_ref, message_ref, image_ref, applied_ref, both_ref
):
    total = arrived_ref[0].astype(jnp.float32)
    for p in range(1, arrived_ref.shape[0]):
        total = total + arrived_ref[p].astype(jnp.float32)
    direction = direction_ref[:, 0, :]
    residual = residual_ref[:, 0, :]
    image = total + kaula_ref[...] * direction
    stack = jnp.concatenate([residual, image], axis=0)
    mixed = jnp.concatenate(
        [dot(stack[:, 128 * k : 128 * k + 128], precond_ref[0, k], ((1,), (1,))) for k in range(2)],
        axis=1,
    )
    applied, image_applied = mixed[0:16], mixed[16:32]
    products = jnp.concatenate(
        [
            residual * applied,
            direction * image,
            image * applied,
            image * image_applied,
            jnp.zeros((64, 256), jnp.float32),
        ],
        axis=0,
    )
    sums = dot(jnp.ones((8, 256), jnp.float32), products, ((1,), (1,)))
    message_ref[...] = jnp.broadcast_to(sums[None, 0:1, :], message_ref.shape)
    image_ref[...] = image
    applied_ref[...] = applied
    both_ref[...] = image_applied


def update_kernel(
    sums_ref, image_ref, applied_ref, both_ref, solution_ref, residual_ref, direction_ref, sol_ref, res_ref, dir_ref
):
    total = jnp.sum(sums_ref[...], axis=0)
    row = lax.broadcasted_iota(jnp.int32, (16, 128), 0)
    lane = lax.broadcasted_iota(jnp.int32, (16, 128), 1)
    wide = jnp.broadcast_to(total, (16, 128))
    old_rz, curvature, cross, square = [
        jnp.sum(jnp.where(lane == row + 16 * k, wide, 0.0), axis=1, keepdims=True)
        for k in range(4)
    ]
    step = old_rz / curvature
    new_rz = old_rz - 2.0 * step * cross + step * step * square
    direction = direction_ref[:, 0, :]
    fresh = applied_ref[...] - step * both_ref[...] + (new_rz / old_rz) * direction
    sol_ref[:, 0, :] = solution_ref[:, 0, :] + step * direction
    res_ref[:, 0, :] = residual_ref[:, 0, :] - step * image_ref[...]
    dir_ref[:, 0, :] = fresh


def run(kernel, outs, args, scalars=(), anywhere=(), scratch=(), flops=100000, limit=SMALL_LIMIT):
    spaces = [
        pltpu.SMEM if i in scalars else pltpu.HBM if i in anywhere else pltpu.VMEM
        for i in range(len(args))
    ]
    shapes = [jax.ShapeDtypeStruct(*out) for out in outs]
    found = pl.pallas_call(
        kernel,
        out_shape=shapes,
        in_specs=[pl.BlockSpec(memory_space=space) for space in spaces],
        out_specs=[pl.BlockSpec(memory_space=pltpu.VMEM) for _ in shapes],
        scratch_shapes=list(scratch),
        cost_estimate=pl.CostEstimate(flops=flops, bytes_accessed=1000000, transcendentals=0),
        compiler_params=pltpu.CompilerParams(vmem_limit_bytes=limit),
    )(*args)
    return found


def exchange(value, axes):
    return lax.all_to_all(value, axes, split_axis=0, concat_axis=0, tiled=True)


def on_device(
    design,
    gap_flags,
    segment_ids,
    ar_order,
    ma_order,
    ar_roots,
    ma_roots,
    kaula,
    precond,
    solution,
    residual,
    direction,
):
    f32, bf16 = jnp.float32, jnp.bfloat16
    count = lax.axis_size(TM)
    others = lax.axis_size(ORDER)
    everyone = count * others
    place = lax.axis_index(TM).astype(jnp.int32).reshape(1, 1)
    gaps = gap_flags.reshape(1, 128)
    (sheets,) = run(
        pack_kernel,
        [((count, 40, 128), bf16)],
        [direction, segment_ids.reshape(1, 128)],
        limit=VMEM_LIMIT,
    )
    got = exchange(sheets, TM)

    def held(chunks):
        return [
            pltpu.VMEM((chunks, 3, 128, design.shape[2] // chunks), bf16),
            pltpu.SemaphoreType.DMA((chunks,)),
        ]

    (partial,) = run(
        observe_kernel,
        [((others, 16, 384), bf16)],
        [got, design],
        anywhere=(1,),
        scratch=held(16),
        limit=VMEM_LIMIT,
    )
    parts = exchange(partial, ORDER)
    own, near, far = run(
        tables_kernel,
        [((3, 8, 128), f32), ((3, 128, 128), f32), ((3, 256, 128), f32)],
        [place, ar_order, ma_order, ar_roots, ma_roots, got],
        scalars=(0, 1, 2, 3, 4),
        scratch=[
            pltpu.VMEM((3, 128, 128), f32),
            pltpu.VMEM((4, 8, 128), f32),
            pltpu.VMEM((4, 8, 128), f32),
            pltpu.VMEM((3, 8, 256), f32),
            pltpu.VMEM((LEVELS - 1, 10, 8, 128), f32),
            pltpu.VMEM((LEVELS - 1, 10, 8, 128), f32),
        ],
        flops=10000000,
    )
    message, masked = run(
        state_kernel, [((count, 3, 128), f32), ((48, 128), f32)], [parts, gaps, own]
    )
    states = exchange(message, TM)
    (gradient,) = run(
        gradient_kernel,
        [((count, 16, 256), bf16)],
        [masked, near, far, gaps, states, design],
        anywhere=(5,),
        scratch=held(8),
        limit=VMEM_LIMIT,
    )
    arrived = exchange(gradient, TM)
    sums, image, applied, image_applied = run(
        image_kernel,
        [((everyone, 1, 128), f32)] + [((16, 256), f32)] * 3,
        [arrived, kaula, precond, residual, direction],
    )
    gathered = exchange(sums, TM_ORDER)
    return tuple(
        run(
            update_kernel,
            [((16, 1, 256), f32)] * 3,
            [gathered, image, applied, image_applied, solution, residual, direction],
        )
    )


def solution(mesh):
    split = Mesh(mesh.devices.reshape(4, 8, 4, 2), TM_ORDER)
    in_specs = (
        P(None, TM, ORDER),
        P(TM),
        P(TM),
        P(),
        P(),
        P(),
        P(),
        P(ORDER, TM),
        P(ORDER, TM, None, None),
        P(None, ORDER, TM),
        P(None, ORDER, TM),
        P(None, ORDER, TM),
    )
    out_specs = (P(None, ORDER, TM),) * 3
    return jax.shard_map(
        on_device, mesh=split, in_specs=in_specs, out_specs=out_specs, check_vma=False
    )
```

```python
import jax
import jax.numpy as jnp
from jax import lax
from jax.experimental import pallas as pl
from jax.experimental.pallas import tpu as pltpu
from jax.sharding import Mesh
from jax.sharding import PartitionSpec as P

TM = ("tm_0", "tm_1")
ORDER = ("order_0", "order_1")
TM_ORDER = TM + ORDER
VMEM_LIMIT = 50 * 1024 * 1024
SMALL_LIMIT = 8 * 1024 * 1024

precise = lax.Precision.HIGHEST
LEVELS = 12
RADIX = 7


def dot(a, b, dims):
    return lax.dot_general(
        a, b, (dims, ((), ())), precision=precise, preferred_element_type=jnp.float32
    )


def splat_rows(read):
    row = lax.broadcasted_iota(jnp.int32, (8, 128), 0)
    out = jnp.zeros((8, 128), jnp.float32)
    for c in range(3):
        out = jnp.where(row == c, read(c), out)
    return out


LOWER = [(i, j) for i in range(4) for j in range(i + 1)]
UPPER = [(i, j) for i in range(4) for j in range(i, 4)]


def active_roots(roots_ref, order_ref):
    return [
        splat_rows(lambda c: jnp.where(k < order_ref[c], roots_ref[c, k], jnp.float32(0.0)))
        for k in range(4)
    ]


def sum_of(terms):
    while len(terms) > 1:
        terms = [
            terms[k] + terms[k + 1] if k + 1 < len(terms) else terms[k]
            for k in range(0, len(terms), 2)
        ]
    return terms[0]


def times(left, right):
    return {
        (i, j): sum_of([left[i, k] * right[k, j] for k in range(j, i + 1)]) for i, j in LOWER
    }


def gram_step(gram, power):
    half = {
        (i, j): sum_of([gram[min(i, k), max(i, k)] * power[k, j] for k in range(j, 4)])
        for i in range(4)
        for j in range(4)
    }
    return {(i, j): sum_of([power[k, i] * half[k, j] for k in range(i, 4)]) for i, j in UPPER}


def row_times(vector, power):
    return [sum_of([vector[i] * power[i, j] for i in range(j, 4)]) for j in range(4)]


def row_power(vector, powers, number, bits):
    for k in range(bits):
        on = ((number >> k) & 1) == 1
        moved = row_times(vector, powers[k])
        vector = [jnp.where(on, moved[j], vector[j]) for j in range(4)]
    return vector


def column_power(vector, powers, number, bits):
    for k in range(bits):
        on = ((number >> k) & 1) == 1
        moved = [sum_of([powers[k][i, j] * vector[j] for j in range(i + 1)]) for i in range(4)]
        vector = [jnp.where(on, moved[i], vector[i]) for i in range(4)]
    return vector


def response_kernel(
    place_ref, aro_ref, mao_ref, arr_ref, mar_ref, toep_ref, gam_ref, fin_ref, reach_ref, pow_ref, gram_ref
):
    poles = active_roots(arr_ref, aro_ref)
    zeros = active_roots(mar_ref, mao_ref)
    kappa = [poles[j] - zeros[j] for j in range(4)]
    one = jnp.ones((8, 128), jnp.float32)
    powers = [{(i, j): poles[i] if i == j else kappa[j] for i, j in LOWER}]
    for _ in range(LEVELS - 1):
        powers.append(times(powers[-1], powers[-1]))
    gram = {(i, j): kappa[i] * kappa[j] for i, j in UPPER}
    for k in range(LEVELS - 1):
        for at, (i, j) in enumerate(LOWER):
            pow_ref[k, at] = powers[k][i, j]
        for at, (i, j) in enumerate(UPPER):
            gram_ref[k, at] = gram[i, j]
        if k < LEVELS - 2:
            add = gram_step(gram, powers[k])
            gram = {at: gram[at] + add[at] for at in UPPER}
    lane = lax.broadcasted_iota(jnp.int32, (8, 128), 1)
    gam = row_power(kappa, powers, lane, RADIX)
    fin = column_power([one] * 4, powers, 127 - lane, RADIX)
    for i in range(4):
        gam_ref[i] = gam[i]
        fin_ref[i] = fin[i]
    eta = jnp.where(lane == 0, 1.0, pltpu.roll(sum_of(gam), 1, 1))
    big_row = lax.broadcasted_iota(jnp.int32, (128, 128), 0)
    big_lane = lax.broadcasted_iota(jnp.int32, (128, 128), 1)
    for c in range(3):
        base = jnp.broadcast_to(eta[c : c + 1, :], (128, 128))
        turned = pltpu.roll(base, 0, 1, stride=1, stride_axis=0)
        toep_ref[c] = jnp.where(big_lane >= big_row, turned, 0.0)
    place = place_ref[0, 0]
    row = lax.broadcasted_iota(jnp.int32, (8, 128), 0)
    front = row < 4
    for side in range(2):
        wide = lane + 128 * side
        peer, kind = wide & 31, wide >> 5
        gap = jnp.where(front, place - 1 - peer, peer - 1 - place)
        steps = jnp.maximum(gap, 0)
        for c in range(3):
            vector = [jnp.where((row & 3) == j, 1.0, 0.0) for j in range(4)]
            for k in range(5):
                cut = {at: powers[RADIX + k][at][c : c + 1, :] for at in LOWER}
                on = ((steps >> k) & 1) == 1
                moved = []
                for j in range(4):
                    terms = [vector[j] * cut[j, j]]
                    for i in range(4):
                        if i > j:
                            terms.append(vector[i] * jnp.where(front, cut[i, j], 0.0))
                        if i < j:
                            terms.append(vector[i] * jnp.where(front, 0.0, cut[j, i]))
                    moved.append(sum_of(terms))
                vector = [jnp.where(on, moved[j], vector[j]) for j in range(4)]
            picked = jnp.zeros((8, 128), jnp.float32)
            for j in range(4):
                picked = jnp.where((kind & 3) == j, vector[j], picked)
            used = ((kind < 4) == front) & (gap >= 0)
            reach_ref[c, :, 128 * side : 128 * side + 128] = jnp.where(used, picked, 0.0)


def segment_kernel(
    place_ref, got_ref, toep_ref, gam_ref, fin_ref, reach_ref, pow_ref, gram_ref, own_ref, near_ref, link_ref, edge_ref
):
    place = place_ref[0, 0]
    row = lax.broadcasted_iota(jnp.int32, (8, 128), 0)
    groups = []
    for g in range(4):
        group = jnp.zeros((8, 128), jnp.float32)
        for s in range(8):
            group = jnp.where(row == s, got_ref[8 * g + s, 32:40, :].astype(jnp.float32), group)
        groups.append(group)
    ids = jnp.concatenate(groups, axis=0)
    peer = lax.broadcasted_iota(jnp.int32, (32, 128), 0)
    mine = jnp.sum(jnp.where(peer == place, ids, 0.0), axis=0, keepdims=True)
    before = jnp.sum(jnp.where(peer == place - 1, ids, 0.0), axis=0, keepdims=True)
    ends = jnp.broadcast_to(ids[:, 127:128], (32, 128))
    last = jnp.broadcast_to(mine[:, 127:128], (1, 128))
    prev = jnp.where(place > 0, jnp.broadcast_to(before[:, 127:128], (1, 128)), -1.0)
    count = jnp.sum(
        jnp.where((peer > place) & (ids == last), 1.0, 0.0), axis=0, keepdims=True
    )
    left = jnp.sum(count, axis=1, keepdims=True).astype(jnp.int32)
    left = jnp.broadcast_to(left, (8, 128))
    ends_before = pltpu.roll(ends, 1, 0)
    keep_past = jnp.where((peer < place) & (ends == prev), 1.0, 0.0)
    keep_next = jnp.where((peer > place) & (ends_before == last), 1.0, 0.0)
    wide_past = jnp.concatenate([keep_past, jnp.zeros((96, 128), jnp.float32)], axis=0).T[0:1, :]
    wide_next = jnp.concatenate([keep_next, jnp.zeros((96, 128), jnp.float32)], axis=0).T[0:1, :]
    keeps = []
    for wide_keep in (wide_past, wide_next):
        part = wide_keep
        for turn in (32, 64, 96):
            part = part + pltpu.roll(wide_keep, turn, 1)
        keeps.append(part)
    keep = jnp.concatenate(keeps, axis=1)
    gram = {at: jnp.zeros((8, 128), jnp.float32) for at in UPPER}
    for k in range(LEVELS - 1):
        power = {pair: pow_ref[k, at] for at, pair in enumerate(LOWER)}
        add = gram_step(gram, power)
        on = ((left >> k) & 1) == 1
        gram = {
            pair: jnp.where(on, gram_ref[k, at] + add[pair], gram[pair])
            for at, pair in enumerate(UPPER)
        }
    lead = jnp.where(mine == prev, 1.0, 0.0)
    trail = jnp.where(mine == last, 1.0, 0.0)
    cont = jnp.where(last == prev, 1.0, 0.0)
    fin = [fin_ref[i] * trail for i in range(4)]
    gam = [gam_ref[i] * lead for i in range(4)]
    fold = [
        sum_of([fin[j] * gram[min(i, j), max(i, j)] for j in range(4)]) for i in range(4)
    ]
    block = {pair: pow_ref[RADIX, at] for at, pair in enumerate(LOWER)}
    past = [cont * value for value in row_times(fold, block)]
    big_row = lax.broadcasted_iota(jnp.int32, (128, 128), 0)
    big_lane = lax.broadcasted_iota(jnp.int32, (128, 128), 1)
    wide = jnp.broadcast_to(mine, (128, 128))
    tall = jnp.sum(jnp.where(big_row == big_lane, wide, 0.0), axis=1, keepdims=True)
    same = wide == jnp.broadcast_to(tall, (128, 128))

    def rows(values, c, start):
        out = jnp.zeros((8, 128), jnp.float32)
        for i in range(4):
            out = jnp.where(row == start + i, values[i][c : c + 1, :], out)
        return out

    for c in range(3):
        toep = jnp.where(same, toep_ref[c], 0.0)
        probe = dot(rows(gam, c, 0), toep, ((1,), (1,)))
        out_p = jnp.where(row < 4, probe, 0.0) + rows(past, c, 0)
        fin_low = rows(fin, c, 0)
        near_ref[c] = dot(toep, toep, ((1,), (1,))) + dot(rows(fold, c, 0), fin_low, ((0,), (0,)))
        own_ref[c] = fin_low + pltpu.roll(out_p, 4, 0)
        edge_ref[c] = out_p + rows(fin, c, 4)
        link_ref[c] = reach_ref[c] * keep


def state_kernel(parts_ref, gaps_ref, own_ref, message_ref, masked_ref):
    total = parts_ref[0].astype(jnp.float32)
    for o in range(1, parts_ref.shape[0]):
        total = total + parts_ref[o].astype(jnp.float32)
    gaps = gaps_ref[...].astype(jnp.float32)
    rows = []
    for c in range(3):
        masked = total[:, 128 * c : 128 * c + 128] * gaps
        masked_ref[16 * c : 16 * c + 16, :] = masked
        padded = jnp.concatenate([masked, jnp.zeros((112, 128), jnp.float32)], axis=0)
        spread = pltpu.roll(
            dot(own_ref[c], padded, ((1,), (1,))), 0, 1, stride=16, stride_axis=0
        )
        rows.append(jnp.sum(spread, axis=0, keepdims=True))
    message_ref[...] = jnp.broadcast_to(jnp.concatenate(rows, axis=0)[None], message_ref.shape)


def split_in_two(value):
    high = value.astype(jnp.bfloat16)
    return high, (value - high.astype(jnp.float32)).astype(jnp.bfloat16)


def spread_kernel(
    masked_ref, near_ref, edge_ref, gaps_ref, design_ref, here_ref, basis_ref, held_ref, sems
):
    copies = chunk_copies(design_ref, held_ref, sems)
    for copy in copies:
        copy.start()
    gaps = gaps_ref[...].astype(jnp.float32)
    pieces = []
    highs, lows = [], []
    blank = jnp.zeros((8, 128), jnp.bfloat16)
    for c in range(3):
        pieces.append(dot(masked_ref[16 * c : 16 * c + 16, :], near_ref[c], ((1,), (0,))) * gaps)
        high, low = split_in_two(edge_ref[c] * gaps)
        highs.append(jnp.concatenate([high if d == c else blank for d in range(3)], axis=1))
        lows.append(jnp.concatenate([low if d == c else blank for d in range(3)], axis=1))
    rows = jnp.concatenate(
        [*split_in_two(jnp.concatenate(pieces, axis=1)), *highs, *lows], axis=0
    )
    count, _, _, width = held_ref.shape
    for k in range(count):
        copies[k].wait()
        found = jnp.dot(
            rows, held_ref[k].reshape(384, width), preferred_element_type=jnp.float32
        )
        here_ref[:, width * k : width * k + width] = found[0:16] + found[16:32]
        high, low = split_in_two(found[32:56] + found[56:80])
        basis_ref[0:24, width * k : width * k + width] = high
        basis_ref[24:48, width * k : width * k + width] = low
        basis_ref[48:72, width * k : width * k + width] = high


def gradient_kernel(states_ref, link_ref, here_ref, basis_ref, out_ref):
    parts = []
    for c in range(3):
        states = states_ref[:, c, :]
        turned = [states] + [pltpu.roll(states, 128 - 16 * i, 1) for i in range(1, 8)]
        parts.append(dot(link_ref[c], jnp.concatenate(turned, axis=0), ((1,), (0,))))
    found = jnp.concatenate(parts, axis=0)
    high = found.astype(jnp.bfloat16).astype(jnp.float32)
    tall = jnp.concatenate(
        [high, high, found - high, jnp.zeros((56, 128), jnp.float32)], axis=0
    )
    left = tall.T[0:16, 0:72].astype(jnp.bfloat16)
    peers = out_ref.shape[0]
    for p in range(0, peers, 4):
        span = slice(256 * p, 256 * p + 1024)
        there = jnp.dot(left, basis_ref[:, span], preferred_element_type=jnp.float32)
        whole = (here_ref[:, span] + there).astype(out_ref.dtype)
        for q in range(4):
            out_ref[p + q] = whole[:, 256 * q : 256 * q + 256]


def tables_kernel(
    place_ref, aro_ref, mao_ref, arr_ref, mar_ref, got_ref, own_ref, near_ref, link_ref, edge_ref, *tables
):
    response_kernel(place_ref, aro_ref, mao_ref, arr_ref, mar_ref, *tables)
    segment_kernel(place_ref, got_ref, *tables, own_ref, near_ref, link_ref, edge_ref)


def pack_kernel(direction_ref, ids_ref, out_ref):
    packed = direction_ref[:, 0, :].astype(jnp.bfloat16)
    ids = jnp.broadcast_to(ids_ref[...].astype(jnp.float32), (8, 128)).astype(jnp.bfloat16)
    sheet = jnp.concatenate([packed[:, :128], packed[:, 128:], ids], axis=0)
    out_ref[...] = jnp.broadcast_to(sheet[None], out_ref.shape)


def chunk_copies(design_ref, held_ref, sems):
    width = held_ref.shape[3]
    return [
        pltpu.make_async_copy(
            design_ref.at[:, :, pl.ds(width * k, width)], held_ref.at[k], sems.at[k]
        )
        for k in range(held_ref.shape[0])
    ]


def observe_kernel(got_ref, design_ref, out_ref, held_ref, sems):
    copies = chunk_copies(design_ref, held_ref, sems)
    for copy in copies:
        copy.start()
    count, _, _, width = held_ref.shape
    peers = width // 256
    total = jnp.zeros((16, 384), jnp.float32)
    for k in range(count):
        pieces = []
        for p in range(peers * k, peers * k + peers):
            pieces += [got_ref[p, 0:16, :], got_ref[p, 16:32, :]]
        packed = jnp.concatenate(pieces, axis=1)
        copies[k].wait()
        total = total + lax.dot_general(
            packed,
            held_ref[k].reshape(384, width),
            (((1,), (1,)), ((), ())),
            preferred_element_type=jnp.float32,
        )
    out_ref[...] = jnp.broadcast_to(total.astype(jnp.bfloat16)[None], out_ref.shape)


def image_kernel(
    arrived_ref, kaula_ref, precond_ref, residual_ref, direction_ref, message_ref, image_ref, applied_ref, both_ref
):
    total = arrived_ref[0].astype(jnp.float32)
    for p in range(1, arrived_ref.shape[0]):
        total = total + arrived_ref[p].astype(jnp.float32)
    direction = direction_ref[:, 0, :]
    residual = residual_ref[:, 0, :]
    image = total + kaula_ref[...] * direction
    stack = jnp.concatenate([residual, image], axis=0)
    mixed = jnp.concatenate(
        [dot(stack[:, 128 * k : 128 * k + 128], precond_ref[0, k], ((1,), (1,))) for k in range(2)],
        axis=1,
    )
    applied, image_applied = mixed[0:16], mixed[16:32]
    products = jnp.concatenate(
        [
            residual * applied,
            direction * image,
            image * applied,
            image * image_applied,
            jnp.zeros((64, 256), jnp.float32),
        ],
        axis=0,
    )
    sums = dot(jnp.ones((8, 256), jnp.float32), products, ((1,), (1,)))
    message_ref[...] = jnp.broadcast_to(sums[None, 0:1, :], message_ref.shape)
    image_ref[...] = image
    applied_ref[...] = applied
    both_ref[...] = image_applied


def update_kernel(
    sums_ref, image_ref, applied_ref, both_ref, solution_ref, residual_ref, direction_ref, sol_ref, res_ref, dir_ref
):
    total = jnp.sum(sums_ref[...], axis=0)
    row = lax.broadcasted_iota(jnp.int32, (16, 128), 0)
    lane = lax.broadcasted_iota(jnp.int32, (16, 128), 1)
    wide = jnp.broadcast_to(total, (16, 128))
    old_rz, curvature, cross, square = [
        jnp.sum(jnp.where(lane == row + 16 * k, wide, 0.0), axis=1, keepdims=True)
        for k in range(4)
    ]
    step = old_rz / curvature
    new_rz = old_rz - 2.0 * step * cross + step * step * square
    direction = direction_ref[:, 0, :]
    fresh = applied_ref[...] - step * both_ref[...] + (new_rz / old_rz) * direction
    sol_ref[:, 0, :] = solution_ref[:, 0, :] + step * direction
    res_ref[:, 0, :] = residual_ref[:, 0, :] - step * image_ref[...]
    dir_ref[:, 0, :] = fresh


def run(kernel, outs, args, scalars=(), anywhere=(), scratch=(), flops=100000, limit=SMALL_LIMIT):
    spaces = [
        pltpu.SMEM if i in scalars else pltpu.HBM if i in anywhere else pltpu.VMEM
        for i in range(len(args))
    ]
    shapes = [jax.ShapeDtypeStruct(*out) for out in outs]
    found = pl.pallas_call(
        kernel,
        out_shape=shapes,
        in_specs=[pl.BlockSpec(memory_space=space) for space in spaces],
        out_specs=[pl.BlockSpec(memory_space=pltpu.VMEM) for _ in shapes],
        scratch_shapes=list(scratch),
        cost_estimate=pl.CostEstimate(flops=flops, bytes_accessed=1000000, transcendentals=0),
        compiler_params=pltpu.CompilerParams(vmem_limit_bytes=limit),
    )(*args)
    return found


def exchange(value, axes):
    return lax.all_to_all(value, axes, split_axis=0, concat_axis=0, tiled=True)


def on_device(
    design,
    gap_flags,
    segment_ids,
    ar_order,
    ma_order,
    ar_roots,
    ma_roots,
    kaula,
    precond,
    solution,
    residual,
    direction,
):
    f32, bf16 = jnp.float32, jnp.bfloat16
    count = lax.axis_size(TM)
    others = lax.axis_size(ORDER)
    everyone = count * others
    place = lax.axis_index(TM).astype(jnp.int32).reshape(1, 1)
    gaps = gap_flags.reshape(1, 128)
    (sheets,) = run(
        pack_kernel,
        [((count, 40, 128), bf16)],
        [direction, segment_ids.reshape(1, 128)],
        limit=VMEM_LIMIT,
    )
    got = exchange(sheets, TM)

    def held(chunks):
        return [
            pltpu.VMEM((chunks, 3, 128, design.shape[2] // chunks), bf16),
            pltpu.SemaphoreType.DMA((chunks,)),
        ]

    (partial,) = run(
        observe_kernel,
        [((others, 16, 384), bf16)],
        [got, design],
        anywhere=(1,),
        scratch=held(16),
        limit=VMEM_LIMIT,
    )
    parts = exchange(partial, ORDER)
    own, near, link, edge = run(
        tables_kernel,
        [((3, 8, 128), f32), ((3, 128, 128), f32), ((3, 8, 256), f32), ((3, 8, 128), f32)],
        [place, ar_order, ma_order, ar_roots, ma_roots, got],
        scalars=(0, 1, 2, 3, 4),
        scratch=[
            pltpu.VMEM((3, 128, 128), f32),
            pltpu.VMEM((4, 8, 128), f32),
            pltpu.VMEM((4, 8, 128), f32),
            pltpu.VMEM((3, 8, 256), f32),
            pltpu.VMEM((LEVELS - 1, 10, 8, 128), f32),
            pltpu.VMEM((LEVELS - 1, 10, 8, 128), f32),
        ],
        flops=10000000,
    )
    message, masked = run(
        state_kernel, [((count, 3, 128), f32), ((48, 128), f32)], [parts, gaps, own]
    )
    states = exchange(message, TM)
    here, basis = run(
        spread_kernel,
        [((16, design.shape[2]), f32), ((72, design.shape[2]), bf16)],
        [masked, near, edge, gaps, design],
        anywhere=(4,),
        scratch=held(8),
        flops=10000000,
        limit=VMEM_LIMIT,
    )
    (gradient,) = run(
        gradient_kernel,
        [((count, 16, 256), bf16)],
        [states, link, here, basis],
        limit=16 * 1024 * 1024,
    )
    arrived = exchange(gradient, TM)
    sums, image, applied, image_applied = run(
        image_kernel,
        [((everyone, 1, 128), f32)] + [((16, 256), f32)] * 3,
        [arrived, kaula, precond, residual, direction],
    )
    gathered = exchange(sums, TM_ORDER)
    return tuple(
        run(
            update_kernel,
            [((16, 1, 256), f32)] * 3,
            [gathered, image, applied, image_applied, solution, residual, direction],
        )
    )


def solution(mesh):
    split = Mesh(mesh.devices.reshape(4, 8, 4, 2), TM_ORDER)
    in_specs = (
        P(None, TM, ORDER),
        P(TM),
        P(TM),
        P(),
        P(),
        P(),
        P(),
        P(ORDER, TM),
        P(ORDER, TM, None, None),
        P(None, ORDER, TM),
        P(None, ORDER, TM),
        P(None, ORDER, TM),
    )
    out_specs = (P(None, ORDER, TM),) * 3
    return jax.shard_map(
        on_device, mesh=split, in_specs=in_specs, out_specs=out_specs, check_vma=False
    )
```

```python
import jax
import jax.numpy as jnp
from jax import lax
from jax.experimental import pallas as pl
from jax.experimental.pallas import tpu as pltpu
from jax.sharding import Mesh
from jax.sharding import PartitionSpec as P

TM = ("tm_0", "tm_1")
ORDER = ("order_0", "order_1")
TM_ORDER = TM + ORDER
VMEM_LIMIT = 50 * 1024 * 1024
SMALL_LIMIT = 8 * 1024 * 1024

precise = lax.Precision.HIGHEST
LEVELS = 12
RADIX = 7


def dot(a, b, dims):
    return lax.dot_general(
        a, b, (dims, ((), ())), precision=precise, preferred_element_type=jnp.float32
    )


def splat_rows(read):
    row = lax.broadcasted_iota(jnp.int32, (8, 128), 0)
    out = jnp.zeros((8, 128), jnp.float32)
    for c in range(3):
        out = jnp.where(row == c, read(c), out)
    return out


LOWER = [(i, j) for i in range(4) for j in range(i + 1)]
UPPER = [(i, j) for i in range(4) for j in range(i, 4)]


def active_roots(roots_ref, order_ref):
    return [
        splat_rows(lambda c: jnp.where(k < order_ref[c], roots_ref[c, k], jnp.float32(0.0)))
        for k in range(4)
    ]


def sum_of(terms):
    while len(terms) > 1:
        terms = [
            terms[k] + terms[k + 1] if k + 1 < len(terms) else terms[k]
            for k in range(0, len(terms), 2)
        ]
    return terms[0]


def times(left, right):
    return {
        (i, j): sum_of([left[i, k] * right[k, j] for k in range(j, i + 1)]) for i, j in LOWER
    }


def gram_step(gram, power):
    half = {
        (i, j): sum_of([gram[min(i, k), max(i, k)] * power[k, j] for k in range(j, 4)])
        for i in range(4)
        for j in range(4)
    }
    return {(i, j): sum_of([power[k, i] * half[k, j] for k in range(i, 4)]) for i, j in UPPER}


def row_times(vector, power):
    return [sum_of([vector[i] * power[i, j] for i in range(j, 4)]) for j in range(4)]


def row_power(vector, powers, number, bits):
    for k in range(bits):
        on = ((number >> k) & 1) == 1
        moved = row_times(vector, powers[k])
        vector = [jnp.where(on, moved[j], vector[j]) for j in range(4)]
    return vector


def column_power(vector, powers, number, bits):
    for k in range(bits):
        on = ((number >> k) & 1) == 1
        moved = [sum_of([powers[k][i, j] * vector[j] for j in range(i + 1)]) for i in range(4)]
        vector = [jnp.where(on, moved[i], vector[i]) for i in range(4)]
    return vector


def response_kernel(
    place_ref, aro_ref, mao_ref, arr_ref, mar_ref, toep_ref, gam_ref, fin_ref, reach_ref, pow_ref, gram_ref
):
    poles = active_roots(arr_ref, aro_ref)
    zeros = active_roots(mar_ref, mao_ref)
    kappa = [poles[j] - zeros[j] for j in range(4)]
    one = jnp.ones((8, 128), jnp.float32)
    powers = [{(i, j): poles[i] if i == j else kappa[j] for i, j in LOWER}]
    for _ in range(LEVELS - 1):
        powers.append(times(powers[-1], powers[-1]))
    gram = {(i, j): kappa[i] * kappa[j] for i, j in UPPER}
    for k in range(LEVELS - 1):
        for at, (i, j) in enumerate(LOWER):
            pow_ref[k, at] = powers[k][i, j]
        for at, (i, j) in enumerate(UPPER):
            gram_ref[k, at] = gram[i, j]
        if k < LEVELS - 2:
            add = gram_step(gram, powers[k])
            gram = {at: gram[at] + add[at] for at in UPPER}
    lane = lax.broadcasted_iota(jnp.int32, (8, 128), 1)
    gam = row_power(kappa, powers, lane, RADIX)
    fin = column_power([one] * 4, powers, 127 - lane, RADIX)
    for i in range(4):
        gam_ref[i] = gam[i]
        fin_ref[i] = fin[i]
    eta = jnp.where(lane == 0, 1.0, pltpu.roll(sum_of(gam), 1, 1))
    big_row = lax.broadcasted_iota(jnp.int32, (128, 128), 0)
    big_lane = lax.broadcasted_iota(jnp.int32, (128, 128), 1)
    for c in range(3):
        base = jnp.broadcast_to(eta[c : c + 1, :], (128, 128))
        turned = pltpu.roll(base, 0, 1, stride=1, stride_axis=0)
        toep_ref[c] = jnp.where(big_lane >= big_row, turned, 0.0)
    place = place_ref[0, 0]
    row = lax.broadcasted_iota(jnp.int32, (8, 128), 0)
    front = row < 4
    for side in range(2):
        wide = lane + 128 * side
        peer, kind = wide & 31, wide >> 5
        gap = jnp.where(front, place - 1 - peer, peer - 1 - place)
        steps = jnp.maximum(gap, 0)
        for c in range(3):
            vector = [jnp.where((row & 3) == j, 1.0, 0.0) for j in range(4)]
            for k in range(5):
                cut = {at: powers[RADIX + k][at][c : c + 1, :] for at in LOWER}
                on = ((steps >> k) & 1) == 1
                moved = []
                for j in range(4):
                    terms = [vector[j] * cut[j, j]]
                    for i in range(4):
                        if i > j:
                            terms.append(vector[i] * jnp.where(front, cut[i, j], 0.0))
                        if i < j:
                            terms.append(vector[i] * jnp.where(front, 0.0, cut[j, i]))
                    moved.append(sum_of(terms))
                vector = [jnp.where(on, moved[j], vector[j]) for j in range(4)]
            picked = jnp.zeros((8, 128), jnp.float32)
            for j in range(4):
                picked = jnp.where((kind & 3) == j, vector[j], picked)
            used = ((kind < 4) == front) & (gap >= 0)
            reach_ref[c, :, 128 * side : 128 * side + 128] = jnp.where(used, picked, 0.0)


def segment_kernel(
    place_ref, got_ref, toep_ref, gam_ref, fin_ref, reach_ref, pow_ref, gram_ref, own_ref, near_ref, link_ref, edge_ref
):
    place = place_ref[0, 0]
    row = lax.broadcasted_iota(jnp.int32, (8, 128), 0)
    groups = []
    for g in range(4):
        group = jnp.zeros((8, 128), jnp.float32)
        for s in range(8):
            group = jnp.where(row == s, got_ref[8 * g + s, 32:40, :].astype(jnp.float32), group)
        groups.append(group)
    ids = jnp.concatenate(groups, axis=0)
    peer = lax.broadcasted_iota(jnp.int32, (32, 128), 0)
    mine = jnp.sum(jnp.where(peer == place, ids, 0.0), axis=0, keepdims=True)
    before = jnp.sum(jnp.where(peer == place - 1, ids, 0.0), axis=0, keepdims=True)
    ends = jnp.broadcast_to(ids[:, 127:128], (32, 128))
    last = jnp.broadcast_to(mine[:, 127:128], (1, 128))
    prev = jnp.where(place > 0, jnp.broadcast_to(before[:, 127:128], (1, 128)), -1.0)
    count = jnp.sum(
        jnp.where((peer > place) & (ids == last), 1.0, 0.0), axis=0, keepdims=True
    )
    left = jnp.sum(count, axis=1, keepdims=True).astype(jnp.int32)
    left = jnp.broadcast_to(left, (8, 128))
    ends_before = pltpu.roll(ends, 1, 0)
    keep_past = jnp.where((peer < place) & (ends == prev), 1.0, 0.0)
    keep_next = jnp.where((peer > place) & (ends_before == last), 1.0, 0.0)
    wide_past = jnp.concatenate([keep_past, jnp.zeros((96, 128), jnp.float32)], axis=0).T[0:1, :]
    wide_next = jnp.concatenate([keep_next, jnp.zeros((96, 128), jnp.float32)], axis=0).T[0:1, :]
    keeps = []
    for wide_keep in (wide_past, wide_next):
        part = wide_keep
        for turn in (32, 64, 96):
            part = part + pltpu.roll(wide_keep, turn, 1)
        keeps.append(part)
    keep = jnp.concatenate(keeps, axis=1)
    gram = {at: jnp.zeros((8, 128), jnp.float32) for at in UPPER}
    for k in range(LEVELS - 1):
        power = {pair: pow_ref[k, at] for at, pair in enumerate(LOWER)}
        add = gram_step(gram, power)
        on = ((left >> k) & 1) == 1
        gram = {
            pair: jnp.where(on, gram_ref[k, at] + add[pair], gram[pair])
            for at, pair in enumerate(UPPER)
        }
    lead = jnp.where(mine == prev, 1.0, 0.0)
    trail = jnp.where(mine == last, 1.0, 0.0)
    cont = jnp.where(last == prev, 1.0, 0.0)
    fin = [fin_ref[i] * trail for i in range(4)]
    gam = [gam_ref[i] * lead for i in range(4)]
    fold = [
        sum_of([fin[j] * gram[min(i, j), max(i, j)] for j in range(4)]) for i in range(4)
    ]
    block = {pair: pow_ref[RADIX, at] for at, pair in enumerate(LOWER)}
    past = [cont * value for value in row_times(fold, block)]
    big_row = lax.broadcasted_iota(jnp.int32, (128, 128), 0)
    big_lane = lax.broadcasted_iota(jnp.int32, (128, 128), 1)
    wide = jnp.broadcast_to(mine, (128, 128))
    tall = jnp.sum(jnp.where(big_row == big_lane, wide, 0.0), axis=1, keepdims=True)
    same = wide == jnp.broadcast_to(tall, (128, 128))

    def rows(values, c, start):
        out = jnp.zeros((8, 128), jnp.float32)
        for i in range(4):
            out = jnp.where(row == start + i, values[i][c : c + 1, :], out)
        return out

    for c in range(3):
        toep = jnp.where(same, toep_ref[c], 0.0)
        probe = dot(rows(gam, c, 0), toep, ((1,), (1,)))
        out_p = jnp.where(row < 4, probe, 0.0) + rows(past, c, 0)
        fin_low = rows(fin, c, 0)
        near_ref[c] = dot(toep, toep, ((1,), (1,))) + dot(rows(fold, c, 0), fin_low, ((0,), (0,)))
        own_ref[c] = fin_low + pltpu.roll(out_p, 4, 0)
        edge_ref[c] = out_p + rows(fin, c, 4)
        link_ref[c] = reach_ref[c] * keep


def state_kernel(parts_ref, gaps_ref, own_ref, message_ref, masked_ref):
    total = parts_ref[0].astype(jnp.float32)
    for o in range(1, parts_ref.shape[0]):
        total = total + parts_ref[o].astype(jnp.float32)
    gaps = gaps_ref[...].astype(jnp.float32)
    rows = []
    for c in range(3):
        masked = total[:, 128 * c : 128 * c + 128] * gaps
        masked_ref[16 * c : 16 * c + 16, :] = masked
        padded = jnp.concatenate([masked, jnp.zeros((112, 128), jnp.float32)], axis=0)
        spread = pltpu.roll(
            dot(own_ref[c], padded, ((1,), (1,))), 0, 1, stride=16, stride_axis=0
        )
        rows.append(jnp.sum(spread, axis=0, keepdims=True))
    message_ref[...] = jnp.broadcast_to(jnp.concatenate(rows, axis=0)[None], message_ref.shape)


def split_in_two(value):
    high = value.astype(jnp.bfloat16)
    return high, (value - high.astype(jnp.float32)).astype(jnp.bfloat16)


def spread_kernel(
    masked_ref, near_ref, edge_ref, gaps_ref, design_ref, here_ref, basis_ref, held_ref, sems
):
    copies = chunk_copies(design_ref, held_ref, sems)
    for copy in copies:
        copy.start()
    gaps = gaps_ref[...].astype(jnp.float32)
    pieces = []
    highs, lows = [], []
    blank = jnp.zeros((8, 128), jnp.bfloat16)
    for c in range(3):
        pieces.append(dot(masked_ref[16 * c : 16 * c + 16, :], near_ref[c], ((1,), (0,))) * gaps)
        high, low = split_in_two(edge_ref[c] * gaps)
        highs.append(jnp.concatenate([high if d == c else blank for d in range(3)], axis=1))
        lows.append(jnp.concatenate([low if d == c else blank for d in range(3)], axis=1))
    rows = jnp.concatenate(
        [*split_in_two(jnp.concatenate(pieces, axis=1)), *highs, *lows], axis=0
    )
    count, _, _, width = held_ref.shape
    for k in range(count):
        copies[k].wait()
        found = jnp.dot(
            rows, held_ref[k].reshape(384, width), preferred_element_type=jnp.float32
        )
        here_ref[:, width * k : width * k + width] = found[0:16] + found[16:32]
        high, low = split_in_two(found[32:56] + found[56:80])
        basis_ref[0:24, width * k : width * k + width] = high
        basis_ref[24:48, width * k : width * k + width] = low
        basis_ref[48:72, width * k : width * k + width] = high


def gradient_kernel(states_ref, link_ref, here_ref, basis_ref, out_ref):
    parts = []
    for c in range(3):
        states = states_ref[:, c, :]
        turned = [states] + [pltpu.roll(states, 128 - 16 * i, 1) for i in range(1, 8)]
        parts.append(dot(link_ref[c], jnp.concatenate(turned, axis=0), ((1,), (0,))))
    found = jnp.concatenate(parts, axis=0)
    high = found.astype(jnp.bfloat16).astype(jnp.float32)
    tall = jnp.concatenate(
        [high, high, found - high, jnp.zeros((56, 128), jnp.float32)], axis=0
    )
    left = tall.T[0:16, 0:72].astype(jnp.bfloat16)
    peers = out_ref.shape[0]
    for p in range(0, peers, 4):
        span = slice(256 * p, 256 * p + 1024)
        there = jnp.dot(left, basis_ref[:, span], preferred_element_type=jnp.float32)
        whole = (here_ref[:, span] + there).astype(out_ref.dtype)
        for q in range(4):
            out_ref[p + q] = whole[:, 256 * q : 256 * q + 256]


def tables_kernel(
    place_ref, aro_ref, mao_ref, arr_ref, mar_ref, got_ref, own_ref, near_ref, link_ref, edge_ref, *tables
):
    response_kernel(place_ref, aro_ref, mao_ref, arr_ref, mar_ref, *tables)
    segment_kernel(place_ref, got_ref, *tables, own_ref, near_ref, link_ref, edge_ref)


def pack_kernel(direction_any, ids_any, out_ref, direction_ref, ids_ref, sems):
    copies = [
        pltpu.make_async_copy(direction_any, direction_ref, sems.at[0]),
        pltpu.make_async_copy(ids_any, ids_ref, sems.at[1]),
    ]
    for copy in copies:
        copy.start()
    for copy in copies:
        copy.wait()
    packed = direction_ref[:, 0, :].astype(jnp.bfloat16)
    ids = jnp.broadcast_to(ids_ref[...].astype(jnp.float32), (8, 128)).astype(jnp.bfloat16)
    sheet = jnp.concatenate([packed[:, :128], packed[:, 128:], ids], axis=0)
    out_ref[...] = jnp.broadcast_to(sheet[None], out_ref.shape)


def chunk_copies(design_ref, held_ref, sems):
    width = held_ref.shape[3]
    return [
        pltpu.make_async_copy(
            design_ref.at[:, :, pl.ds(width * k, width)], held_ref.at[k], sems.at[k]
        )
        for k in range(held_ref.shape[0])
    ]


def observe_kernel(got_ref, design_ref, out_ref, held_ref, sems):
    copies = chunk_copies(design_ref, held_ref, sems)
    for copy in copies:
        copy.start()
    count, _, _, width = held_ref.shape
    peers = width // 256
    total = jnp.zeros((16, 384), jnp.float32)
    for k in range(count):
        pieces = []
        for p in range(peers * k, peers * k + peers):
            pieces += [got_ref[p, 0:16, :], got_ref[p, 16:32, :]]
        packed = jnp.concatenate(pieces, axis=1)
        copies[k].wait()
        total = total + lax.dot_general(
            packed,
            held_ref[k].reshape(384, width),
            (((1,), (1,)), ((), ())),
            preferred_element_type=jnp.float32,
        )
    out_ref[...] = jnp.broadcast_to(total.astype(jnp.bfloat16)[None], out_ref.shape)


def image_kernel(
    arrived_ref, kaula_ref, precond_ref, residual_ref, direction_ref, message_ref, image_ref, applied_ref, both_ref
):
    total = arrived_ref[0].astype(jnp.float32)
    for p in range(1, arrived_ref.shape[0]):
        total = total + arrived_ref[p].astype(jnp.float32)
    direction = direction_ref[:, 0, :]
    residual = residual_ref[:, 0, :]
    image = total + kaula_ref[...] * direction
    stack = jnp.concatenate([residual, image], axis=0)
    mixed = jnp.concatenate(
        [dot(stack[:, 128 * k : 128 * k + 128], precond_ref[0, k], ((1,), (1,))) for k in range(2)],
        axis=1,
    )
    applied, image_applied = mixed[0:16], mixed[16:32]
    products = jnp.concatenate(
        [
            residual * applied,
            direction * image,
            image * applied,
            image * image_applied,
            jnp.zeros((64, 256), jnp.float32),
        ],
        axis=0,
    )
    sums = dot(jnp.ones((8, 256), jnp.float32), products, ((1,), (1,)))
    message_ref[...] = jnp.broadcast_to(sums[None, 0:1, :], message_ref.shape)
    image_ref[...] = image
    applied_ref[...] = applied
    both_ref[...] = image_applied


def update_kernel(
    sums_ref, image_ref, applied_ref, both_ref, solution_ref, residual_ref, direction_ref, sol_ref, res_ref, dir_ref
):
    total = jnp.sum(sums_ref[...], axis=0)
    row = lax.broadcasted_iota(jnp.int32, (16, 128), 0)
    lane = lax.broadcasted_iota(jnp.int32, (16, 128), 1)
    wide = jnp.broadcast_to(total, (16, 128))
    old_rz, curvature, cross, square = [
        jnp.sum(jnp.where(lane == row + 16 * k, wide, 0.0), axis=1, keepdims=True)
        for k in range(4)
    ]
    step = old_rz / curvature
    new_rz = old_rz - 2.0 * step * cross + step * step * square
    direction = direction_ref[:, 0, :]
    fresh = applied_ref[...] - step * both_ref[...] + (new_rz / old_rz) * direction
    sol_ref[:, 0, :] = solution_ref[:, 0, :] + step * direction
    res_ref[:, 0, :] = residual_ref[:, 0, :] - step * image_ref[...]
    dir_ref[:, 0, :] = fresh


def run(kernel, outs, args, scalars=(), anywhere=(), scratch=(), flops=100000, limit=SMALL_LIMIT):
    spaces = [
        pltpu.SMEM if i in scalars else pltpu.HBM if i in anywhere else pltpu.VMEM
        for i in range(len(args))
    ]
    shapes = [jax.ShapeDtypeStruct(*out) for out in outs]
    found = pl.pallas_call(
        kernel,
        out_shape=shapes,
        in_specs=[pl.BlockSpec(memory_space=space) for space in spaces],
        out_specs=[pl.BlockSpec(memory_space=pltpu.VMEM) for _ in shapes],
        scratch_shapes=list(scratch),
        cost_estimate=pl.CostEstimate(flops=flops, bytes_accessed=1000000, transcendentals=0),
        compiler_params=pltpu.CompilerParams(vmem_limit_bytes=limit),
    )(*args)
    return found


def exchange(value, axes):
    return lax.all_to_all(value, axes, split_axis=0, concat_axis=0, tiled=True)


def on_device(
    design,
    gap_flags,
    segment_ids,
    ar_order,
    ma_order,
    ar_roots,
    ma_roots,
    kaula,
    precond,
    solution,
    residual,
    direction,
):
    f32, bf16 = jnp.float32, jnp.bfloat16
    count = lax.axis_size(TM)
    others = lax.axis_size(ORDER)
    everyone = count * others
    place = lax.axis_index(TM).astype(jnp.int32).reshape(1, 1)
    gaps = gap_flags.reshape(1, 128)
    (sheets,) = run(
        pack_kernel,
        [((count, 40, 128), bf16)],
        [
            pltpu.with_memory_space_constraint(direction, pltpu.HBM),
            pltpu.with_memory_space_constraint(segment_ids.reshape(1, 128), pltpu.HBM),
        ],
        anywhere=(0, 1),
        scratch=[
            pltpu.VMEM((16, 1, 256), f32),
            pltpu.VMEM((1, 128), jnp.int32),
            pltpu.SemaphoreType.DMA((2,)),
        ],
        limit=VMEM_LIMIT,
    )
    got = exchange(sheets, TM)

    def held(chunks):
        return [
            pltpu.VMEM((chunks, 3, 128, design.shape[2] // chunks), bf16),
            pltpu.SemaphoreType.DMA((chunks,)),
        ]

    (partial,) = run(
        observe_kernel,
        [((others, 16, 384), bf16)],
        [got, design],
        anywhere=(1,),
        scratch=held(16),
        limit=VMEM_LIMIT,
    )
    parts = exchange(partial, ORDER)
    own, near, link, edge = run(
        tables_kernel,
        [((3, 8, 128), f32), ((3, 128, 128), f32), ((3, 8, 256), f32), ((3, 8, 128), f32)],
        [place, ar_order, ma_order, ar_roots, ma_roots, got],
        scalars=(0, 1, 2, 3, 4),
        scratch=[
            pltpu.VMEM((3, 128, 128), f32),
            pltpu.VMEM((4, 8, 128), f32),
            pltpu.VMEM((4, 8, 128), f32),
            pltpu.VMEM((3, 8, 256), f32),
            pltpu.VMEM((LEVELS - 1, 10, 8, 128), f32),
            pltpu.VMEM((LEVELS - 1, 10, 8, 128), f32),
        ],
        flops=10000000,
    )
    message, masked = run(
        state_kernel, [((count, 3, 128), f32), ((48, 128), f32)], [parts, gaps, own]
    )
    states = exchange(message, TM)
    here, basis = run(
        spread_kernel,
        [((16, design.shape[2]), f32), ((72, design.shape[2]), bf16)],
        [masked, near, edge, gaps, design],
        anywhere=(4,),
        scratch=held(8),
        flops=10000000,
        limit=VMEM_LIMIT,
    )
    (gradient,) = run(
        gradient_kernel,
        [((count, 16, 256), bf16)],
        [states, link, here, basis],
        limit=16 * 1024 * 1024,
    )
    arrived = exchange(gradient, TM)
    sums, image, applied, image_applied = run(
        image_kernel,
        [((everyone, 1, 128), f32)] + [((16, 256), f32)] * 3,
        [arrived, kaula, precond, residual, direction],
    )
    gathered = exchange(sums, TM_ORDER)
    return tuple(
        run(
            update_kernel,
            [((16, 1, 256), f32)] * 3,
            [gathered, image, applied, image_applied, solution, residual, direction],
        )
    )


def solution(mesh):
    split = Mesh(mesh.devices.reshape(4, 8, 4, 2), TM_ORDER)
    in_specs = (
        P(None, TM, ORDER),
        P(TM),
        P(TM),
        P(),
        P(),
        P(),
        P(),
        P(ORDER, TM),
        P(ORDER, TM, None, None),
        P(None, ORDER, TM),
        P(None, ORDER, TM),
        P(None, ORDER, TM),
    )
    out_specs = (P(None, ORDER, TM),) * 3
    return jax.shard_map(
        on_device, mesh=split, in_specs=in_specs, out_specs=out_specs, check_vma=False
    )
```

```python
import jax
import jax.numpy as jnp
from jax import lax
from jax.experimental import pallas as pl
from jax.experimental.pallas import tpu as pltpu
from jax.sharding import Mesh
from jax.sharding import PartitionSpec as P

TM = ("tm_0", "tm_1")
ORDER = ("order_0", "order_1")
TM_ORDER = TM + ORDER
VMEM_LIMIT = 50 * 1024 * 1024
SMALL_LIMIT = 8 * 1024 * 1024
EARLY = 3584

precise = lax.Precision.HIGHEST
LEVELS = 12
RADIX = 7


def dot(a, b, dims):
    return lax.dot_general(
        a, b, (dims, ((), ())), precision=precise, preferred_element_type=jnp.float32
    )


def splat_rows(read):
    row = lax.broadcasted_iota(jnp.int32, (8, 128), 0)
    out = jnp.zeros((8, 128), jnp.float32)
    for c in range(3):
        out = jnp.where(row == c, read(c), out)
    return out


LOWER = [(i, j) for i in range(4) for j in range(i + 1)]
UPPER = [(i, j) for i in range(4) for j in range(i, 4)]


def active_roots(roots_ref, order_ref):
    return [
        splat_rows(lambda c: jnp.where(k < order_ref[c], roots_ref[c, k], jnp.float32(0.0)))
        for k in range(4)
    ]


def sum_of(terms):
    while len(terms) > 1:
        terms = [
            terms[k] + terms[k + 1] if k + 1 < len(terms) else terms[k]
            for k in range(0, len(terms), 2)
        ]
    return terms[0]


def times(left, right):
    return {
        (i, j): sum_of([left[i, k] * right[k, j] for k in range(j, i + 1)]) for i, j in LOWER
    }


def gram_step(gram, power):
    half = {
        (i, j): sum_of([gram[min(i, k), max(i, k)] * power[k, j] for k in range(j, 4)])
        for i in range(4)
        for j in range(4)
    }
    return {(i, j): sum_of([power[k, i] * half[k, j] for k in range(i, 4)]) for i, j in UPPER}


def row_times(vector, power):
    return [sum_of([vector[i] * power[i, j] for i in range(j, 4)]) for j in range(4)]


def row_power(vector, powers, number, bits):
    for k in range(bits):
        on = ((number >> k) & 1) == 1
        moved = row_times(vector, powers[k])
        vector = [jnp.where(on, moved[j], vector[j]) for j in range(4)]
    return vector


def column_power(vector, powers, number, bits):
    for k in range(bits):
        on = ((number >> k) & 1) == 1
        moved = [sum_of([powers[k][i, j] * vector[j] for j in range(i + 1)]) for i in range(4)]
        vector = [jnp.where(on, moved[i], vector[i]) for i in range(4)]
    return vector


def response_kernel(
    place_ref, aro_ref, mao_ref, arr_ref, mar_ref, toep_ref, gam_ref, fin_ref, reach_ref, pow_ref, gram_ref
):
    poles = active_roots(arr_ref, aro_ref)
    zeros = active_roots(mar_ref, mao_ref)
    kappa = [poles[j] - zeros[j] for j in range(4)]
    one = jnp.ones((8, 128), jnp.float32)
    powers = [{(i, j): poles[i] if i == j else kappa[j] for i, j in LOWER}]
    for _ in range(LEVELS - 1):
        powers.append(times(powers[-1], powers[-1]))
    gram = {(i, j): kappa[i] * kappa[j] for i, j in UPPER}
    for k in range(LEVELS - 1):
        for at, (i, j) in enumerate(LOWER):
            pow_ref[k, at] = powers[k][i, j]
        for at, (i, j) in enumerate(UPPER):
            gram_ref[k, at] = gram[i, j]
        if k < LEVELS - 2:
            add = gram_step(gram, powers[k])
            gram = {at: gram[at] + add[at] for at in UPPER}
    lane = lax.broadcasted_iota(jnp.int32, (8, 128), 1)
    gam = row_power(kappa, powers, lane, RADIX)
    fin = column_power([one] * 4, powers, 127 - lane, RADIX)
    for i in range(4):
        gam_ref[i] = gam[i]
        fin_ref[i] = fin[i]
    eta = jnp.where(lane == 0, 1.0, pltpu.roll(sum_of(gam), 1, 1))
    big_row = lax.broadcasted_iota(jnp.int32, (128, 128), 0)
    big_lane = lax.broadcasted_iota(jnp.int32, (128, 128), 1)
    for c in range(3):
        base = jnp.broadcast_to(eta[c : c + 1, :], (128, 128))
        turned = pltpu.roll(base, 0, 1, stride=1, stride_axis=0)
        toep_ref[c] = jnp.where(big_lane >= big_row, turned, 0.0)
    place = place_ref[0, 0]
    row = lax.broadcasted_iota(jnp.int32, (8, 128), 0)
    front = row < 4
    for side in range(2):
        wide = lane + 128 * side
        peer, kind = wide & 31, wide >> 5
        gap = jnp.where(front, place - 1 - peer, peer - 1 - place)
        steps = jnp.maximum(gap, 0)
        for c in range(3):
            vector = [jnp.where((row & 3) == j, 1.0, 0.0) for j in range(4)]
            for k in range(5):
                cut = {at: powers[RADIX + k][at][c : c + 1, :] for at in LOWER}
                on = ((steps >> k) & 1) == 1
                moved = []
                for j in range(4):
                    terms = [vector[j] * cut[j, j]]
                    for i in range(4):
                        if i > j:
                            terms.append(vector[i] * jnp.where(front, cut[i, j], 0.0))
                        if i < j:
                            terms.append(vector[i] * jnp.where(front, 0.0, cut[j, i]))
                    moved.append(sum_of(terms))
                vector = [jnp.where(on, moved[j], vector[j]) for j in range(4)]
            picked = jnp.zeros((8, 128), jnp.float32)
            for j in range(4):
                picked = jnp.where((kind & 3) == j, vector[j], picked)
            used = ((kind < 4) == front) & (gap >= 0)
            reach_ref[c, :, 128 * side : 128 * side + 128] = jnp.where(used, picked, 0.0)


def segment_kernel(
    place_ref, got_ref, toep_ref, gam_ref, fin_ref, reach_ref, pow_ref, gram_ref, own_ref, near_ref, link_ref, edge_ref
):
    place = place_ref[0, 0]
    row = lax.broadcasted_iota(jnp.int32, (8, 128), 0)
    groups = []
    for g in range(4):
        group = jnp.zeros((8, 128), jnp.float32)
        for s in range(8):
            group = jnp.where(row == s, got_ref[8 * g + s, 32:40, :].astype(jnp.float32), group)
        groups.append(group)
    ids = jnp.concatenate(groups, axis=0)
    peer = lax.broadcasted_iota(jnp.int32, (32, 128), 0)
    mine = jnp.sum(jnp.where(peer == place, ids, 0.0), axis=0, keepdims=True)
    before = jnp.sum(jnp.where(peer == place - 1, ids, 0.0), axis=0, keepdims=True)
    ends = jnp.broadcast_to(ids[:, 127:128], (32, 128))
    last = jnp.broadcast_to(mine[:, 127:128], (1, 128))
    prev = jnp.where(place > 0, jnp.broadcast_to(before[:, 127:128], (1, 128)), -1.0)
    count = jnp.sum(
        jnp.where((peer > place) & (ids == last), 1.0, 0.0), axis=0, keepdims=True
    )
    left = jnp.sum(count, axis=1, keepdims=True).astype(jnp.int32)
    left = jnp.broadcast_to(left, (8, 128))
    ends_before = pltpu.roll(ends, 1, 0)
    keep_past = jnp.where((peer < place) & (ends == prev), 1.0, 0.0)
    keep_next = jnp.where((peer > place) & (ends_before == last), 1.0, 0.0)
    wide_past = jnp.concatenate([keep_past, jnp.zeros((96, 128), jnp.float32)], axis=0).T[0:1, :]
    wide_next = jnp.concatenate([keep_next, jnp.zeros((96, 128), jnp.float32)], axis=0).T[0:1, :]
    keeps = []
    for wide_keep in (wide_past, wide_next):
        part = wide_keep
        for turn in (32, 64, 96):
            part = part + pltpu.roll(wide_keep, turn, 1)
        keeps.append(part)
    keep = jnp.concatenate(keeps, axis=1)
    gram = {at: jnp.zeros((8, 128), jnp.float32) for at in UPPER}
    for k in range(LEVELS - 1):
        power = {pair: pow_ref[k, at] for at, pair in enumerate(LOWER)}
        add = gram_step(gram, power)
        on = ((left >> k) & 1) == 1
        gram = {
            pair: jnp.where(on, gram_ref[k, at] + add[pair], gram[pair])
            for at, pair in enumerate(UPPER)
        }
    lead = jnp.where(mine == prev, 1.0, 0.0)
    trail = jnp.where(mine == last, 1.0, 0.0)
    cont = jnp.where(last == prev, 1.0, 0.0)
    fin = [fin_ref[i] * trail for i in range(4)]
    gam = [gam_ref[i] * lead for i in range(4)]
    fold = [
        sum_of([fin[j] * gram[min(i, j), max(i, j)] for j in range(4)]) for i in range(4)
    ]
    block = {pair: pow_ref[RADIX, at] for at, pair in enumerate(LOWER)}
    past = [cont * value for value in row_times(fold, block)]
    big_row = lax.broadcasted_iota(jnp.int32, (128, 128), 0)
    big_lane = lax.broadcasted_iota(jnp.int32, (128, 128), 1)
    wide = jnp.broadcast_to(mine, (128, 128))
    tall = jnp.sum(jnp.where(big_row == big_lane, wide, 0.0), axis=1, keepdims=True)
    same = wide == jnp.broadcast_to(tall, (128, 128))

    def rows(values, c, start):
        out = jnp.zeros((8, 128), jnp.float32)
        for i in range(4):
            out = jnp.where(row == start + i, values[i][c : c + 1, :], out)
        return out

    for c in range(3):
        toep = jnp.where(same, toep_ref[c], 0.0)
        probe = dot(rows(gam, c, 0), toep, ((1,), (1,)))
        out_p = jnp.where(row < 4, probe, 0.0) + rows(past, c, 0)
        fin_low = rows(fin, c, 0)
        near_ref[c] = dot(toep, toep, ((1,), (1,))) + dot(rows(fold, c, 0), fin_low, ((0,), (0,)))
        own_ref[c] = fin_low + pltpu.roll(out_p, 4, 0)
        edge_ref[c] = out_p + rows(fin, c, 4)
        link_ref[c] = reach_ref[c] * keep


def state_kernel(parts_ref, gaps_ref, own_ref, message_ref, masked_ref):
    total = parts_ref[0].astype(jnp.float32)
    for o in range(1, parts_ref.shape[0]):
        total = total + parts_ref[o].astype(jnp.float32)
    gaps = gaps_ref[...].astype(jnp.float32)
    rows = []
    for c in range(3):
        masked = total[:, 128 * c : 128 * c + 128] * gaps
        masked_ref[16 * c : 16 * c + 16, :] = masked
        padded = jnp.concatenate([masked, jnp.zeros((112, 128), jnp.float32)], axis=0)
        spread = pltpu.roll(
            dot(own_ref[c], padded, ((1,), (1,))), 0, 1, stride=16, stride_axis=0
        )
        rows.append(jnp.sum(spread, axis=0, keepdims=True))
    message_ref[...] = jnp.broadcast_to(jnp.concatenate(rows, axis=0)[None], message_ref.shape)


def split_in_two(value):
    high = value.astype(jnp.bfloat16)
    return high, (value - high.astype(jnp.float32)).astype(jnp.bfloat16)


def spread_kernel(
    masked_ref, near_ref, edge_ref, gaps_ref, design_ref, here_ref, basis_ref, held_ref, sems
):
    copies = chunk_copies(design_ref, held_ref, sems)
    for copy in copies:
        copy.start()
    gaps = gaps_ref[...].astype(jnp.float32)
    pieces = []
    highs, lows = [], []
    blank = jnp.zeros((8, 128), jnp.bfloat16)
    for c in range(3):
        pieces.append(dot(masked_ref[16 * c : 16 * c + 16, :], near_ref[c], ((1,), (0,))) * gaps)
        high, low = split_in_two(edge_ref[c] * gaps)
        highs.append(jnp.concatenate([high if d == c else blank for d in range(3)], axis=1))
        lows.append(jnp.concatenate([low if d == c else blank for d in range(3)], axis=1))
    rows = jnp.concatenate(
        [*split_in_two(jnp.concatenate(pieces, axis=1)), *highs, *lows], axis=0
    )
    count, _, _, width = held_ref.shape
    for k in range(count):
        copies[k].wait()
        found = jnp.dot(
            rows, held_ref[k].reshape(384, width), preferred_element_type=jnp.float32
        )
        here_ref[:, width * k : width * k + width] = found[0:16] + found[16:32]
        high, low = split_in_two(found[32:56] + found[56:80])
        basis_ref[0:24, width * k : width * k + width] = high
        basis_ref[24:48, width * k : width * k + width] = low
        basis_ref[48:72, width * k : width * k + width] = high


def gradient_kernel(states_ref, link_ref, here_ref, basis_ref, out_ref):
    parts = []
    for c in range(3):
        states = states_ref[:, c, :]
        turned = [states] + [pltpu.roll(states, 128 - 16 * i, 1) for i in range(1, 8)]
        parts.append(dot(link_ref[c], jnp.concatenate(turned, axis=0), ((1,), (0,))))
    found = jnp.concatenate(parts, axis=0)
    high = found.astype(jnp.bfloat16).astype(jnp.float32)
    tall = jnp.concatenate(
        [high, high, found - high, jnp.zeros((56, 128), jnp.float32)], axis=0
    )
    left = tall.T[0:16, 0:72].astype(jnp.bfloat16)
    peers = out_ref.shape[0]
    for p in range(0, peers, 4):
        span = slice(256 * p, 256 * p + 1024)
        there = jnp.dot(left, basis_ref[:, span], preferred_element_type=jnp.float32)
        whole = (here_ref[:, span] + there).astype(out_ref.dtype)
        for q in range(4):
            out_ref[p + q] = whole[:, 256 * q : 256 * q + 256]


def tables_kernel(
    place_ref, aro_ref, mao_ref, arr_ref, mar_ref, got_ref, own_ref, near_ref, link_ref, edge_ref, *tables
):
    response_kernel(place_ref, aro_ref, mao_ref, arr_ref, mar_ref, *tables)
    segment_kernel(place_ref, got_ref, *tables, own_ref, near_ref, link_ref, edge_ref)


def pack_kernel(direction_any, ids_any, out_ref, direction_ref, ids_ref, sems):
    copies = [
        pltpu.make_async_copy(direction_any, direction_ref, sems.at[0]),
        pltpu.make_async_copy(ids_any, ids_ref, sems.at[1]),
    ]
    for copy in copies:
        copy.start()
    for copy in copies:
        copy.wait()
    packed = direction_ref[:, 0, :].astype(jnp.bfloat16)
    ids = jnp.broadcast_to(ids_ref[...].astype(jnp.float32), (8, 128)).astype(jnp.bfloat16)
    sheet = jnp.concatenate([packed[:, :128], packed[:, 128:], ids], axis=0)
    out_ref[...] = jnp.broadcast_to(sheet[None], out_ref.shape)


def chunk_copies(design_ref, held_ref, sems):
    width = held_ref.shape[3]
    return [
        pltpu.make_async_copy(
            design_ref.at[:, :, pl.ds(width * k, width)], held_ref.at[k], sems.at[k]
        )
        for k in range(held_ref.shape[0])
    ]


def observe_kernel(got_ref, design_ref, early_ref, out_ref, held_ref, sems):
    count, _, _, width = held_ref.shape
    start = early_ref.shape[2]
    copies = [
        pltpu.make_async_copy(
            design_ref.at[:, :, pl.ds(start + width * k, width)], held_ref.at[k], sems.at[k]
        )
        for k in range(count)
    ]
    for copy in copies:
        copy.start()

    def product(first, block):
        pieces = []
        for p in range(first, first + block.shape[1] // 256):
            pieces += [got_ref[p, 0:16, :], got_ref[p, 16:32, :]]
        return lax.dot_general(
            jnp.concatenate(pieces, axis=1),
            block,
            (((1,), (1,)), ((), ())),
            preferred_element_type=jnp.float32,
        )

    total = jnp.zeros((16, 384), jnp.float32)
    for at in range(0, start, width):
        total = total + product(at // 256, early_ref[:, :, at : at + width].reshape(384, width))
    for k in range(count):
        copies[k].wait()
        total = total + product((start + width * k) // 256, held_ref[k].reshape(384, width))
    out_ref[...] = jnp.broadcast_to(total.astype(jnp.bfloat16)[None], out_ref.shape)


def image_kernel(
    arrived_ref, kaula_ref, precond_ref, residual_ref, direction_ref, message_ref, image_ref, applied_ref, both_ref
):
    total = arrived_ref[0].astype(jnp.float32)
    for p in range(1, arrived_ref.shape[0]):
        total = total + arrived_ref[p].astype(jnp.float32)
    direction = direction_ref[:, 0, :]
    residual = residual_ref[:, 0, :]
    image = total + kaula_ref[...] * direction
    stack = jnp.concatenate([residual, image], axis=0)
    mixed = jnp.concatenate(
        [dot(stack[:, 128 * k : 128 * k + 128], precond_ref[0, k], ((1,), (1,))) for k in range(2)],
        axis=1,
    )
    applied, image_applied = mixed[0:16], mixed[16:32]
    products = jnp.concatenate(
        [
            residual * applied,
            direction * image,
            image * applied,
            image * image_applied,
            jnp.zeros((64, 256), jnp.float32),
        ],
        axis=0,
    )
    sums = dot(jnp.ones((8, 256), jnp.float32), products, ((1,), (1,)))
    message_ref[...] = jnp.broadcast_to(sums[None, 0:1, :], message_ref.shape)
    image_ref[...] = image
    applied_ref[...] = applied
    both_ref[...] = image_applied


def update_kernel(
    sums_ref, image_ref, applied_ref, both_ref, solution_ref, residual_ref, direction_ref, sol_ref, res_ref, dir_ref
):
    total = jnp.sum(sums_ref[...], axis=0)
    row = lax.broadcasted_iota(jnp.int32, (16, 128), 0)
    lane = lax.broadcasted_iota(jnp.int32, (16, 128), 1)
    wide = jnp.broadcast_to(total, (16, 128))
    old_rz, curvature, cross, square = [
        jnp.sum(jnp.where(lane == row + 16 * k, wide, 0.0), axis=1, keepdims=True)
        for k in range(4)
    ]
    step = old_rz / curvature
    new_rz = old_rz - 2.0 * step * cross + step * step * square
    direction = direction_ref[:, 0, :]
    fresh = applied_ref[...] - step * both_ref[...] + (new_rz / old_rz) * direction
    sol_ref[:, 0, :] = solution_ref[:, 0, :] + step * direction
    res_ref[:, 0, :] = residual_ref[:, 0, :] - step * image_ref[...]
    dir_ref[:, 0, :] = fresh


def run(kernel, outs, args, scalars=(), anywhere=(), scratch=(), flops=100000, limit=SMALL_LIMIT):
    spaces = [
        pltpu.SMEM if i in scalars else pltpu.HBM if i in anywhere else pltpu.VMEM
        for i in range(len(args))
    ]
    shapes = [jax.ShapeDtypeStruct(*out) for out in outs]
    found = pl.pallas_call(
        kernel,
        out_shape=shapes,
        in_specs=[pl.BlockSpec(memory_space=space) for space in spaces],
        out_specs=[pl.BlockSpec(memory_space=pltpu.VMEM) for _ in shapes],
        scratch_shapes=list(scratch),
        cost_estimate=pl.CostEstimate(flops=flops, bytes_accessed=1000000, transcendentals=0),
        compiler_params=pltpu.CompilerParams(vmem_limit_bytes=limit),
    )(*args)
    return found


def exchange(value, axes):
    return lax.all_to_all(value, axes, split_axis=0, concat_axis=0, tiled=True)


def on_device(
    design,
    gap_flags,
    segment_ids,
    ar_order,
    ma_order,
    ar_roots,
    ma_roots,
    kaula,
    precond,
    solution,
    residual,
    direction,
):
    f32, bf16 = jnp.float32, jnp.bfloat16
    count = lax.axis_size(TM)
    others = lax.axis_size(ORDER)
    everyone = count * others
    place = lax.axis_index(TM).astype(jnp.int32).reshape(1, 1)
    gaps = gap_flags.reshape(1, 128)
    (sheets,) = run(
        pack_kernel,
        [((count, 40, 128), bf16)],
        [
            pltpu.with_memory_space_constraint(direction, pltpu.HBM),
            pltpu.with_memory_space_constraint(segment_ids.reshape(1, 128), pltpu.HBM),
        ],
        anywhere=(0, 1),
        scratch=[
            pltpu.VMEM((16, 1, 256), f32),
            pltpu.VMEM((1, 128), jnp.int32),
            pltpu.SemaphoreType.DMA((2,)),
        ],
        limit=VMEM_LIMIT,
    )
    got = exchange(sheets, TM)

    def held(chunks):
        return [
            pltpu.VMEM((chunks, 3, 128, design.shape[2] // chunks), bf16),
            pltpu.SemaphoreType.DMA((chunks,)),
        ]

    (partial,) = run(
        observe_kernel,
        [((others, 16, 384), bf16)],
        [got, design, lax.slice_in_dim(design, 0, EARLY, axis=2)],
        anywhere=(1,),
        scratch=[
            pltpu.VMEM(((design.shape[2] - EARLY) // 512, 3, 128, 512), bf16),
            pltpu.SemaphoreType.DMA(((design.shape[2] - EARLY) // 512,)),
        ],
        limit=VMEM_LIMIT,
    )
    parts = exchange(partial, ORDER)
    own, near, link, edge = run(
        tables_kernel,
        [((3, 8, 128), f32), ((3, 128, 128), f32), ((3, 8, 256), f32), ((3, 8, 128), f32)],
        [place, ar_order, ma_order, ar_roots, ma_roots, got],
        scalars=(0, 1, 2, 3, 4),
        scratch=[
            pltpu.VMEM((3, 128, 128), f32),
            pltpu.VMEM((4, 8, 128), f32),
            pltpu.VMEM((4, 8, 128), f32),
            pltpu.VMEM((3, 8, 256), f32),
            pltpu.VMEM((LEVELS - 1, 10, 8, 128), f32),
            pltpu.VMEM((LEVELS - 1, 10, 8, 128), f32),
        ],
        flops=10000000,
    )
    message, masked = run(
        state_kernel, [((count, 3, 128), f32), ((48, 128), f32)], [parts, gaps, own]
    )
    states = exchange(message, TM)
    here, basis = run(
        spread_kernel,
        [((16, design.shape[2]), f32), ((72, design.shape[2]), bf16)],
        [masked, near, edge, gaps, design],
        anywhere=(4,),
        scratch=held(8),
        flops=10000000,
        limit=VMEM_LIMIT,
    )
    (gradient,) = run(
        gradient_kernel,
        [((count, 16, 256), bf16)],
        [states, link, here, basis],
        limit=16 * 1024 * 1024,
    )
    arrived = exchange(gradient, TM)
    sums, image, applied, image_applied = run(
        image_kernel,
        [((everyone, 1, 128), f32)] + [((16, 256), f32)] * 3,
        [arrived, kaula, precond, residual, direction],
    )
    gathered = exchange(sums, TM_ORDER)
    return tuple(
        run(
            update_kernel,
            [((16, 1, 256), f32)] * 3,
            [gathered, image, applied, image_applied, solution, residual, direction],
        )
    )


def solution(mesh):
    split = Mesh(mesh.devices.reshape(4, 8, 4, 2), TM_ORDER)
    in_specs = (
        P(None, TM, ORDER),
        P(TM),
        P(TM),
        P(),
        P(),
        P(),
        P(),
        P(ORDER, TM),
        P(ORDER, TM, None, None),
        P(None, ORDER, TM),
        P(None, ORDER, TM),
        P(None, ORDER, TM),
    )
    out_specs = (P(None, ORDER, TM),) * 3
    return jax.shard_map(
        on_device, mesh=split, in_specs=in_specs, out_specs=out_specs, check_vma=False
    )
```

```python
import jax
import jax.numpy as jnp
from jax import lax
from jax.experimental import pallas as pl
from jax.experimental.pallas import tpu as pltpu
from jax.sharding import Mesh
from jax.sharding import PartitionSpec as P

TM = ("tm_0", "tm_1")
ORDER = ("order_0", "order_1")
TM_ORDER = TM + ORDER
VMEM_LIMIT = 50 * 1024 * 1024
SMALL_LIMIT = 8 * 1024 * 1024
EARLY = 3584

precise = lax.Precision.HIGHEST
LEVELS = 12
RADIX = 7


def dot(a, b, dims):
    return lax.dot_general(
        a, b, (dims, ((), ())), precision=precise, preferred_element_type=jnp.float32
    )


def splat_rows(read):
    row = lax.broadcasted_iota(jnp.int32, (8, 128), 0)
    out = jnp.zeros((8, 128), jnp.float32)
    for c in range(3):
        out = jnp.where(row == c, read(c), out)
    return out


LOWER = [(i, j) for i in range(4) for j in range(i + 1)]
UPPER = [(i, j) for i in range(4) for j in range(i, 4)]


def active_roots(roots_ref, order_ref):
    return [
        splat_rows(lambda c: jnp.where(k < order_ref[c], roots_ref[c, k], jnp.float32(0.0)))
        for k in range(4)
    ]


def sum_of(terms):
    while len(terms) > 1:
        terms = [
            terms[k] + terms[k + 1] if k + 1 < len(terms) else terms[k]
            for k in range(0, len(terms), 2)
        ]
    return terms[0]


def times(left, right):
    return {
        (i, j): sum_of([left[i, k] * right[k, j] for k in range(j, i + 1)]) for i, j in LOWER
    }


def gram_step(gram, power):
    half = {
        (i, j): sum_of([gram[min(i, k), max(i, k)] * power[k, j] for k in range(j, 4)])
        for i in range(4)
        for j in range(4)
    }
    return {(i, j): sum_of([power[k, i] * half[k, j] for k in range(i, 4)]) for i, j in UPPER}


def row_times(vector, power):
    return [sum_of([vector[i] * power[i, j] for i in range(j, 4)]) for j in range(4)]


def row_power(vector, powers, number, bits):
    for k in range(bits):
        on = ((number >> k) & 1) == 1
        moved = row_times(vector, powers[k])
        vector = [jnp.where(on, moved[j], vector[j]) for j in range(4)]
    return vector


def column_power(vector, powers, number, bits):
    for k in range(bits):
        on = ((number >> k) & 1) == 1
        moved = [sum_of([powers[k][i, j] * vector[j] for j in range(i + 1)]) for i in range(4)]
        vector = [jnp.where(on, moved[i], vector[i]) for i in range(4)]
    return vector


def response_kernel(
    place_ref, aro_ref, mao_ref, arr_ref, mar_ref, toep_ref, gam_ref, fin_ref, reach_ref, pow_ref, gram_ref
):
    poles = active_roots(arr_ref, aro_ref)
    zeros = active_roots(mar_ref, mao_ref)
    kappa = [poles[j] - zeros[j] for j in range(4)]
    one = jnp.ones((8, 128), jnp.float32)
    powers = [{(i, j): poles[i] if i == j else kappa[j] for i, j in LOWER}]
    for _ in range(LEVELS - 1):
        powers.append(times(powers[-1], powers[-1]))
    gram = {(i, j): kappa[i] * kappa[j] for i, j in UPPER}
    for k in range(LEVELS - 1):
        for at, (i, j) in enumerate(LOWER):
            pow_ref[k, at] = powers[k][i, j]
        for at, (i, j) in enumerate(UPPER):
            gram_ref[k, at] = gram[i, j]
        if k < LEVELS - 2:
            add = gram_step(gram, powers[k])
            gram = {at: gram[at] + add[at] for at in UPPER}
    lane = lax.broadcasted_iota(jnp.int32, (8, 128), 1)
    gam = row_power(kappa, powers, lane, RADIX)
    fin = column_power([one] * 4, powers, 127 - lane, RADIX)
    for i in range(4):
        gam_ref[i] = gam[i]
        fin_ref[i] = fin[i]
    eta = jnp.where(lane == 0, 1.0, pltpu.roll(sum_of(gam), 1, 1))
    big_row = lax.broadcasted_iota(jnp.int32, (128, 128), 0)
    big_lane = lax.broadcasted_iota(jnp.int32, (128, 128), 1)
    for c in range(3):
        base = jnp.broadcast_to(eta[c : c + 1, :], (128, 128))
        turned = pltpu.roll(base, 0, 1, stride=1, stride_axis=0)
        toep_ref[c] = jnp.where(big_lane >= big_row, turned, 0.0)
    place = place_ref[0, 0]
    row = lax.broadcasted_iota(jnp.int32, (8, 128), 0)
    front = row < 4
    for side in range(2):
        wide = lane + 128 * side
        peer, kind = wide & 31, wide >> 5
        gap = jnp.where(front, place - 1 - peer, peer - 1 - place)
        steps = jnp.maximum(gap, 0)
        for c in range(3):
            vector = [jnp.where((row & 3) == j, 1.0, 0.0) for j in range(4)]
            for k in range(5):
                cut = {at: powers[RADIX + k][at][c : c + 1, :] for at in LOWER}
                on = ((steps >> k) & 1) == 1
                moved = []
                for j in range(4):
                    terms = [vector[j] * cut[j, j]]
                    for i in range(4):
                        if i > j:
                            terms.append(vector[i] * jnp.where(front, cut[i, j], 0.0))
                        if i < j:
                            terms.append(vector[i] * jnp.where(front, 0.0, cut[j, i]))
                    moved.append(sum_of(terms))
                vector = [jnp.where(on, moved[j], vector[j]) for j in range(4)]
            picked = jnp.zeros((8, 128), jnp.float32)
            for j in range(4):
                picked = jnp.where((kind & 3) == j, vector[j], picked)
            used = ((kind < 4) == front) & (gap >= 0)
            reach_ref[c, :, 128 * side : 128 * side + 128] = jnp.where(used, picked, 0.0)


def segment_kernel(
    place_ref, got_ref, toep_ref, gam_ref, fin_ref, reach_ref, pow_ref, gram_ref, own_ref, near_ref, link_ref, edge_ref
):
    place = place_ref[0, 0]
    row = lax.broadcasted_iota(jnp.int32, (8, 128), 0)
    groups = []
    for g in range(4):
        group = jnp.zeros((8, 128), jnp.float32)
        for s in range(8):
            group = jnp.where(row == s, got_ref[8 * g + s, 32:40, :].astype(jnp.float32), group)
        groups.append(group)
    ids = jnp.concatenate(groups, axis=0)
    peer = lax.broadcasted_iota(jnp.int32, (32, 128), 0)
    mine = jnp.sum(jnp.where(peer == place, ids, 0.0), axis=0, keepdims=True)
    before = jnp.sum(jnp.where(peer == place - 1, ids, 0.0), axis=0, keepdims=True)
    ends = jnp.broadcast_to(ids[:, 127:128], (32, 128))
    last = jnp.broadcast_to(mine[:, 127:128], (1, 128))
    prev = jnp.where(place > 0, jnp.broadcast_to(before[:, 127:128], (1, 128)), -1.0)
    count = jnp.sum(
        jnp.where((peer > place) & (ids == last), 1.0, 0.0), axis=0, keepdims=True
    )
    left = jnp.sum(count, axis=1, keepdims=True).astype(jnp.int32)
    left = jnp.broadcast_to(left, (8, 128))
    ends_before = pltpu.roll(ends, 1, 0)
    keep_past = jnp.where((peer < place) & (ends == prev), 1.0, 0.0)
    keep_next = jnp.where((peer > place) & (ends_before == last), 1.0, 0.0)
    wide_past = jnp.concatenate([keep_past, jnp.zeros((96, 128), jnp.float32)], axis=0).T[0:1, :]
    wide_next = jnp.concatenate([keep_next, jnp.zeros((96, 128), jnp.float32)], axis=0).T[0:1, :]
    keeps = []
    for wide_keep in (wide_past, wide_next):
        part = wide_keep
        for turn in (32, 64, 96):
            part = part + pltpu.roll(wide_keep, turn, 1)
        keeps.append(part)
    keep = jnp.concatenate(keeps, axis=1)
    gram = {at: jnp.zeros((8, 128), jnp.float32) for at in UPPER}
    for k in range(LEVELS - 1):
        power = {pair: pow_ref[k, at] for at, pair in enumerate(LOWER)}
        add = gram_step(gram, power)
        on = ((left >> k) & 1) == 1
        gram = {
            pair: jnp.where(on, gram_ref[k, at] + add[pair], gram[pair])
            for at, pair in enumerate(UPPER)
        }
    lead = jnp.where(mine == prev, 1.0, 0.0)
    trail = jnp.where(mine == last, 1.0, 0.0)
    cont = jnp.where(last == prev, 1.0, 0.0)
    fin = [fin_ref[i] * trail for i in range(4)]
    gam = [gam_ref[i] * lead for i in range(4)]
    fold = [
        sum_of([fin[j] * gram[min(i, j), max(i, j)] for j in range(4)]) for i in range(4)
    ]
    block = {pair: pow_ref[RADIX, at] for at, pair in enumerate(LOWER)}
    past = [cont * value for value in row_times(fold, block)]
    big_row = lax.broadcasted_iota(jnp.int32, (128, 128), 0)
    big_lane = lax.broadcasted_iota(jnp.int32, (128, 128), 1)
    wide = jnp.broadcast_to(mine, (128, 128))
    tall = jnp.sum(jnp.where(big_row == big_lane, wide, 0.0), axis=1, keepdims=True)
    same = wide == jnp.broadcast_to(tall, (128, 128))

    def rows(values, c, start):
        out = jnp.zeros((8, 128), jnp.float32)
        for i in range(4):
            out = jnp.where(row == start + i, values[i][c : c + 1, :], out)
        return out

    for c in range(3):
        toep = jnp.where(same, toep_ref[c], 0.0)
        probe = dot(rows(gam, c, 0), toep, ((1,), (1,)))
        out_p = jnp.where(row < 4, probe, 0.0) + rows(past, c, 0)
        fin_low = rows(fin, c, 0)
        near_ref[c] = dot(toep, toep, ((1,), (1,))) + dot(rows(fold, c, 0), fin_low, ((0,), (0,)))
        own_ref[c] = fin_low + pltpu.roll(out_p, 4, 0)
        edge_ref[c] = out_p + rows(fin, c, 4)
        link_ref[c] = reach_ref[c] * keep


def state_kernel(parts_ref, gaps_ref, own_ref, message_ref, masked_ref):
    total = parts_ref[0].astype(jnp.float32)
    for o in range(1, parts_ref.shape[0]):
        total = total + parts_ref[o].astype(jnp.float32)
    gaps = gaps_ref[...].astype(jnp.float32)
    rows = []
    for c in range(3):
        masked = total[:, 128 * c : 128 * c + 128] * gaps
        masked_ref[16 * c : 16 * c + 16, :] = masked
        padded = jnp.concatenate([masked, jnp.zeros((112, 128), jnp.float32)], axis=0)
        spread = pltpu.roll(
            dot(own_ref[c], padded, ((1,), (1,))), 0, 1, stride=16, stride_axis=0
        )
        rows.append(jnp.sum(spread, axis=0, keepdims=True))
    message_ref[...] = jnp.broadcast_to(jnp.concatenate(rows, axis=0)[None], message_ref.shape)


def split_in_two(value):
    high = value.astype(jnp.bfloat16)
    return high, (value - high.astype(jnp.float32)).astype(jnp.bfloat16)


def spread_kernel(
    masked_ref, near_ref, edge_ref, gaps_ref, design_ref, here_ref, basis_ref, held_ref, sems
):
    copies = chunk_copies(design_ref, held_ref, sems)
    for copy in copies:
        copy.start()
    gaps = gaps_ref[...].astype(jnp.float32)
    pieces = []
    highs, lows = [], []
    blank = jnp.zeros((8, 128), jnp.bfloat16)
    for c in range(3):
        pieces.append(dot(masked_ref[16 * c : 16 * c + 16, :], near_ref[c], ((1,), (0,))) * gaps)
        high, low = split_in_two(edge_ref[c] * gaps)
        highs.append(jnp.concatenate([high if d == c else blank for d in range(3)], axis=1))
        lows.append(jnp.concatenate([low if d == c else blank for d in range(3)], axis=1))
    rows = jnp.concatenate(
        [*split_in_two(jnp.concatenate(pieces, axis=1)), *highs, *lows], axis=0
    )
    count, _, _, width = held_ref.shape
    for k in range(count):
        copies[k].wait()
        found = jnp.dot(
            rows, held_ref[k].reshape(384, width), preferred_element_type=jnp.float32
        )
        here_ref[:, width * k : width * k + width] = found[0:16] + found[16:32]
        high, low = split_in_two(found[32:56] + found[56:80])
        basis_ref[0:24, width * k : width * k + width] = high
        basis_ref[24:48, width * k : width * k + width] = low
        basis_ref[48:72, width * k : width * k + width] = high


def gradient_kernel(states_ref, link_ref, here_ref, basis_ref, out_ref):
    parts = []
    for c in range(3):
        states = states_ref[:, c, :]
        turned = [states] + [pltpu.roll(states, 128 - 16 * i, 1) for i in range(1, 8)]
        parts.append(dot(link_ref[c], jnp.concatenate(turned, axis=0), ((1,), (0,))))
    found = jnp.concatenate(parts, axis=0)
    high = found.astype(jnp.bfloat16).astype(jnp.float32)
    tall = jnp.concatenate(
        [high, high, found - high, jnp.zeros((56, 128), jnp.float32)], axis=0
    )
    left = tall.T[0:16, 0:72].astype(jnp.bfloat16)
    peers = out_ref.shape[0]
    for p in range(0, peers, 4):
        span = slice(256 * p, 256 * p + 1024)
        there = jnp.dot(left, basis_ref[:, span], preferred_element_type=jnp.float32)
        whole = (here_ref[:, span] + there).astype(out_ref.dtype)
        for q in range(4):
            out_ref[p + q] = whole[:, 256 * q : 256 * q + 256]


def tables_kernel(
    place_ref, aro_ref, mao_ref, arr_ref, mar_ref, got_ref, own_ref, near_ref, link_ref, edge_ref, *tables
):
    response_kernel(place_ref, aro_ref, mao_ref, arr_ref, mar_ref, *tables)
    segment_kernel(place_ref, got_ref, *tables, own_ref, near_ref, link_ref, edge_ref)


def pack_kernel(direction_any, ids_any, out_ref, direction_ref, ids_ref, sems):
    copies = [
        pltpu.make_async_copy(direction_any, direction_ref, sems.at[0]),
        pltpu.make_async_copy(ids_any, ids_ref, sems.at[1]),
    ]
    for copy in copies:
        copy.start()
    for copy in copies:
        copy.wait()
    packed = direction_ref[:, 0, :].astype(jnp.bfloat16)
    ids = jnp.broadcast_to(ids_ref[...].astype(jnp.float32), (8, 128)).astype(jnp.bfloat16)
    sheet = jnp.concatenate([packed[:, :128], packed[:, 128:], ids], axis=0)
    out_ref[...] = jnp.broadcast_to(sheet[None], out_ref.shape)


def chunk_copies(design_ref, held_ref, sems):
    width = held_ref.shape[3]
    return [
        pltpu.make_async_copy(
            design_ref.at[:, :, pl.ds(width * k, width)], held_ref.at[k], sems.at[k]
        )
        for k in range(held_ref.shape[0])
    ]


def observe_kernel(got_ref, design_ref, early_ref, out_ref, held_ref, sems):
    count, _, _, width = held_ref.shape
    start = early_ref.shape[2]
    copies = [
        pltpu.make_async_copy(
            design_ref.at[:, :, pl.ds(start + width * k, width)], held_ref.at[k], sems.at[k]
        )
        for k in range(count)
    ]
    for copy in copies:
        copy.start()

    def product(first, block):
        pieces = []
        for p in range(first, first + block.shape[1] // 256):
            pieces += [got_ref[p, 0:16, :], got_ref[p, 16:32, :]]
        return lax.dot_general(
            jnp.concatenate(pieces, axis=1),
            block,
            (((1,), (1,)), ((), ())),
            preferred_element_type=jnp.float32,
        )

    total = jnp.zeros((16, 384), jnp.float32)
    for at in range(0, start, width):
        total = total + product(at // 256, early_ref[:, :, at : at + width].reshape(384, width))
    for k in range(count):
        copies[k].wait()
        total = total + product((start + width * k) // 256, held_ref[k].reshape(384, width))
    out_ref[...] = jnp.broadcast_to(total.astype(jnp.bfloat16)[None], out_ref.shape)


def precondition(vector, precond_ref):
    return jnp.concatenate(
        [dot(vector[:, 128 * k : 128 * k + 128], precond_ref[0, k], ((1,), (1,))) for k in range(2)],
        axis=1,
    )


def applied_kernel(precond_ref, residual_ref, applied_ref):
    applied_ref[...] = precondition(residual_ref[:, 0, :], precond_ref)


def image_kernel(
    arrived_ref, kaula_ref, precond_ref, residual_ref, direction_ref, applied_ref, message_ref, image_ref, both_ref
):
    total = arrived_ref[0].astype(jnp.float32)
    for p in range(1, arrived_ref.shape[0]):
        total = total + arrived_ref[p].astype(jnp.float32)
    direction = direction_ref[:, 0, :]
    residual = residual_ref[:, 0, :]
    image = total + kaula_ref[...] * direction
    applied = applied_ref[...]
    image_applied = precondition(image, precond_ref)
    products = jnp.concatenate(
        [
            residual * applied,
            direction * image,
            image * applied,
            image * image_applied,
            jnp.zeros((64, 256), jnp.float32),
        ],
        axis=0,
    )
    sums = dot(jnp.ones((8, 256), jnp.float32), products, ((1,), (1,)))
    message_ref[...] = jnp.broadcast_to(sums[None, 0:1, :], message_ref.shape)
    image_ref[...] = image
    both_ref[...] = image_applied


def update_kernel(
    sums_ref, image_ref, applied_ref, both_ref, solution_ref, residual_ref, direction_ref, sol_ref, res_ref, dir_ref
):
    total = jnp.sum(sums_ref[...], axis=0)
    row = lax.broadcasted_iota(jnp.int32, (16, 128), 0)
    lane = lax.broadcasted_iota(jnp.int32, (16, 128), 1)
    wide = jnp.broadcast_to(total, (16, 128))
    old_rz, curvature, cross, square = [
        jnp.sum(jnp.where(lane == row + 16 * k, wide, 0.0), axis=1, keepdims=True)
        for k in range(4)
    ]
    step = old_rz / curvature
    new_rz = old_rz - 2.0 * step * cross + step * step * square
    direction = direction_ref[:, 0, :]
    fresh = applied_ref[...] - step * both_ref[...] + (new_rz / old_rz) * direction
    sol_ref[:, 0, :] = solution_ref[:, 0, :] + step * direction
    res_ref[:, 0, :] = residual_ref[:, 0, :] - step * image_ref[...]
    dir_ref[:, 0, :] = fresh


def run(kernel, outs, args, scalars=(), anywhere=(), scratch=(), flops=100000, limit=SMALL_LIMIT):
    spaces = [
        pltpu.SMEM if i in scalars else pltpu.HBM if i in anywhere else pltpu.VMEM
        for i in range(len(args))
    ]
    shapes = [jax.ShapeDtypeStruct(*out) for out in outs]
    found = pl.pallas_call(
        kernel,
        out_shape=shapes,
        in_specs=[pl.BlockSpec(memory_space=space) for space in spaces],
        out_specs=[pl.BlockSpec(memory_space=pltpu.VMEM) for _ in shapes],
        scratch_shapes=list(scratch),
        cost_estimate=pl.CostEstimate(flops=flops, bytes_accessed=1000000, transcendentals=0),
        compiler_params=pltpu.CompilerParams(vmem_limit_bytes=limit),
    )(*args)
    return found


def exchange(value, axes):
    return lax.all_to_all(value, axes, split_axis=0, concat_axis=0, tiled=True)


def on_device(
    design,
    gap_flags,
    segment_ids,
    ar_order,
    ma_order,
    ar_roots,
    ma_roots,
    kaula,
    precond,
    solution,
    residual,
    direction,
):
    f32, bf16 = jnp.float32, jnp.bfloat16
    count = lax.axis_size(TM)
    others = lax.axis_size(ORDER)
    everyone = count * others
    place = lax.axis_index(TM).astype(jnp.int32).reshape(1, 1)
    gaps = gap_flags.reshape(1, 128)
    (sheets,) = run(
        pack_kernel,
        [((count, 40, 128), bf16)],
        [
            pltpu.with_memory_space_constraint(direction, pltpu.HBM),
            pltpu.with_memory_space_constraint(segment_ids.reshape(1, 128), pltpu.HBM),
        ],
        anywhere=(0, 1),
        scratch=[
            pltpu.VMEM((16, 1, 256), f32),
            pltpu.VMEM((1, 128), jnp.int32),
            pltpu.SemaphoreType.DMA((2,)),
        ],
        limit=VMEM_LIMIT,
    )
    got = exchange(sheets, TM)

    def held(chunks):
        return [
            pltpu.VMEM((chunks, 3, 128, design.shape[2] // chunks), bf16),
            pltpu.SemaphoreType.DMA((chunks,)),
        ]

    (partial,) = run(
        observe_kernel,
        [((others, 16, 384), bf16)],
        [got, design, lax.slice_in_dim(design, 0, EARLY, axis=2)],
        anywhere=(1,),
        scratch=[
            pltpu.VMEM(((design.shape[2] - EARLY) // 512, 3, 128, 512), bf16),
            pltpu.SemaphoreType.DMA(((design.shape[2] - EARLY) // 512,)),
        ],
        limit=VMEM_LIMIT,
    )
    parts = exchange(partial, ORDER)
    own, near, link, edge = run(
        tables_kernel,
        [((3, 8, 128), f32), ((3, 128, 128), f32), ((3, 8, 256), f32), ((3, 8, 128), f32)],
        [place, ar_order, ma_order, ar_roots, ma_roots, got],
        scalars=(0, 1, 2, 3, 4),
        scratch=[
            pltpu.VMEM((3, 128, 128), f32),
            pltpu.VMEM((4, 8, 128), f32),
            pltpu.VMEM((4, 8, 128), f32),
            pltpu.VMEM((3, 8, 256), f32),
            pltpu.VMEM((LEVELS - 1, 10, 8, 128), f32),
            pltpu.VMEM((LEVELS - 1, 10, 8, 128), f32),
        ],
        flops=10000000,
    )
    message, masked = run(
        state_kernel, [((count, 3, 128), f32), ((48, 128), f32)], [parts, gaps, own]
    )
    states = exchange(message, TM)
    here, basis = run(
        spread_kernel,
        [((16, design.shape[2]), f32), ((72, design.shape[2]), bf16)],
        [masked, near, edge, gaps, design],
        anywhere=(4,),
        scratch=held(8),
        flops=10000000,
        limit=VMEM_LIMIT,
    )
    (gradient,) = run(
        gradient_kernel,
        [((count, 16, 256), bf16)],
        [states, link, here, basis],
        limit=16 * 1024 * 1024,
    )
    arrived = exchange(gradient, TM)
    (applied,) = run(applied_kernel, [((16, 256), f32)], [precond, residual], flops=10000000)
    sums, image, image_applied = run(
        image_kernel,
        [((everyone, 1, 128), f32)] + [((16, 256), f32)] * 2,
        [arrived, kaula, precond, residual, direction, applied],
    )
    gathered = exchange(sums, TM_ORDER)
    return tuple(
        run(
            update_kernel,
            [((16, 1, 256), f32)] * 3,
            [gathered, image, applied, image_applied, solution, residual, direction],
        )
    )


def solution(mesh):
    split = Mesh(mesh.devices.reshape(4, 8, 4, 2), TM_ORDER)
    in_specs = (
        P(None, TM, ORDER),
        P(TM),
        P(TM),
        P(),
        P(),
        P(),
        P(),
        P(ORDER, TM),
        P(ORDER, TM, None, None),
        P(None, ORDER, TM),
        P(None, ORDER, TM),
        P(None, ORDER, TM),
    )
    out_specs = (P(None, ORDER, TM),) * 3
    return jax.shard_map(
        on_device, mesh=split, in_specs=in_specs, out_specs=out_specs, check_vma=False
    )
```

```python
import jax
import jax.numpy as jnp
from jax import lax
from jax.experimental import pallas as pl
from jax.experimental.pallas import tpu as pltpu
from jax.sharding import Mesh
from jax.sharding import PartitionSpec as P

TM = ("tm_0", "tm_1")
ORDER = ("order_0", "order_1")
TM_ORDER = TM + ORDER
VMEM_LIMIT = 50 * 1024 * 1024
SMALL_LIMIT = 8 * 1024 * 1024
KEPT = 2048
EARLY = 3584

precise = lax.Precision.HIGHEST
LEVELS = 12
RADIX = 7


def dot(a, b, dims):
    return lax.dot_general(
        a, b, (dims, ((), ())), precision=precise, preferred_element_type=jnp.float32
    )


def splat_rows(read):
    row = lax.broadcasted_iota(jnp.int32, (8, 128), 0)
    out = jnp.zeros((8, 128), jnp.float32)
    for c in range(3):
        out = jnp.where(row == c, read(c), out)
    return out


LOWER = [(i, j) for i in range(4) for j in range(i + 1)]
UPPER = [(i, j) for i in range(4) for j in range(i, 4)]


def active_roots(roots_ref, order_ref):
    return [
        splat_rows(lambda c: jnp.where(k < order_ref[c], roots_ref[c, k], jnp.float32(0.0)))
        for k in range(4)
    ]


def sum_of(terms):
    while len(terms) > 1:
        terms = [
            terms[k] + terms[k + 1] if k + 1 < len(terms) else terms[k]
            for k in range(0, len(terms), 2)
        ]
    return terms[0]


def times(left, right):
    return {
        (i, j): sum_of([left[i, k] * right[k, j] for k in range(j, i + 1)]) for i, j in LOWER
    }


def gram_step(gram, power):
    half = {
        (i, j): sum_of([gram[min(i, k), max(i, k)] * power[k, j] for k in range(j, 4)])
        for i in range(4)
        for j in range(4)
    }
    return {(i, j): sum_of([power[k, i] * half[k, j] for k in range(i, 4)]) for i, j in UPPER}


def row_times(vector, power):
    return [sum_of([vector[i] * power[i, j] for i in range(j, 4)]) for j in range(4)]


def row_power(vector, powers, number, bits):
    for k in range(bits):
        on = ((number >> k) & 1) == 1
        moved = row_times(vector, powers[k])
        vector = [jnp.where(on, moved[j], vector[j]) for j in range(4)]
    return vector


def column_power(vector, powers, number, bits):
    for k in range(bits):
        on = ((number >> k) & 1) == 1
        moved = [sum_of([powers[k][i, j] * vector[j] for j in range(i + 1)]) for i in range(4)]
        vector = [jnp.where(on, moved[i], vector[i]) for i in range(4)]
    return vector


def response_kernel(
    place_ref, aro_ref, mao_ref, arr_ref, mar_ref, toep_ref, gam_ref, fin_ref, reach_ref, pow_ref, gram_ref
):
    poles = active_roots(arr_ref, aro_ref)
    zeros = active_roots(mar_ref, mao_ref)
    kappa = [poles[j] - zeros[j] for j in range(4)]
    one = jnp.ones((8, 128), jnp.float32)
    powers = [{(i, j): poles[i] if i == j else kappa[j] for i, j in LOWER}]
    for _ in range(LEVELS - 1):
        powers.append(times(powers[-1], powers[-1]))
    gram = {(i, j): kappa[i] * kappa[j] for i, j in UPPER}
    for k in range(LEVELS - 1):
        for at, (i, j) in enumerate(LOWER):
            pow_ref[k, at] = powers[k][i, j]
        for at, (i, j) in enumerate(UPPER):
            gram_ref[k, at] = gram[i, j]
        if k < LEVELS - 2:
            add = gram_step(gram, powers[k])
            gram = {at: gram[at] + add[at] for at in UPPER}
    lane = lax.broadcasted_iota(jnp.int32, (8, 128), 1)
    gam = row_power(kappa, powers, lane, RADIX)
    fin = column_power([one] * 4, powers, 127 - lane, RADIX)
    for i in range(4):
        gam_ref[i] = gam[i]
        fin_ref[i] = fin[i]
    eta = jnp.where(lane == 0, 1.0, pltpu.roll(sum_of(gam), 1, 1))
    big_row = lax.broadcasted_iota(jnp.int32, (128, 128), 0)
    big_lane = lax.broadcasted_iota(jnp.int32, (128, 128), 1)
    for c in range(3):
        base = jnp.broadcast_to(eta[c : c + 1, :], (128, 128))
        turned = pltpu.roll(base, 0, 1, stride=1, stride_axis=0)
        toep_ref[c] = jnp.where(big_lane >= big_row, turned, 0.0)
    place = place_ref[0, 0]
    row = lax.broadcasted_iota(jnp.int32, (8, 128), 0)
    front = row < 4
    for side in range(2):
        wide = lane + 128 * side
        peer, kind = wide & 31, wide >> 5
        gap = jnp.where(front, place - 1 - peer, peer - 1 - place)
        steps = jnp.maximum(gap, 0)
        for c in range(3):
            vector = [jnp.where((row & 3) == j, 1.0, 0.0) for j in range(4)]
            for k in range(5):
                cut = {at: powers[RADIX + k][at][c : c + 1, :] for at in LOWER}
                on = ((steps >> k) & 1) == 1
                moved = []
                for j in range(4):
                    terms = [vector[j] * cut[j, j]]
                    for i in range(4):
                        if i > j:
                            terms.append(vector[i] * jnp.where(front, cut[i, j], 0.0))
                        if i < j:
                            terms.append(vector[i] * jnp.where(front, 0.0, cut[j, i]))
                    moved.append(sum_of(terms))
                vector = [jnp.where(on, moved[j], vector[j]) for j in range(4)]
            picked = jnp.zeros((8, 128), jnp.float32)
            for j in range(4):
                picked = jnp.where((kind & 3) == j, vector[j], picked)
            used = ((kind < 4) == front) & (gap >= 0)
            reach_ref[c, :, 128 * side : 128 * side + 128] = jnp.where(used, picked, 0.0)


def segment_kernel(
    place_ref, got_ref, toep_ref, gam_ref, fin_ref, reach_ref, pow_ref, gram_ref, own_ref, near_ref, link_ref, edge_ref
):
    place = place_ref[0, 0]
    row = lax.broadcasted_iota(jnp.int32, (8, 128), 0)
    groups = []
    for g in range(4):
        group = jnp.zeros((8, 128), jnp.float32)
        for s in range(8):
            group = jnp.where(row == s, got_ref[8 * g + s, 32:40, :].astype(jnp.float32), group)
        groups.append(group)
    ids = jnp.concatenate(groups, axis=0)
    peer = lax.broadcasted_iota(jnp.int32, (32, 128), 0)
    mine = jnp.sum(jnp.where(peer == place, ids, 0.0), axis=0, keepdims=True)
    before = jnp.sum(jnp.where(peer == place - 1, ids, 0.0), axis=0, keepdims=True)
    ends = jnp.broadcast_to(ids[:, 127:128], (32, 128))
    last = jnp.broadcast_to(mine[:, 127:128], (1, 128))
    prev = jnp.where(place > 0, jnp.broadcast_to(before[:, 127:128], (1, 128)), -1.0)
    count = jnp.sum(
        jnp.where((peer > place) & (ids == last), 1.0, 0.0), axis=0, keepdims=True
    )
    left = jnp.sum(count, axis=1, keepdims=True).astype(jnp.int32)
    left = jnp.broadcast_to(left, (8, 128))
    ends_before = pltpu.roll(ends, 1, 0)
    keep_past = jnp.where((peer < place) & (ends == prev), 1.0, 0.0)
    keep_next = jnp.where((peer > place) & (ends_before == last), 1.0, 0.0)
    wide_past = jnp.concatenate([keep_past, jnp.zeros((96, 128), jnp.float32)], axis=0).T[0:1, :]
    wide_next = jnp.concatenate([keep_next, jnp.zeros((96, 128), jnp.float32)], axis=0).T[0:1, :]
    keeps = []
    for wide_keep in (wide_past, wide_next):
        part = wide_keep
        for turn in (32, 64, 96):
            part = part + pltpu.roll(wide_keep, turn, 1)
        keeps.append(part)
    keep = jnp.concatenate(keeps, axis=1)
    gram = {at: jnp.zeros((8, 128), jnp.float32) for at in UPPER}
    for k in range(LEVELS - 1):
        power = {pair: pow_ref[k, at] for at, pair in enumerate(LOWER)}
        add = gram_step(gram, power)
        on = ((left >> k) & 1) == 1
        gram = {
            pair: jnp.where(on, gram_ref[k, at] + add[pair], gram[pair])
            for at, pair in enumerate(UPPER)
        }
    lead = jnp.where(mine == prev, 1.0, 0.0)
    trail = jnp.where(mine == last, 1.0, 0.0)
    cont = jnp.where(last == prev, 1.0, 0.0)
    fin = [fin_ref[i] * trail for i in range(4)]
    gam = [gam_ref[i] * lead for i in range(4)]
    fold = [
        sum_of([fin[j] * gram[min(i, j), max(i, j)] for j in range(4)]) for i in range(4)
    ]
    block = {pair: pow_ref[RADIX, at] for at, pair in enumerate(LOWER)}
    past = [cont * value for value in row_times(fold, block)]
    big_row = lax.broadcasted_iota(jnp.int32, (128, 128), 0)
    big_lane = lax.broadcasted_iota(jnp.int32, (128, 128), 1)
    wide = jnp.broadcast_to(mine, (128, 128))
    tall = jnp.sum(jnp.where(big_row == big_lane, wide, 0.0), axis=1, keepdims=True)
    same = wide == jnp.broadcast_to(tall, (128, 128))

    def rows(values, c, start):
        out = jnp.zeros((8, 128), jnp.float32)
        for i in range(4):
            out = jnp.where(row == start + i, values[i][c : c + 1, :], out)
        return out

    for c in range(3):
        toep = jnp.where(same, toep_ref[c], 0.0)
        probe = dot(rows(gam, c, 0), toep, ((1,), (1,)))
        out_p = jnp.where(row < 4, probe, 0.0) + rows(past, c, 0)
        fin_low = rows(fin, c, 0)
        near_ref[c] = dot(toep, toep, ((1,), (1,))) + dot(rows(fold, c, 0), fin_low, ((0,), (0,)))
        own_ref[c] = fin_low + pltpu.roll(out_p, 4, 0)
        edge_ref[c] = out_p + rows(fin, c, 4)
        link_ref[c] = reach_ref[c] * keep


def state_kernel(parts_ref, gaps_ref, own_ref, message_ref, masked_ref):
    total = parts_ref[0].astype(jnp.float32)
    for o in range(1, parts_ref.shape[0]):
        total = total + parts_ref[o].astype(jnp.float32)
    gaps = gaps_ref[...].astype(jnp.float32)
    rows = []
    for c in range(3):
        masked = total[:, 128 * c : 128 * c + 128] * gaps
        masked_ref[16 * c : 16 * c + 16, :] = masked
        padded = jnp.concatenate([masked, jnp.zeros((112, 128), jnp.float32)], axis=0)
        spread = pltpu.roll(
            dot(own_ref[c], padded, ((1,), (1,))), 0, 1, stride=16, stride_axis=0
        )
        rows.append(jnp.sum(spread, axis=0, keepdims=True))
    message_ref[...] = jnp.broadcast_to(jnp.concatenate(rows, axis=0)[None], message_ref.shape)


def split_in_two(value):
    high = value.astype(jnp.bfloat16)
    return high, (value - high.astype(jnp.float32)).astype(jnp.bfloat16)


def spread_kernel(
    masked_ref, near_ref, edge_ref, gaps_ref, design_ref, kept_ref, here_ref, basis_ref, held_ref, sems
):
    count, _, _, width = held_ref.shape
    start = kept_ref.shape[2]
    copies = [
        pltpu.make_async_copy(
            design_ref.at[:, :, pl.ds(start + width * k, width)], held_ref.at[k], sems.at[k]
        )
        for k in range(count)
    ]
    for copy in copies:
        copy.start()
    gaps = gaps_ref[...].astype(jnp.float32)
    pieces = []
    highs, lows = [], []
    blank = jnp.zeros((8, 128), jnp.bfloat16)
    for c in range(3):
        pieces.append(dot(masked_ref[16 * c : 16 * c + 16, :], near_ref[c], ((1,), (0,))) * gaps)
        high, low = split_in_two(edge_ref[c] * gaps)
        highs.append(jnp.concatenate([high if d == c else blank for d in range(3)], axis=1))
        lows.append(jnp.concatenate([low if d == c else blank for d in range(3)], axis=1))
    rows = jnp.concatenate(
        [*split_in_two(jnp.concatenate(pieces, axis=1)), *highs, *lows], axis=0
    )

    def spread(at, block):
        found = jnp.dot(rows, block, preferred_element_type=jnp.float32)
        here_ref[:, at : at + width] = found[0:16] + found[16:32]
        high, low = split_in_two(found[32:56] + found[56:80])
        basis_ref[0:24, at : at + width] = high
        basis_ref[24:48, at : at + width] = low

    for at in range(0, start, width):
        spread(at, kept_ref[:, :, at : at + width].reshape(384, width))
    for k in range(count):
        copies[k].wait()
        spread(start + width * k, held_ref[k].reshape(384, width))


def gradient_kernel(states_ref, link_ref, here_ref, basis_ref, out_ref):
    parts = []
    for c in range(3):
        states = states_ref[:, c, :]
        turned = [states] + [pltpu.roll(states, 128 - 16 * i, 1) for i in range(1, 8)]
        parts.append(dot(link_ref[c], jnp.concatenate(turned, axis=0), ((1,), (0,))))
    lane = lax.broadcasted_iota(jnp.int32, (24, 128), 1)
    found = jnp.where(lane < 16, jnp.concatenate(parts, axis=0), 0.0)
    high = found.astype(jnp.bfloat16).astype(jnp.float32)
    low = pltpu.roll(found - high, 16, 1)
    tall = jnp.concatenate([high + low, high, jnp.zeros((80, 128), jnp.float32)], axis=0)
    left = tall.T[0:32, 0:48].astype(jnp.bfloat16)
    peers = out_ref.shape[0]
    for p in range(0, peers, 4):
        span = slice(256 * p, 256 * p + 1024)
        there = jnp.dot(left, basis_ref[:, span], preferred_element_type=jnp.float32)
        whole = (here_ref[:, span] + there[0:16] + there[16:32]).astype(out_ref.dtype)
        for q in range(4):
            out_ref[p + q] = whole[:, 256 * q : 256 * q + 256]


def tables_kernel(
    place_ref, aro_ref, mao_ref, arr_ref, mar_ref, got_ref, own_ref, near_ref, link_ref, edge_ref, *tables
):
    response_kernel(place_ref, aro_ref, mao_ref, arr_ref, mar_ref, *tables)
    segment_kernel(place_ref, got_ref, *tables, own_ref, near_ref, link_ref, edge_ref)


def pack_kernel(direction_any, ids_any, out_ref, direction_ref, ids_ref, sems):
    copies = [
        pltpu.make_async_copy(direction_any, direction_ref, sems.at[0]),
        pltpu.make_async_copy(ids_any, ids_ref, sems.at[1]),
    ]
    for copy in copies:
        copy.start()
    for copy in copies:
        copy.wait()
    packed = direction_ref[:, 0, :].astype(jnp.bfloat16)
    ids = jnp.broadcast_to(ids_ref[...].astype(jnp.float32), (8, 128)).astype(jnp.bfloat16)
    sheet = jnp.concatenate([packed[:, :128], packed[:, 128:], ids], axis=0)
    out_ref[...] = jnp.broadcast_to(sheet[None], out_ref.shape)


def observe_kernel(got_ref, design_ref, kept_ref, early_ref, out_ref, held_ref, sems):
    count, _, _, width = held_ref.shape
    middle = kept_ref.shape[2]
    start = middle + early_ref.shape[2]
    copies = [
        pltpu.make_async_copy(
            design_ref.at[:, :, pl.ds(start + width * k, width)], held_ref.at[k], sems.at[k]
        )
        for k in range(count)
    ]
    for copy in copies:
        copy.start()

    def product(first, block):
        pieces = []
        for p in range(first, first + block.shape[1] // 256):
            pieces += [got_ref[p, 0:16, :], got_ref[p, 16:32, :]]
        return lax.dot_general(
            jnp.concatenate(pieces, axis=1),
            block,
            (((1,), (1,)), ((), ())),
            preferred_element_type=jnp.float32,
        )

    total = jnp.zeros((16, 384), jnp.float32)
    for at in range(0, middle, width):
        total = total + product(at // 256, kept_ref[:, :, at : at + width].reshape(384, width))
    for at in range(middle, start, width):
        block = early_ref[:, :, at - middle : at - middle + width].reshape(384, width)
        total = total + product(at // 256, block)
    for k in range(count):
        copies[k].wait()
        total = total + product((start + width * k) // 256, held_ref[k].reshape(384, width))
    out_ref[...] = jnp.broadcast_to(total.astype(jnp.bfloat16)[None], out_ref.shape)


def image_kernel(
    arrived_ref, kaula_ref, precond_ref, residual_ref, direction_ref, message_ref, image_ref, applied_ref, both_ref
):
    total = arrived_ref[0].astype(jnp.float32)
    for p in range(1, arrived_ref.shape[0]):
        total = total + arrived_ref[p].astype(jnp.float32)
    direction = direction_ref[:, 0, :]
    residual = residual_ref[:, 0, :]
    image = total + kaula_ref[...] * direction
    stack = jnp.concatenate([residual, image], axis=0)
    mixed = jnp.concatenate(
        [dot(stack[:, 128 * k : 128 * k + 128], precond_ref[0, k], ((1,), (1,))) for k in range(2)],
        axis=1,
    )
    applied, image_applied = mixed[0:16], mixed[16:32]
    products = jnp.concatenate(
        [
            residual * applied,
            direction * image,
            image * applied,
            image * image_applied,
            jnp.zeros((64, 256), jnp.float32),
        ],
        axis=0,
    )
    sums = dot(jnp.ones((8, 256), jnp.float32), products, ((1,), (1,)))
    message_ref[...] = jnp.broadcast_to(sums[None, 0:1, :], message_ref.shape)
    image_ref[...] = image
    applied_ref[...] = applied
    both_ref[...] = image_applied


def update_kernel(
    sums_ref, image_ref, applied_ref, both_ref, solution_ref, residual_ref, direction_ref, sol_ref, res_ref, dir_ref
):
    total = jnp.sum(sums_ref[...], axis=0)
    row = lax.broadcasted_iota(jnp.int32, (16, 128), 0)
    lane = lax.broadcasted_iota(jnp.int32, (16, 128), 1)
    wide = jnp.broadcast_to(total, (16, 128))
    old_rz, curvature, cross, square = [
        jnp.sum(jnp.where(lane == row + 16 * k, wide, 0.0), axis=1, keepdims=True)
        for k in range(4)
    ]
    step = old_rz / curvature
    new_rz = old_rz - 2.0 * step * cross + step * step * square
    direction = direction_ref[:, 0, :]
    fresh = applied_ref[...] - step * both_ref[...] + (new_rz / old_rz) * direction
    sol_ref[:, 0, :] = solution_ref[:, 0, :] + step * direction
    res_ref[:, 0, :] = residual_ref[:, 0, :] - step * image_ref[...]
    dir_ref[:, 0, :] = fresh


def run(kernel, outs, args, scalars=(), anywhere=(), scratch=(), flops=100000, limit=SMALL_LIMIT):
    spaces = [
        pltpu.SMEM if i in scalars else pltpu.HBM if i in anywhere else pltpu.VMEM
        for i in range(len(args))
    ]
    shapes = [jax.ShapeDtypeStruct(*out) for out in outs]
    found = pl.pallas_call(
        kernel,
        out_shape=shapes,
        in_specs=[pl.BlockSpec(memory_space=space) for space in spaces],
        out_specs=[pl.BlockSpec(memory_space=pltpu.VMEM) for _ in shapes],
        scratch_shapes=list(scratch),
        cost_estimate=pl.CostEstimate(flops=flops, bytes_accessed=1000000, transcendentals=0),
        compiler_params=pltpu.CompilerParams(vmem_limit_bytes=limit),
    )(*args)
    return found


def exchange(value, axes):
    return lax.all_to_all(value, axes, split_axis=0, concat_axis=0, tiled=True)


def on_device(
    design,
    gap_flags,
    segment_ids,
    ar_order,
    ma_order,
    ar_roots,
    ma_roots,
    kaula,
    precond,
    solution,
    residual,
    direction,
):
    f32, bf16 = jnp.float32, jnp.bfloat16
    count = lax.axis_size(TM)
    others = lax.axis_size(ORDER)
    everyone = count * others
    place = lax.axis_index(TM).astype(jnp.int32).reshape(1, 1)
    gaps = gap_flags.reshape(1, 128)
    (sheets,) = run(
        pack_kernel,
        [((count, 40, 128), bf16)],
        [
            pltpu.with_memory_space_constraint(direction, pltpu.HBM),
            pltpu.with_memory_space_constraint(segment_ids.reshape(1, 128), pltpu.HBM),
        ],
        anywhere=(0, 1),
        scratch=[
            pltpu.VMEM((16, 1, 256), f32),
            pltpu.VMEM((1, 128), jnp.int32),
            pltpu.SemaphoreType.DMA((2,)),
        ],
        limit=VMEM_LIMIT,
    )
    got = exchange(sheets, TM)

    (sheets,) = run(
        pack_kernel,
        [((count, 40, 128), bf16)],
        [
            pltpu.with_memory_space_constraint(direction, pltpu.HBM),
            pltpu.with_memory_space_constraint(segment_ids.reshape(1, 128), pltpu.HBM),
        ],
        anywhere=(0, 1),
        scratch=[
            pltpu.VMEM((16, 1, 256), f32),
            pltpu.VMEM((1, 128), jnp.int32),
            pltpu.SemaphoreType.DMA((2,)),
        ],
        limit=VMEM_LIMIT,
    )
    got = exchange(sheets, TM)

    def held(chunks):
        return [
            pltpu.VMEM((chunks, 3, 128, design.shape[2] // chunks), bf16),
            pltpu.SemaphoreType.DMA((chunks,)),
        ]

    kept = lax.slice_in_dim(design, 0, KEPT, axis=2)
    (partial,) = run(
        observe_kernel,
        [((others, 16, 384), bf16)],
        [got, design, kept, lax.slice_in_dim(design, KEPT, EARLY, axis=2)],
        anywhere=(1,),
        scratch=[
            pltpu.VMEM(((design.shape[2] - EARLY) // 512, 3, 128, 512), bf16),
            pltpu.SemaphoreType.DMA(((design.shape[2] - EARLY) // 512,)),
        ],
        limit=VMEM_LIMIT,
    )
    parts = exchange(partial, ORDER)
    own, near, link, edge = run(
        tables_kernel,
        [((3, 8, 128), f32), ((3, 128, 128), f32), ((3, 8, 256), f32), ((3, 8, 128), f32)],
        [place, ar_order, ma_order, ar_roots, ma_roots, got],
        scalars=(0, 1, 2, 3, 4),
        scratch=[
            pltpu.VMEM((3, 128, 128), f32),
            pltpu.VMEM((4, 8, 128), f32),
            pltpu.VMEM((4, 8, 128), f32),
            pltpu.VMEM((3, 8, 256), f32),
            pltpu.VMEM((LEVELS - 1, 10, 8, 128), f32),
            pltpu.VMEM((LEVELS - 1, 10, 8, 128), f32),
        ],
        flops=10000000,
    )
    message, masked = run(
        state_kernel, [((count, 3, 128), f32), ((48, 128), f32)], [parts, gaps, own]
    )
    states = exchange(message, TM)
    here, basis = run(
        spread_kernel,
        [((16, design.shape[2]), f32), ((48, design.shape[2]), bf16)],
        [masked, near, edge, gaps, design, kept],
        anywhere=(4,),
        scratch=[
            pltpu.VMEM(((design.shape[2] - KEPT) // 1024, 3, 128, 1024), bf16),
            pltpu.SemaphoreType.DMA(((design.shape[2] - KEPT) // 1024,)),
        ],
        flops=10000000,
        limit=VMEM_LIMIT,
    )
    (gradient,) = run(
        gradient_kernel,
        [((count, 16, 256), bf16)],
        [states, link, here, basis],
        limit=16 * 1024 * 1024,
    )
    arrived = exchange(gradient, TM)
    sums, image, applied, image_applied = run(
        image_kernel,
        [((everyone, 1, 128), f32)] + [((16, 256), f32)] * 3,
        [arrived, kaula, precond, residual, direction],
    )
    gathered = exchange(sums, TM_ORDER)
    return tuple(
        run(
            update_kernel,
            [((16, 1, 256), f32)] * 3,
            [gathered, image, applied, image_applied, solution, residual, direction],
        )
    )


def solution(mesh):
    split = Mesh(mesh.devices.reshape(4, 8, 4, 2), TM_ORDER)
    in_specs = (
        P(None, TM, ORDER),
        P(TM),
        P(TM),
        P(),
        P(),
        P(),
        P(),
        P(ORDER, TM),
        P(ORDER, TM, None, None),
        P(None, ORDER, TM),
        P(None, ORDER, TM),
        P(None, ORDER, TM),
    )
    out_specs = (P(None, ORDER, TM),) * 3
    return jax.shard_map(
        on_device, mesh=split, in_specs=in_specs, out_specs=out_specs, check_vma=False
    )
```

```python
import jax
import jax.numpy as jnp
from jax import lax
from jax.experimental import pallas as pl
from jax.experimental.pallas import tpu as pltpu
from jax.sharding import Mesh
from jax.sharding import PartitionSpec as P

TM = ("tm_0", "tm_1")
ORDER = ("order_0", "order_1")
TM_ORDER = TM + ORDER
VMEM_LIMIT = 50 * 1024 * 1024
SMALL_LIMIT = 8 * 1024 * 1024
KEPT = 2048
EARLY = 3584

precise = lax.Precision.HIGHEST
LEVELS = 12
RADIX = 7


def dot(a, b, dims):
    return lax.dot_general(
        a, b, (dims, ((), ())), precision=precise, preferred_element_type=jnp.float32
    )


def splat_rows(read):
    row = lax.broadcasted_iota(jnp.int32, (8, 128), 0)
    out = jnp.zeros((8, 128), jnp.float32)
    for c in range(3):
        out = jnp.where(row == c, read(c), out)
    return out


LOWER = [(i, j) for i in range(4) for j in range(i + 1)]
UPPER = [(i, j) for i in range(4) for j in range(i, 4)]


def active_roots(roots_ref, order_ref):
    return [
        splat_rows(lambda c: jnp.where(k < order_ref[c], roots_ref[c, k], jnp.float32(0.0)))
        for k in range(4)
    ]


def sum_of(terms):
    while len(terms) > 1:
        terms = [
            terms[k] + terms[k + 1] if k + 1 < len(terms) else terms[k]
            for k in range(0, len(terms), 2)
        ]
    return terms[0]


def times(left, right):
    return {
        (i, j): sum_of([left[i, k] * right[k, j] for k in range(j, i + 1)]) for i, j in LOWER
    }


def gram_step(gram, power):
    half = {
        (i, j): sum_of([gram[min(i, k), max(i, k)] * power[k, j] for k in range(j, 4)])
        for i in range(4)
        for j in range(4)
    }
    return {(i, j): sum_of([power[k, i] * half[k, j] for k in range(i, 4)]) for i, j in UPPER}


def row_times(vector, power):
    return [sum_of([vector[i] * power[i, j] for i in range(j, 4)]) for j in range(4)]


def row_power(vector, powers, number, bits):
    for k in range(bits):
        on = ((number >> k) & 1) == 1
        moved = row_times(vector, powers[k])
        vector = [jnp.where(on, moved[j], vector[j]) for j in range(4)]
    return vector


def column_power(vector, powers, number, bits):
    for k in range(bits):
        on = ((number >> k) & 1) == 1
        moved = [sum_of([powers[k][i, j] * vector[j] for j in range(i + 1)]) for i in range(4)]
        vector = [jnp.where(on, moved[i], vector[i]) for i in range(4)]
    return vector


def response_kernel(
    place_ref, aro_ref, mao_ref, arr_ref, mar_ref, toep_ref, gam_ref, fin_ref, reach_ref, pow_ref, gram_ref
):
    poles = active_roots(arr_ref, aro_ref)
    zeros = active_roots(mar_ref, mao_ref)
    kappa = [poles[j] - zeros[j] for j in range(4)]
    one = jnp.ones((8, 128), jnp.float32)
    powers = [{(i, j): poles[i] if i == j else kappa[j] for i, j in LOWER}]
    for _ in range(LEVELS - 1):
        powers.append(times(powers[-1], powers[-1]))
    gram = {(i, j): kappa[i] * kappa[j] for i, j in UPPER}
    for k in range(LEVELS - 1):
        for at, (i, j) in enumerate(LOWER):
            pow_ref[k, at] = powers[k][i, j]
        for at, (i, j) in enumerate(UPPER):
            gram_ref[k, at] = gram[i, j]
        if k < LEVELS - 2:
            add = gram_step(gram, powers[k])
            gram = {at: gram[at] + add[at] for at in UPPER}
    lane = lax.broadcasted_iota(jnp.int32, (8, 128), 1)
    gam = row_power(kappa, powers, lane, RADIX)
    fin = column_power([one] * 4, powers, 127 - lane, RADIX)
    for i in range(4):
        gam_ref[i] = gam[i]
        fin_ref[i] = fin[i]
    eta = jnp.where(lane == 0, 1.0, pltpu.roll(sum_of(gam), 1, 1))
    big_row = lax.broadcasted_iota(jnp.int32, (128, 128), 0)
    big_lane = lax.broadcasted_iota(jnp.int32, (128, 128), 1)
    for c in range(3):
        base = jnp.broadcast_to(eta[c : c + 1, :], (128, 128))
        turned = pltpu.roll(base, 0, 1, stride=1, stride_axis=0)
        toep_ref[c] = jnp.where(big_lane >= big_row, turned, 0.0)
    place = place_ref[0, 0]
    row = lax.broadcasted_iota(jnp.int32, (8, 128), 0)
    front = row < 4
    for side in range(2):
        wide = lane + 128 * side
        peer, kind = wide & 31, wide >> 5
        gap = jnp.where(front, place - 1 - peer, peer - 1 - place)
        steps = jnp.maximum(gap, 0)
        for c in range(3):
            vector = [jnp.where((row & 3) == j, 1.0, 0.0) for j in range(4)]
            for k in range(5):
                cut = {at: powers[RADIX + k][at][c : c + 1, :] for at in LOWER}
                on = ((steps >> k) & 1) == 1
                moved = []
                for j in range(4):
                    terms = [vector[j] * cut[j, j]]
                    for i in range(4):
                        if i > j:
                            terms.append(vector[i] * jnp.where(front, cut[i, j], 0.0))
                        if i < j:
                            terms.append(vector[i] * jnp.where(front, 0.0, cut[j, i]))
                    moved.append(sum_of(terms))
                vector = [jnp.where(on, moved[j], vector[j]) for j in range(4)]
            picked = jnp.zeros((8, 128), jnp.float32)
            for j in range(4):
                picked = jnp.where((kind & 3) == j, vector[j], picked)
            used = ((kind < 4) == front) & (gap >= 0)
            reach_ref[c, :, 128 * side : 128 * side + 128] = jnp.where(used, picked, 0.0)


def segment_kernel(
    place_ref, got_ref, toep_ref, gam_ref, fin_ref, reach_ref, pow_ref, gram_ref, own_ref, near_ref, link_ref, edge_ref
):
    place = place_ref[0, 0]
    row = lax.broadcasted_iota(jnp.int32, (8, 128), 0)
    groups = []
    for g in range(4):
        group = jnp.zeros((8, 128), jnp.float32)
        for s in range(8):
            group = jnp.where(row == s, got_ref[8 * g + s, 32:40, :].astype(jnp.float32), group)
        groups.append(group)
    ids = jnp.concatenate(groups, axis=0)
    peer = lax.broadcasted_iota(jnp.int32, (32, 128), 0)
    mine = jnp.sum(jnp.where(peer == place, ids, 0.0), axis=0, keepdims=True)
    before = jnp.sum(jnp.where(peer == place - 1, ids, 0.0), axis=0, keepdims=True)
    ends = jnp.broadcast_to(ids[:, 127:128], (32, 128))
    last = jnp.broadcast_to(mine[:, 127:128], (1, 128))
    prev = jnp.where(place > 0, jnp.broadcast_to(before[:, 127:128], (1, 128)), -1.0)
    count = jnp.sum(
        jnp.where((peer > place) & (ids == last), 1.0, 0.0), axis=0, keepdims=True
    )
    left = jnp.sum(count, axis=1, keepdims=True).astype(jnp.int32)
    left = jnp.broadcast_to(left, (8, 128))
    ends_before = pltpu.roll(ends, 1, 0)
    keep_past = jnp.where((peer < place) & (ends == prev), 1.0, 0.0)
    keep_next = jnp.where((peer > place) & (ends_before == last), 1.0, 0.0)
    wide_past = jnp.concatenate([keep_past, jnp.zeros((96, 128), jnp.float32)], axis=0).T[0:1, :]
    wide_next = jnp.concatenate([keep_next, jnp.zeros((96, 128), jnp.float32)], axis=0).T[0:1, :]
    keeps = []
    for wide_keep in (wide_past, wide_next):
        part = wide_keep
        for turn in (32, 64, 96):
            part = part + pltpu.roll(wide_keep, turn, 1)
        keeps.append(part)
    keep = jnp.concatenate(keeps, axis=1)
    gram = {at: jnp.zeros((8, 128), jnp.float32) for at in UPPER}
    for k in range(LEVELS - 1):
        power = {pair: pow_ref[k, at] for at, pair in enumerate(LOWER)}
        add = gram_step(gram, power)
        on = ((left >> k) & 1) == 1
        gram = {
            pair: jnp.where(on, gram_ref[k, at] + add[pair], gram[pair])
            for at, pair in enumerate(UPPER)
        }
    lead = jnp.where(mine == prev, 1.0, 0.0)
    trail = jnp.where(mine == last, 1.0, 0.0)
    cont = jnp.where(last == prev, 1.0, 0.0)
    fin = [fin_ref[i] * trail for i in range(4)]
    gam = [gam_ref[i] * lead for i in range(4)]
    fold = [
        sum_of([fin[j] * gram[min(i, j), max(i, j)] for j in range(4)]) for i in range(4)
    ]
    block = {pair: pow_ref[RADIX, at] for at, pair in enumerate(LOWER)}
    past = [cont * value for value in row_times(fold, block)]
    big_row = lax.broadcasted_iota(jnp.int32, (128, 128), 0)
    big_lane = lax.broadcasted_iota(jnp.int32, (128, 128), 1)
    wide = jnp.broadcast_to(mine, (128, 128))
    tall = jnp.sum(jnp.where(big_row == big_lane, wide, 0.0), axis=1, keepdims=True)
    same = wide == jnp.broadcast_to(tall, (128, 128))

    def rows(values, c, start):
        out = jnp.zeros((8, 128), jnp.float32)
        for i in range(4):
            out = jnp.where(row == start + i, values[i][c : c + 1, :], out)
        return out

    for c in range(3):
        toep = jnp.where(same, toep_ref[c], 0.0)
        probe = dot(rows(gam, c, 0), toep, ((1,), (1,)))
        out_p = jnp.where(row < 4, probe, 0.0) + rows(past, c, 0)
        fin_low = rows(fin, c, 0)
        near_ref[c] = dot(toep, toep, ((1,), (1,))) + dot(rows(fold, c, 0), fin_low, ((0,), (0,)))
        own_ref[c] = fin_low + pltpu.roll(out_p, 4, 0)
        edge_ref[c] = out_p + rows(fin, c, 4)
        link_ref[c] = reach_ref[c] * keep


def state_kernel(parts_ref, gaps_ref, own_ref, message_ref, masked_ref):
    total = parts_ref[0].astype(jnp.float32)
    for o in range(1, parts_ref.shape[0]):
        total = total + parts_ref[o].astype(jnp.float32)
    gaps = gaps_ref[...].astype(jnp.float32)
    rows = []
    for c in range(3):
        masked = total[:, 128 * c : 128 * c + 128] * gaps
        masked_ref[16 * c : 16 * c + 16, :] = masked
        padded = jnp.concatenate([masked, jnp.zeros((112, 128), jnp.float32)], axis=0)
        spread = pltpu.roll(
            dot(own_ref[c], padded, ((1,), (1,))), 0, 1, stride=16, stride_axis=0
        )
        rows.append(jnp.sum(spread, axis=0, keepdims=True))
    message_ref[...] = jnp.broadcast_to(jnp.concatenate(rows, axis=0)[None], message_ref.shape)


def split_in_two(value):
    high = value.astype(jnp.bfloat16)
    return high, (value - high.astype(jnp.float32)).astype(jnp.bfloat16)


def spread_kernel(
    masked_ref, near_ref, edge_ref, gaps_ref, design_ref, kept_ref, here_ref, basis_ref, held_ref, sems
):
    count, _, _, width = held_ref.shape
    start = kept_ref.shape[2]
    copies = [
        pltpu.make_async_copy(
            design_ref.at[:, :, pl.ds(start + width * k, width)], held_ref.at[k], sems.at[k]
        )
        for k in range(count)
    ]
    for copy in copies:
        copy.start()
    gaps = gaps_ref[...].astype(jnp.float32)
    pieces = []
    edges = []
    blank = jnp.zeros((8, 128), jnp.bfloat16)
    for c in range(3):
        pieces.append(dot(masked_ref[16 * c : 16 * c + 16, :], near_ref[c], ((1,), (0,))) * gaps)
        edge = (edge_ref[c] * gaps).astype(jnp.bfloat16)
        edges.append(jnp.concatenate([edge if d == c else blank for d in range(3)], axis=1))
    rows = jnp.concatenate([*split_in_two(jnp.concatenate(pieces, axis=1)), *edges], axis=0)

    def spread(at, block):
        found = jnp.dot(rows, block, preferred_element_type=jnp.float32)
        here_ref[:, at : at + width] = found[0:16] + found[16:32]
        high, low = split_in_two(found[32:56])
        basis_ref[0:24, at : at + width] = high
        basis_ref[24:48, at : at + width] = low

    for at in range(0, start, width):
        spread(at, kept_ref[:, :, at : at + width].reshape(384, width))
    for k in range(count):
        copies[k].wait()
        spread(start + width * k, held_ref[k].reshape(384, width))


def gradient_kernel(states_ref, link_ref, here_ref, basis_ref, out_ref):
    parts = []
    for c in range(3):
        states = states_ref[:, c, :]
        turned = [states] + [pltpu.roll(states, 128 - 16 * i, 1) for i in range(1, 8)]
        parts.append(dot(link_ref[c], jnp.concatenate(turned, axis=0), ((1,), (0,))))
    lane = lax.broadcasted_iota(jnp.int32, (24, 128), 1)
    found = jnp.where(lane < 16, jnp.concatenate(parts, axis=0), 0.0)
    high = found.astype(jnp.bfloat16).astype(jnp.float32)
    low = pltpu.roll(found - high, 16, 1)
    tall = jnp.concatenate([high + low, high, jnp.zeros((80, 128), jnp.float32)], axis=0)
    left = tall.T[0:32, 0:48].astype(jnp.bfloat16)
    peers = out_ref.shape[0]
    for p in range(0, peers, 4):
        span = slice(256 * p, 256 * p + 1024)
        there = jnp.dot(left, basis_ref[:, span], preferred_element_type=jnp.float32)
        whole = (here_ref[:, span] + there[0:16] + there[16:32]).astype(out_ref.dtype)
        for q in range(4):
            out_ref[p + q] = whole[:, 256 * q : 256 * q + 256]


def tables_kernel(
    place_ref, aro_ref, mao_ref, arr_ref, mar_ref, got_ref, own_ref, near_ref, link_ref, edge_ref, *tables
):
    response_kernel(place_ref, aro_ref, mao_ref, arr_ref, mar_ref, *tables)
    segment_kernel(place_ref, got_ref, *tables, own_ref, near_ref, link_ref, edge_ref)


def pack_kernel(direction_any, ids_any, out_ref, direction_ref, ids_ref, sems):
    copies = [
        pltpu.make_async_copy(direction_any, direction_ref, sems.at[0]),
        pltpu.make_async_copy(ids_any, ids_ref, sems.at[1]),
    ]
    for copy in copies:
        copy.start()
    for copy in copies:
        copy.wait()
    packed = direction_ref[:, 0, :].astype(jnp.bfloat16)
    ids = jnp.broadcast_to(ids_ref[...].astype(jnp.float32), (8, 128)).astype(jnp.bfloat16)
    sheet = jnp.concatenate([packed[:, :128], packed[:, 128:], ids], axis=0)
    out_ref[...] = jnp.broadcast_to(sheet[None], out_ref.shape)


def observe_kernel(got_ref, design_ref, kept_ref, early_ref, out_ref, held_ref, sems):
    count, _, _, width = held_ref.shape
    middle = kept_ref.shape[2]
    start = middle + early_ref.shape[2]
    copies = [
        pltpu.make_async_copy(
            design_ref.at[:, :, pl.ds(start + width * k, width)], held_ref.at[k], sems.at[k]
        )
        for k in range(count)
    ]
    for copy in copies:
        copy.start()

    def product(first, block):
        pieces = []
        for p in range(first, first + block.shape[1] // 256):
            pieces += [got_ref[p, 0:16, :], got_ref[p, 16:32, :]]
        return lax.dot_general(
            jnp.concatenate(pieces, axis=1),
            block,
            (((1,), (1,)), ((), ())),
            preferred_element_type=jnp.float32,
        )

    total = jnp.zeros((16, 384), jnp.float32)
    for at in range(0, middle, width):
        total = total + product(at // 256, kept_ref[:, :, at : at + width].reshape(384, width))
    for at in range(middle, start, width):
        block = early_ref[:, :, at - middle : at - middle + width].reshape(384, width)
        total = total + product(at // 256, block)
    for k in range(count):
        copies[k].wait()
        total = total + product((start + width * k) // 256, held_ref[k].reshape(384, width))
    out_ref[...] = jnp.broadcast_to(total.astype(jnp.bfloat16)[None], out_ref.shape)


def image_kernel(
    arrived_ref, kaula_ref, precond_ref, residual_ref, direction_ref, message_ref, image_ref, applied_ref, both_ref
):
    total = arrived_ref[0].astype(jnp.float32)
    for p in range(1, arrived_ref.shape[0]):
        total = total + arrived_ref[p].astype(jnp.float32)
    direction = direction_ref[:, 0, :]
    residual = residual_ref[:, 0, :]
    image = total + kaula_ref[...] * direction
    stack = jnp.concatenate([residual, image], axis=0)
    mixed = jnp.concatenate(
        [dot(stack[:, 128 * k : 128 * k + 128], precond_ref[0, k], ((1,), (1,))) for k in range(2)],
        axis=1,
    )
    applied, image_applied = mixed[0:16], mixed[16:32]
    products = jnp.concatenate(
        [
            residual * applied,
            direction * image,
            image * applied,
            image * image_applied,
            jnp.zeros((64, 256), jnp.float32),
        ],
        axis=0,
    )
    sums = dot(jnp.ones((8, 256), jnp.float32), products, ((1,), (1,)))
    message_ref[...] = jnp.broadcast_to(sums[None, 0:1, :], message_ref.shape)
    image_ref[...] = image
    applied_ref[...] = applied
    both_ref[...] = image_applied


def update_kernel(
    sums_ref, image_ref, applied_ref, both_ref, solution_ref, residual_ref, direction_ref, sol_ref, res_ref, dir_ref
):
    total = jnp.sum(sums_ref[...], axis=0)
    row = lax.broadcasted_iota(jnp.int32, (16, 128), 0)
    lane = lax.broadcasted_iota(jnp.int32, (16, 128), 1)
    wide = jnp.broadcast_to(total, (16, 128))
    old_rz, curvature, cross, square = [
        jnp.sum(jnp.where(lane == row + 16 * k, wide, 0.0), axis=1, keepdims=True)
        for k in range(4)
    ]
    step = old_rz / curvature
    new_rz = old_rz - 2.0 * step * cross + step * step * square
    direction = direction_ref[:, 0, :]
    fresh = applied_ref[...] - step * both_ref[...] + (new_rz / old_rz) * direction
    sol_ref[:, 0, :] = solution_ref[:, 0, :] + step * direction
    res_ref[:, 0, :] = residual_ref[:, 0, :] - step * image_ref[...]
    dir_ref[:, 0, :] = fresh


def run(kernel, outs, args, scalars=(), anywhere=(), scratch=(), flops=100000, limit=SMALL_LIMIT):
    spaces = [
        pltpu.SMEM if i in scalars else pltpu.HBM if i in anywhere else pltpu.VMEM
        for i in range(len(args))
    ]
    shapes = [jax.ShapeDtypeStruct(*out) for out in outs]
    found = pl.pallas_call(
        kernel,
        out_shape=shapes,
        in_specs=[pl.BlockSpec(memory_space=space) for space in spaces],
        out_specs=[pl.BlockSpec(memory_space=pltpu.VMEM) for _ in shapes],
        scratch_shapes=list(scratch),
        cost_estimate=pl.CostEstimate(flops=flops, bytes_accessed=1000000, transcendentals=0),
        compiler_params=pltpu.CompilerParams(vmem_limit_bytes=limit),
    )(*args)
    return found


def exchange(value, axes):
    return lax.all_to_all(value, axes, split_axis=0, concat_axis=0, tiled=True)


def on_device(
    design,
    gap_flags,
    segment_ids,
    ar_order,
    ma_order,
    ar_roots,
    ma_roots,
    kaula,
    precond,
    solution,
    residual,
    direction,
):
    f32, bf16 = jnp.float32, jnp.bfloat16
    count = lax.axis_size(TM)
    others = lax.axis_size(ORDER)
    everyone = count * others
    place = lax.axis_index(TM).astype(jnp.int32).reshape(1, 1)
    gaps = gap_flags.reshape(1, 128)
    (sheets,) = run(
        pack_kernel,
        [((count, 40, 128), bf16)],
        [
            pltpu.with_memory_space_constraint(direction, pltpu.HBM),
            pltpu.with_memory_space_constraint(segment_ids.reshape(1, 128), pltpu.HBM),
        ],
        anywhere=(0, 1),
        scratch=[
            pltpu.VMEM((16, 1, 256), f32),
            pltpu.VMEM((1, 128), jnp.int32),
            pltpu.SemaphoreType.DMA((2,)),
        ],
        limit=VMEM_LIMIT,
    )
    got = exchange(sheets, TM)

    (sheets,) = run(
        pack_kernel,
        [((count, 40, 128), bf16)],
        [
            pltpu.with_memory_space_constraint(direction, pltpu.HBM),
            pltpu.with_memory_space_constraint(segment_ids.reshape(1, 128), pltpu.HBM),
        ],
        anywhere=(0, 1),
        scratch=[
            pltpu.VMEM((16, 1, 256), f32),
            pltpu.VMEM((1, 128), jnp.int32),
            pltpu.SemaphoreType.DMA((2,)),
        ],
        limit=VMEM_LIMIT,
    )
    got = exchange(sheets, TM)

    def held(chunks):
        return [
            pltpu.VMEM((chunks, 3, 128, design.shape[2] // chunks), bf16),
            pltpu.SemaphoreType.DMA((chunks,)),
        ]

    kept = lax.slice_in_dim(design, 0, KEPT, axis=2)
    (partial,) = run(
        observe_kernel,
        [((others, 16, 384), bf16)],
        [got, design, kept, lax.slice_in_dim(design, KEPT, EARLY, axis=2)],
        anywhere=(1,),
        scratch=[
            pltpu.VMEM(((design.shape[2] - EARLY) // 512, 3, 128, 512), bf16),
            pltpu.SemaphoreType.DMA(((design.shape[2] - EARLY) // 512,)),
        ],
        limit=VMEM_LIMIT,
    )
    parts = exchange(partial, ORDER)
    own, near, link, edge = run(
        tables_kernel,
        [((3, 8, 128), f32), ((3, 128, 128), f32), ((3, 8, 256), f32), ((3, 8, 128), f32)],
        [place, ar_order, ma_order, ar_roots, ma_roots, got],
        scalars=(0, 1, 2, 3, 4),
        scratch=[
            pltpu.VMEM((3, 128, 128), f32),
            pltpu.VMEM((4, 8, 128), f32),
            pltpu.VMEM((4, 8, 128), f32),
            pltpu.VMEM((3, 8, 256), f32),
            pltpu.VMEM((LEVELS - 1, 10, 8, 128), f32),
            pltpu.VMEM((LEVELS - 1, 10, 8, 128), f32),
        ],
        flops=10000000,
    )
    message, masked = run(
        state_kernel, [((count, 3, 128), f32), ((48, 128), f32)], [parts, gaps, own]
    )
    states = exchange(message, TM)
    here, basis = run(
        spread_kernel,
        [((16, design.shape[2]), f32), ((48, design.shape[2]), bf16)],
        [masked, near, edge, gaps, design, kept],
        anywhere=(4,),
        scratch=[
            pltpu.VMEM(((design.shape[2] - KEPT) // 1024, 3, 128, 1024), bf16),
            pltpu.SemaphoreType.DMA(((design.shape[2] - KEPT) // 1024,)),
        ],
        flops=10000000,
        limit=VMEM_LIMIT,
    )
    (gradient,) = run(
        gradient_kernel,
        [((count, 16, 256), bf16)],
        [states, link, here, basis],
        limit=16 * 1024 * 1024,
    )
    arrived = exchange(gradient, TM)
    sums, image, applied, image_applied = run(
        image_kernel,
        [((everyone, 1, 128), f32)] + [((16, 256), f32)] * 3,
        [arrived, kaula, precond, residual, direction],
    )
    gathered = exchange(sums, TM_ORDER)
    return tuple(
        run(
            update_kernel,
            [((16, 1, 256), f32)] * 3,
            [gathered, image, applied, image_applied, solution, residual, direction],
        )
    )


def solution(mesh):
    split = Mesh(mesh.devices.reshape(4, 8, 4, 2), TM_ORDER)
    in_specs = (
        P(None, TM, ORDER),
        P(TM),
        P(TM),
        P(),
        P(),
        P(),
        P(),
        P(ORDER, TM),
        P(ORDER, TM, None, None),
        P(None, ORDER, TM),
        P(None, ORDER, TM),
        P(None, ORDER, TM),
    )
    out_specs = (P(None, ORDER, TM),) * 3
    return jax.shard_map(
        on_device, mesh=split, in_specs=in_specs, out_specs=out_specs, check_vma=False
    )
```

```python
import jax
import jax.numpy as jnp
from jax import lax
from jax.experimental import pallas as pl
from jax.experimental.pallas import tpu as pltpu
from jax.sharding import Mesh
from jax.sharding import PartitionSpec as P

TM = ("tm_0", "tm_1")
ORDER = ("order_0", "order_1")
TM_ORDER = TM + ORDER
VMEM_LIMIT = 50 * 1024 * 1024
SMALL_LIMIT = 8 * 1024 * 1024
KEPT = 2048
EARLY = 3584

precise = lax.Precision.HIGHEST
LEVELS = 12
RADIX = 7


def dot(a, b, dims):
    return lax.dot_general(
        a, b, (dims, ((), ())), precision=precise, preferred_element_type=jnp.float32
    )


def splat_rows(read):
    row = lax.broadcasted_iota(jnp.int32, (8, 128), 0)
    out = jnp.zeros((8, 128), jnp.float32)
    for c in range(3):
        out = jnp.where(row == c, read(c), out)
    return out


LOWER = [(i, j) for i in range(4) for j in range(i + 1)]
UPPER = [(i, j) for i in range(4) for j in range(i, 4)]


def active_roots(roots_ref, order_ref):
    return [
        splat_rows(lambda c: jnp.where(k < order_ref[c], roots_ref[c, k], jnp.float32(0.0)))
        for k in range(4)
    ]


def sum_of(terms):
    while len(terms) > 1:
        terms = [
            terms[k] + terms[k + 1] if k + 1 < len(terms) else terms[k]
            for k in range(0, len(terms), 2)
        ]
    return terms[0]


def times(left, right):
    return {
        (i, j): sum_of([left[i, k] * right[k, j] for k in range(j, i + 1)]) for i, j in LOWER
    }


def gram_step(gram, power):
    half = {
        (i, j): sum_of([gram[min(i, k), max(i, k)] * power[k, j] for k in range(j, 4)])
        for i in range(4)
        for j in range(4)
    }
    return {(i, j): sum_of([power[k, i] * half[k, j] for k in range(i, 4)]) for i, j in UPPER}


def row_times(vector, power):
    return [sum_of([vector[i] * power[i, j] for i in range(j, 4)]) for j in range(4)]


def row_power(vector, powers, number, bits):
    for k in range(bits):
        on = ((number >> k) & 1) == 1
        moved = row_times(vector, powers[k])
        vector = [jnp.where(on, moved[j], vector[j]) for j in range(4)]
    return vector


def column_power(vector, powers, number, bits):
    for k in range(bits):
        on = ((number >> k) & 1) == 1
        moved = [sum_of([powers[k][i, j] * vector[j] for j in range(i + 1)]) for i in range(4)]
        vector = [jnp.where(on, moved[i], vector[i]) for i in range(4)]
    return vector


def response_kernel(
    place_ref, aro_ref, mao_ref, arr_ref, mar_ref, toep_ref, gam_ref, fin_ref, reach_ref, pow_ref, gram_ref
):
    poles = active_roots(arr_ref, aro_ref)
    zeros = active_roots(mar_ref, mao_ref)
    kappa = [poles[j] - zeros[j] for j in range(4)]
    one = jnp.ones((8, 128), jnp.float32)
    powers = [{(i, j): poles[i] if i == j else kappa[j] for i, j in LOWER}]
    for _ in range(LEVELS - 1):
        powers.append(times(powers[-1], powers[-1]))
    gram = {(i, j): kappa[i] * kappa[j] for i, j in UPPER}
    for k in range(LEVELS - 1):
        for at, (i, j) in enumerate(LOWER):
            pow_ref[k, at] = powers[k][i, j]
        for at, (i, j) in enumerate(UPPER):
            gram_ref[k, at] = gram[i, j]
        if k < LEVELS - 2:
            add = gram_step(gram, powers[k])
            gram = {at: gram[at] + add[at] for at in UPPER}
    lane = lax.broadcasted_iota(jnp.int32, (8, 128), 1)
    gam = row_power(kappa, powers, lane, RADIX)
    fin = column_power([one] * 4, powers, 127 - lane, RADIX)
    for i in range(4):
        gam_ref[i] = gam[i]
        fin_ref[i] = fin[i]
    eta = jnp.where(lane == 0, 1.0, pltpu.roll(sum_of(gam), 1, 1))
    big_row = lax.broadcasted_iota(jnp.int32, (128, 128), 0)
    big_lane = lax.broadcasted_iota(jnp.int32, (128, 128), 1)
    for c in range(3):
        base = jnp.broadcast_to(eta[c : c + 1, :], (128, 128))
        turned = pltpu.roll(base, 0, 1, stride=1, stride_axis=0)
        toep_ref[c] = jnp.where(big_lane >= big_row, turned, 0.0)
    place = place_ref[0, 0]
    row = lax.broadcasted_iota(jnp.int32, (8, 128), 0)
    front = row < 4
    for side in range(2):
        wide = lane + 128 * side
        peer, kind = wide & 31, wide >> 5
        gap = jnp.where(front, place - 1 - peer, peer - 1 - place)
        steps = jnp.maximum(gap, 0)
        for c in range(3):
            vector = [jnp.where((row & 3) == j, 1.0, 0.0) for j in range(4)]
            for k in range(5):
                cut = {at: powers[RADIX + k][at][c : c + 1, :] for at in LOWER}
                on = ((steps >> k) & 1) == 1
                moved = []
                for j in range(4):
                    terms = [vector[j] * cut[j, j]]
                    for i in range(4):
                        if i > j:
                            terms.append(vector[i] * jnp.where(front, cut[i, j], 0.0))
                        if i < j:
                            terms.append(vector[i] * jnp.where(front, 0.0, cut[j, i]))
                    moved.append(sum_of(terms))
                vector = [jnp.where(on, moved[j], vector[j]) for j in range(4)]
            picked = jnp.zeros((8, 128), jnp.float32)
            for j in range(4):
                picked = jnp.where((kind & 3) == j, vector[j], picked)
            used = ((kind < 4) == front) & (gap >= 0)
            reach_ref[c, :, 128 * side : 128 * side + 128] = jnp.where(used, picked, 0.0)


def segment_kernel(
    place_ref, got_ref, toep_ref, gam_ref, fin_ref, reach_ref, pow_ref, gram_ref, own_ref, near_ref, link_ref, edge_ref
):
    place = place_ref[0, 0]
    row = lax.broadcasted_iota(jnp.int32, (8, 128), 0)
    groups = []
    for g in range(4):
        group = jnp.zeros((8, 128), jnp.float32)
        for s in range(8):
            group = jnp.where(row == s, got_ref[8 * g + s, 32:40, :].astype(jnp.float32), group)
        groups.append(group)
    ids = jnp.concatenate(groups, axis=0)
    peer = lax.broadcasted_iota(jnp.int32, (32, 128), 0)
    mine = jnp.sum(jnp.where(peer == place, ids, 0.0), axis=0, keepdims=True)
    before = jnp.sum(jnp.where(peer == place - 1, ids, 0.0), axis=0, keepdims=True)
    ends = jnp.broadcast_to(ids[:, 127:128], (32, 128))
    last = jnp.broadcast_to(mine[:, 127:128], (1, 128))
    prev = jnp.where(place > 0, jnp.broadcast_to(before[:, 127:128], (1, 128)), -1.0)
    count = jnp.sum(
        jnp.where((peer > place) & (ids == last), 1.0, 0.0), axis=0, keepdims=True
    )
    left = jnp.sum(count, axis=1, keepdims=True).astype(jnp.int32)
    left = jnp.broadcast_to(left, (8, 128))
    ends_before = pltpu.roll(ends, 1, 0)
    keep_past = jnp.where((peer < place) & (ends == prev), 1.0, 0.0)
    keep_next = jnp.where((peer > place) & (ends_before == last), 1.0, 0.0)
    wide_past = jnp.concatenate([keep_past, jnp.zeros((96, 128), jnp.float32)], axis=0).T[0:1, :]
    wide_next = jnp.concatenate([keep_next, jnp.zeros((96, 128), jnp.float32)], axis=0).T[0:1, :]
    keeps = []
    for wide_keep in (wide_past, wide_next):
        part = wide_keep
        for turn in (32, 64, 96):
            part = part + pltpu.roll(wide_keep, turn, 1)
        keeps.append(part)
    keep = jnp.concatenate(keeps, axis=1)
    gram = {at: jnp.zeros((8, 128), jnp.float32) for at in UPPER}
    for k in range(LEVELS - 1):
        power = {pair: pow_ref[k, at] for at, pair in enumerate(LOWER)}
        add = gram_step(gram, power)
        on = ((left >> k) & 1) == 1
        gram = {
            pair: jnp.where(on, gram_ref[k, at] + add[pair], gram[pair])
            for at, pair in enumerate(UPPER)
        }
    lead = jnp.where(mine == prev, 1.0, 0.0)
    trail = jnp.where(mine == last, 1.0, 0.0)
    cont = jnp.where(last == prev, 1.0, 0.0)
    fin = [fin_ref[i] * trail for i in range(4)]
    gam = [gam_ref[i] * lead for i in range(4)]
    fold = [
        sum_of([fin[j] * gram[min(i, j), max(i, j)] for j in range(4)]) for i in range(4)
    ]
    block = {pair: pow_ref[RADIX, at] for at, pair in enumerate(LOWER)}
    past = [cont * value for value in row_times(fold, block)]
    big_row = lax.broadcasted_iota(jnp.int32, (128, 128), 0)
    big_lane = lax.broadcasted_iota(jnp.int32, (128, 128), 1)
    wide = jnp.broadcast_to(mine, (128, 128))
    tall = jnp.sum(jnp.where(big_row == big_lane, wide, 0.0), axis=1, keepdims=True)
    same = wide == jnp.broadcast_to(tall, (128, 128))

    def rows(values, c, start):
        out = jnp.zeros((8, 128), jnp.float32)
        for i in range(4):
            out = jnp.where(row == start + i, values[i][c : c + 1, :], out)
        return out

    for c in range(3):
        toep = jnp.where(same, toep_ref[c], 0.0)
        probe = dot(rows(gam, c, 0), toep, ((1,), (1,)))
        out_p = jnp.where(row < 4, probe, 0.0) + rows(past, c, 0)
        fin_low = rows(fin, c, 0)
        near_ref[c] = dot(toep, toep, ((1,), (1,))) + dot(rows(fold, c, 0), fin_low, ((0,), (0,)))
        own_ref[c] = fin_low + pltpu.roll(out_p, 4, 0)
        edge_ref[c] = out_p + rows(fin, c, 4)
        link_ref[c] = reach_ref[c] * keep


def state_kernel(parts_ref, gaps_ref, own_ref, message_ref, masked_ref):
    total = parts_ref[0].astype(jnp.float32)
    for o in range(1, parts_ref.shape[0]):
        total = total + parts_ref[o].astype(jnp.float32)
    gaps = gaps_ref[...].astype(jnp.float32)
    rows = []
    for c in range(3):
        masked = total[:, 128 * c : 128 * c + 128] * gaps
        masked_ref[16 * c : 16 * c + 16, :] = masked
        padded = jnp.concatenate([masked, jnp.zeros((112, 128), jnp.float32)], axis=0)
        spread = pltpu.roll(
            dot(own_ref[c], padded, ((1,), (1,))), 0, 1, stride=16, stride_axis=0
        )
        rows.append(jnp.sum(spread, axis=0, keepdims=True))
    message_ref[...] = jnp.broadcast_to(jnp.concatenate(rows, axis=0)[None], message_ref.shape)


def split_in_two(value):
    high = value.astype(jnp.bfloat16)
    return high, (value - high.astype(jnp.float32)).astype(jnp.bfloat16)


def spread_kernel(
    masked_ref, near_ref, edge_ref, gaps_ref, design_ref, kept_ref, here_ref, basis_ref, held_ref, sems
):
    count, _, _, width = held_ref.shape
    start = kept_ref.shape[2]
    copies = [
        pltpu.make_async_copy(
            design_ref.at[:, :, pl.ds(start + width * k, width)], held_ref.at[k], sems.at[k]
        )
        for k in range(count)
    ]
    for copy in copies:
        copy.start()
    gaps = gaps_ref[...].astype(jnp.float32)
    pieces = []
    edges = []
    blank = jnp.zeros((8, 128), jnp.bfloat16)
    for c in range(3):
        pieces.append(dot(masked_ref[16 * c : 16 * c + 16, :], near_ref[c], ((1,), (0,))) * gaps)
        edge = (edge_ref[c] * gaps).astype(jnp.bfloat16)
        edges.append(jnp.concatenate([edge if d == c else blank for d in range(3)], axis=1))
    rows = jnp.concatenate([*split_in_two(jnp.concatenate(pieces, axis=1)), *edges], axis=0)

    def spread(at, block):
        found = jnp.dot(rows, block, preferred_element_type=jnp.float32)
        here_ref[:, at : at + width] = found[0:16] + found[16:32]
        basis_ref[:, at : at + width] = found[32:56].astype(jnp.bfloat16)

    for at in range(0, start, width):
        spread(at, kept_ref[:, :, at : at + width].reshape(384, width))
    for k in range(count):
        copies[k].wait()
        spread(start + width * k, held_ref[k].reshape(384, width))


def gradient_kernel(states_ref, link_ref, here_ref, basis_ref, out_ref):
    parts = []
    for c in range(3):
        states = states_ref[:, c, :]
        turned = [states] + [pltpu.roll(states, 128 - 16 * i, 1) for i in range(1, 8)]
        parts.append(dot(link_ref[c], jnp.concatenate(turned, axis=0), ((1,), (0,))))
    lane = lax.broadcasted_iota(jnp.int32, (24, 128), 1)
    found = jnp.where(lane < 16, jnp.concatenate(parts, axis=0), 0.0)
    high = found.astype(jnp.bfloat16).astype(jnp.float32)
    low = pltpu.roll(found - high, 16, 1)
    tall = jnp.concatenate([high + low, jnp.zeros((104, 128), jnp.float32)], axis=0)
    left = tall.T[0:32, 0:24].astype(jnp.bfloat16)
    peers = out_ref.shape[0]
    for p in range(0, peers, 4):
        span = slice(256 * p, 256 * p + 1024)
        there = jnp.dot(left, basis_ref[:, span], preferred_element_type=jnp.float32)
        whole = (here_ref[:, span] + there[0:16] + there[16:32]).astype(out_ref.dtype)
        for q in range(4):
            out_ref[p + q] = whole[:, 256 * q : 256 * q + 256]


def tables_kernel(
    place_ref, aro_ref, mao_ref, arr_ref, mar_ref, got_ref, own_ref, near_ref, link_ref, edge_ref, *tables
):
    response_kernel(place_ref, aro_ref, mao_ref, arr_ref, mar_ref, *tables)
    segment_kernel(place_ref, got_ref, *tables, own_ref, near_ref, link_ref, edge_ref)


def pack_kernel(direction_any, ids_any, out_ref, direction_ref, ids_ref, sems):
    copies = [
        pltpu.make_async_copy(direction_any, direction_ref, sems.at[0]),
        pltpu.make_async_copy(ids_any, ids_ref, sems.at[1]),
    ]
    for copy in copies:
        copy.start()
    for copy in copies:
        copy.wait()
    packed = direction_ref[:, 0, :].astype(jnp.bfloat16)
    ids = jnp.broadcast_to(ids_ref[...].astype(jnp.float32), (8, 128)).astype(jnp.bfloat16)
    sheet = jnp.concatenate([packed[:, :128], packed[:, 128:], ids], axis=0)
    out_ref[...] = jnp.broadcast_to(sheet[None], out_ref.shape)


def observe_kernel(got_ref, design_ref, kept_ref, early_ref, out_ref, held_ref, sems):
    count, _, _, width = held_ref.shape
    middle = kept_ref.shape[2]
    start = middle + early_ref.shape[2]
    copies = [
        pltpu.make_async_copy(
            design_ref.at[:, :, pl.ds(start + width * k, width)], held_ref.at[k], sems.at[k]
        )
        for k in range(count)
    ]
    for copy in copies:
        copy.start()

    def product(first, block):
        pieces = []
        for p in range(first, first + block.shape[1] // 256):
            pieces += [got_ref[p, 0:16, :], got_ref[p, 16:32, :]]
        return lax.dot_general(
            jnp.concatenate(pieces, axis=1),
            block,
            (((1,), (1,)), ((), ())),
            preferred_element_type=jnp.float32,
        )

    total = jnp.zeros((16, 384), jnp.float32)
    for at in range(0, middle, width):
        total = total + product(at // 256, kept_ref[:, :, at : at + width].reshape(384, width))
    for at in range(middle, start, width):
        block = early_ref[:, :, at - middle : at - middle + width].reshape(384, width)
        total = total + product(at // 256, block)
    for k in range(count):
        copies[k].wait()
        total = total + product((start + width * k) // 256, held_ref[k].reshape(384, width))
    out_ref[...] = jnp.broadcast_to(total.astype(jnp.bfloat16)[None], out_ref.shape)


def image_kernel(
    arrived_ref, kaula_ref, precond_ref, residual_ref, direction_ref, message_ref, image_ref, applied_ref, both_ref
):
    total = arrived_ref[0].astype(jnp.float32)
    for p in range(1, arrived_ref.shape[0]):
        total = total + arrived_ref[p].astype(jnp.float32)
    direction = direction_ref[:, 0, :]
    residual = residual_ref[:, 0, :]
    image = total + kaula_ref[...] * direction
    stack = jnp.concatenate([residual, image], axis=0)
    mixed = jnp.concatenate(
        [dot(stack[:, 128 * k : 128 * k + 128], precond_ref[0, k], ((1,), (1,))) for k in range(2)],
        axis=1,
    )
    applied, image_applied = mixed[0:16], mixed[16:32]
    products = jnp.concatenate(
        [
            residual * applied,
            direction * image,
            image * applied,
            image * image_applied,
            jnp.zeros((64, 256), jnp.float32),
        ],
        axis=0,
    )
    sums = dot(jnp.ones((8, 256), jnp.float32), products, ((1,), (1,)))
    message_ref[...] = jnp.broadcast_to(sums[None, 0:1, :], message_ref.shape)
    image_ref[...] = image
    applied_ref[...] = applied
    both_ref[...] = image_applied


def update_kernel(
    sums_ref, image_ref, applied_ref, both_ref, solution_ref, residual_ref, direction_ref, sol_ref, res_ref, dir_ref
):
    total = jnp.sum(sums_ref[...], axis=0)
    row = lax.broadcasted_iota(jnp.int32, (16, 128), 0)
    lane = lax.broadcasted_iota(jnp.int32, (16, 128), 1)
    wide = jnp.broadcast_to(total, (16, 128))
    old_rz, curvature, cross, square = [
        jnp.sum(jnp.where(lane == row + 16 * k, wide, 0.0), axis=1, keepdims=True)
        for k in range(4)
    ]
    step = old_rz / curvature
    new_rz = old_rz - 2.0 * step * cross + step * step * square
    direction = direction_ref[:, 0, :]
    fresh = applied_ref[...] - step * both_ref[...] + (new_rz / old_rz) * direction
    sol_ref[:, 0, :] = solution_ref[:, 0, :] + step * direction
    res_ref[:, 0, :] = residual_ref[:, 0, :] - step * image_ref[...]
    dir_ref[:, 0, :] = fresh


def run(kernel, outs, args, scalars=(), anywhere=(), scratch=(), flops=100000, limit=SMALL_LIMIT):
    spaces = [
        pltpu.SMEM if i in scalars else pltpu.HBM if i in anywhere else pltpu.VMEM
        for i in range(len(args))
    ]
    shapes = [jax.ShapeDtypeStruct(*out) for out in outs]
    found = pl.pallas_call(
        kernel,
        out_shape=shapes,
        in_specs=[pl.BlockSpec(memory_space=space) for space in spaces],
        out_specs=[pl.BlockSpec(memory_space=pltpu.VMEM) for _ in shapes],
        scratch_shapes=list(scratch),
        cost_estimate=pl.CostEstimate(flops=flops, bytes_accessed=1000000, transcendentals=0),
        compiler_params=pltpu.CompilerParams(vmem_limit_bytes=limit),
    )(*args)
    return found


def exchange(value, axes):
    return lax.all_to_all(value, axes, split_axis=0, concat_axis=0, tiled=True)


def on_device(
    design,
    gap_flags,
    segment_ids,
    ar_order,
    ma_order,
    ar_roots,
    ma_roots,
    kaula,
    precond,
    solution,
    residual,
    direction,
):
    f32, bf16 = jnp.float32, jnp.bfloat16
    count = lax.axis_size(TM)
    others = lax.axis_size(ORDER)
    everyone = count * others
    place = lax.axis_index(TM).astype(jnp.int32).reshape(1, 1)
    gaps = gap_flags.reshape(1, 128)
    (sheets,) = run(
        pack_kernel,
        [((count, 40, 128), bf16)],
        [
            pltpu.with_memory_space_constraint(direction, pltpu.HBM),
            pltpu.with_memory_space_constraint(segment_ids.reshape(1, 128), pltpu.HBM),
        ],
        anywhere=(0, 1),
        scratch=[
            pltpu.VMEM((16, 1, 256), f32),
            pltpu.VMEM((1, 128), jnp.int32),
            pltpu.SemaphoreType.DMA((2,)),
        ],
        limit=VMEM_LIMIT,
    )
    got = exchange(sheets, TM)

    (sheets,) = run(
        pack_kernel,
        [((count, 40, 128), bf16)],
        [
            pltpu.with_memory_space_constraint(direction, pltpu.HBM),
            pltpu.with_memory_space_constraint(segment_ids.reshape(1, 128), pltpu.HBM),
        ],
        anywhere=(0, 1),
        scratch=[
            pltpu.VMEM((16, 1, 256), f32),
            pltpu.VMEM((1, 128), jnp.int32),
            pltpu.SemaphoreType.DMA((2,)),
        ],
        limit=VMEM_LIMIT,
    )
    got = exchange(sheets, TM)

    def held(chunks):
        return [
            pltpu.VMEM((chunks, 3, 128, design.shape[2] // chunks), bf16),
            pltpu.SemaphoreType.DMA((chunks,)),
        ]

    kept = lax.slice_in_dim(design, 0, KEPT, axis=2)
    (partial,) = run(
        observe_kernel,
        [((others, 16, 384), bf16)],
        [got, design, kept, lax.slice_in_dim(design, KEPT, EARLY, axis=2)],
        anywhere=(1,),
        scratch=[
            pltpu.VMEM(((design.shape[2] - EARLY) // 512, 3, 128, 512), bf16),
            pltpu.SemaphoreType.DMA(((design.shape[2] - EARLY) // 512,)),
        ],
        limit=VMEM_LIMIT,
    )
    parts = exchange(partial, ORDER)
    own, near, link, edge = run(
        tables_kernel,
        [((3, 8, 128), f32), ((3, 128, 128), f32), ((3, 8, 256), f32), ((3, 8, 128), f32)],
        [place, ar_order, ma_order, ar_roots, ma_roots, got],
        scalars=(0, 1, 2, 3, 4),
        scratch=[
            pltpu.VMEM((3, 128, 128), f32),
            pltpu.VMEM((4, 8, 128), f32),
            pltpu.VMEM((4, 8, 128), f32),
            pltpu.VMEM((3, 8, 256), f32),
            pltpu.VMEM((LEVELS - 1, 10, 8, 128), f32),
            pltpu.VMEM((LEVELS - 1, 10, 8, 128), f32),
        ],
        flops=10000000,
    )
    message, masked = run(
        state_kernel, [((count, 3, 128), f32), ((48, 128), f32)], [parts, gaps, own]
    )
    states = exchange(message, TM)
    here, basis = run(
        spread_kernel,
        [((16, design.shape[2]), f32), ((24, design.shape[2]), bf16)],
        [masked, near, edge, gaps, design, kept],
        anywhere=(4,),
        scratch=[
            pltpu.VMEM(((design.shape[2] - KEPT) // 1024, 3, 128, 1024), bf16),
            pltpu.SemaphoreType.DMA(((design.shape[2] - KEPT) // 1024,)),
        ],
        flops=10000000,
        limit=VMEM_LIMIT,
    )
    (gradient,) = run(
        gradient_kernel,
        [((count, 16, 256), bf16)],
        [states, link, here, basis],
        limit=16 * 1024 * 1024,
    )
    arrived = exchange(gradient, TM)
    sums, image, applied, image_applied = run(
        image_kernel,
        [((everyone, 1, 128), f32)] + [((16, 256), f32)] * 3,
        [arrived, kaula, precond, residual, direction],
    )
    gathered = exchange(sums, TM_ORDER)
    return tuple(
        run(
            update_kernel,
            [((16, 1, 256), f32)] * 3,
            [gathered, image, applied, image_applied, solution, residual, direction],
        )
    )


def solution(mesh):
    split = Mesh(mesh.devices.reshape(4, 8, 4, 2), TM_ORDER)
    in_specs = (
        P(None, TM, ORDER),
        P(TM),
        P(TM),
        P(),
        P(),
        P(),
        P(),
        P(ORDER, TM),
        P(ORDER, TM, None, None),
        P(None, ORDER, TM),
        P(None, ORDER, TM),
        P(None, ORDER, TM),
    )
    out_specs = (P(None, ORDER, TM),) * 3
    return jax.shard_map(
        on_device, mesh=split, in_specs=in_specs, out_specs=out_specs, check_vma=False
    )
```
